32 devices in a mesh: group: 8 (over z, y), psg: 4 (over x, core).
Axes of the slice: x: 2, y: 2, z: 4, core: 2. Of those that a mesh axis runs over, the one named last changes fastest.
Arguments:
- query_input: bfloat16 [2, 64, 32, 768], P(None, ('group', 'psg')), may hold values from -6 to 6
- passage_input: bfloat16 [2, 32, 256, 768], P(None, ('group', 'psg')), may hold values from -6 to 6
- lengths: int32 [2, 32], P(None, ('group', 'psg')), may hold values from 1 to 256, 4096 in all within a row
- positive: int32 [2, 64], P(None, 'group'), may hold values from 0 to 3
- w_qkv: bfloat16 [768, 2304], replicated, may hold values from -0.21875 to 0.21875
- bias_q: bfloat16 [768], replicated, may hold values from -2 to 2
- bias_v: bfloat16 [768], replicated, may hold values from -2 to 2
- w_out: bfloat16 [768, 768], replicated, may hold values from -0.625 to 0.625
- bias_out: bfloat16 [768], replicated, may hold values from -2 to 2
- norm1_gain: bfloat16 [768], replicated, may hold values from 0.5 to 1.5
- norm1_bias: bfloat16 [768], replicated, may hold values from -2 to 2
- w_in: bfloat16 [768, 3072], replicated, may hold values from -0.21875 to 0.21875
- bias_in: bfloat16 [3072], replicated, may hold values from -2 to 2
- w_back: bfloat16 [3072, 768], replicated, may hold values from -0.109375 to 0.109375
- bias_back: bfloat16 [768], replicated, may hold values from -2 to 2
- norm2_gain: bfloat16 [768], replicated, may hold values from 0.5 to 1.5
- norm2_bias: bfloat16 [768], replicated, may hold values from -2 to 2
- w_proj: bfloat16 [768, 128], replicated, may hold values from -0.21875 to 0.21875
Outputs:
- losses: float32 [2, 64], P(None, ('group', 'psg'))
- query_embeddings: bfloat16 [2, 64, 32, 128], P(None, ('group', 'psg'))
- passage_embeddings: bfloat16 [2, 32, 256, 128], P(None, ('group', 'psg'))
- grad_query_input: bfloat16 [2, 64, 32, 768], P(None, ('group', 'psg'))
- grad_passage_input: bfloat16 [2, 32, 256, 768], P(None, ('group', 'psg'))
- grad_w_qkv: float32 [768, 2304], P('group')
- grad_bias_q: float32 [768], P('group')
- grad_bias_v: float32 [768], P('group')
- grad_w_out: float32 [768, 768], P('group')
- grad_bias_out: float32 [768], P('group')
- grad_norm1_gain: float32 [768], P('group')
- grad_norm1_bias: float32 [768], P('group')
- grad_w_in: float32 [768, 3072], P('group')
- grad_bias_in: float32 [3072], P('group')
- grad_w_back: float32 [3072, 768], P('group')
- grad_bias_back: float32 [768], P('group')
- grad_norm2_gain: float32 [768], P('group')
- grad_norm2_bias: float32 [768], P('group')
- grad_w_proj: float32 [768, 128], P('group')
The draws below stay inside these ranges and needn't reach their ends.
Inputs may be any that keep to these rules, and one draw needn't show every extreme that they name: In each micro-batch the lengths sum to 4096 and some passage has 256. `positive`: candidates of a query are numbered in the order of its group's passages.
All inputs are finite; a program needn't handle non-finite values. No bound on the sum of `lengths` on one device may be relied on, other than what follows from the above.
Results may differ from the reference program's by a relative error of at most 0.024.
Values may be sent and summed in bfloat16 or wider, within the bound.
A program may use at most 192 MiB of HBM per device.

```python
import math
import jax
import jax.numpy as jnp
import numpy as np
from jax import lax

D = 768
H = 12
HD = 64
FF = 3072
PROJ = 128
QLEN = 32
PLEN = 256
MB = 2
PDEV = 1
QDEV = 2
QUERIES = 64
PASSAGES = 32
N_GROUP = 8
N_PSG = 4


def set_ends(array, rng, low, largest):
    index_at = [jax.random.randint(jax.random.fold_in(rng, axis), (), 0, length) for axis, length in enumerate(array.shape)]
    widest = array.shape.index(max(array.shape))
    neighbour = index_at[:widest] + [(index_at[widest] + 1) % array.shape[widest]] + index_at[widest + 1:]
    return array.at[tuple(index_at)].set(low).at[tuple(neighbour)].set(largest)


def steps_of(key, dims, shards, smallest, high):
    level = 1.0
    for axis_at, parts in shards:
        draws = jax.random.uniform(jax.random.fold_in(jax.random.fold_in(key, 6), axis_at), (parts,), jnp.float32, smallest / len(shards), high / len(shards))
        level = level * jnp.repeat(jnp.exp(draws), dims[axis_at] // parts).reshape((-1,) + (1,) * (len(dims) - 1 - axis_at))
    return level


def length_profile(count, total, reach, slope):
    portions = [(1 << 20) // math.isqrt(rank ** slope) + 1 for rank in range(2, count + 1)]
    rest, holding = total - reach - (count - 1), [1] * (count - 1)
    while rest > 0:
        movable = [i for i in range(count - 1) if holding[i] < reach]
        pool, remaining = sum([portions[i] for i in movable]), rest
        for i in movable:
            extra = min(reach - holding[i], max(1, remaining * portions[i] // pool), rest)
            holding[i] = holding[i] + extra
            rest = rest - extra
    return np.array([reach] + holding)


def ragged_sizes(own_key, count, total, reach, skew):
    if count == 2:
        one = jax.random.randint(own_key, (), max(1, total - reach), min(reach, total - 1) + 1)
        return jnp.stack([one, total - one])
    sizes = jnp.asarray(length_profile(count, total, reach, skew), jnp.int32)
    twos = (count - 1) // 2
    donor, receiver = sizes[1:1 + 2 * twos:2], sizes[2:2 + 2 * twos:2]
    slack = jnp.minimum(donor - 1, reach - receiver)
    moved = jax.random.randint(jax.random.fold_in(own_key, 1), (twos,), 0, 1 << 20) % (slack + 1)
    sizes = sizes.at[1:1 + 2 * twos:2].set(donor - moved).at[2:2 + 2 * twos:2].set(receiver + moved)
    return sizes[jax.random.permutation(jax.random.fold_in(own_key, 2), count)]


def bell_draw(own_key, extent, spread, limit, cuts=(), kind=jnp.bfloat16):
    drawn = jax.random.normal(own_key, extent, jnp.float32) * spread
    if len(cuts) > 0:
        drawn = steps_of(own_key, extent, cuts, -0.22, 0.18) * drawn
    return jnp.clip(drawn, min=-limit, max=limit).astype(kind)


def setup_inputs(seed: int = 0) -> dict:
    key_list = jax.random.split(jax.random.key(seed), 19)
    return {
        "query_input": bell_draw(key_list[0], (MB, QUERIES, QLEN, D), 1.0, 6.0, ((1, 32),)),
        "passage_input": bell_draw(key_list[1], (MB, PASSAGES, PLEN, D), 1.0, 6.0, ((1, 32),)),
        "lengths": jax.vmap(lambda own: ragged_sizes(own, PASSAGES, PASSAGES * PLEN // 2, PLEN, 2))(jax.random.split(key_list[2], MB)).reshape((MB, PASSAGES)).astype(jnp.int32),
        "positive": set_ends(jax.random.randint(key_list[3], (MB, QUERIES), 0, PDEV * N_PSG), jax.random.fold_in(key_list[3], 1), 0, (PDEV * N_PSG) - 1).astype(jnp.int32),
        "w_qkv": bell_draw(key_list[4], (D, 3 * D), D ** -0.5, 0.21875),
        "bias_q": bell_draw(key_list[5], (D,), 0.3, 2.0),
        "bias_v": bell_draw(key_list[6], (D,), 0.3, 2.0),
        "w_out": bell_draw(key_list[7], (D, D), (D // 8) ** -0.5, 0.625),
        "bias_out": bell_draw(key_list[8], (D,), 0.3, 2.0),
        "norm1_gain": jnp.clip(1.0 + 0.1 * jax.random.normal(key_list[9], (D,), jnp.float32), 0.5, 1.5).astype(jnp.bfloat16),
        "norm1_bias": bell_draw(key_list[10], (D,), 0.3, 2.0),
        "w_in": bell_draw(key_list[11], (D, FF), D ** -0.5, 0.21875),
        "bias_in": bell_draw(key_list[12], (FF,), 0.3, 2.0),
        "w_back": bell_draw(key_list[13], (FF, D), FF ** -0.5, 0.109375),
        "bias_back": bell_draw(key_list[14], (D,), 0.3, 2.0),
        "norm2_gain": jnp.clip(1.0 + 0.1 * jax.random.normal(key_list[15], (D,), jnp.float32), 0.5, 1.5).astype(jnp.bfloat16),
        "norm2_bias": bell_draw(key_list[16], (D,), 0.3, 2.0),
        "w_proj": bell_draw(key_list[17], (D, PROJ), D ** -0.5, 0.21875),
    }


temper = 0.1
epsilon = 1e-06
masked = -1e+30

@jax.custom_vjp
def low(v):
    return lax.optimization_barrier(v.astype(jnp.bfloat16)).astype(jnp.float32)

@jax.custom_vjp
def low_back(v):
    return v

def low_keep(v):
    return (low(v), None)

def low_pass(kept, grad):
    return (grad,)

def back_keep(v):
    return (v, None)

def back_low(kept, grad):
    return (low(grad),)
low.defvjp(low_keep, low_pass)
low_back.defvjp(back_keep, back_low)

def matmul(left_side, right_side):
    return jnp.dot(left_side, right_side, precision=lax.Precision.HIGHEST)

def layer_norm(resid_in, gain_vec, shift_vec):
    row_mean = lax.optimization_barrier(jnp.mean(resid_in, -1, keepdims=True))
    centred = resid_in - row_mean
    variance = lax.optimization_barrier(jnp.mean(centred * centred, -1, keepdims=True))
    return centred * lax.rsqrt(variance + epsilon) * gain_vec + shift_vec

def encode(params, inputs, key_valid):
    w_qkv, bias_q, bias_v, w_out, bias_out, gain_one, shift_one, w_in, bias_in, w_back, bias_back, gain_two, shift_two, w_proj = params
    seq_count, length = key_valid.shape
    flat_rows = inputs.reshape(seq_count * length, D)
    bias_all = jnp.concatenate([bias_q, jnp.zeros_like(bias_q), bias_v])
    qkv_all = low(low_back(matmul(flat_rows, w_qkv) + bias_all))
    qkv_split = qkv_all.reshape(seq_count, length, 3, H, HD)
    scores = low_back(jnp.einsum('slhe,smhe->shlm', qkv_split[:, :, 0], qkv_split[:, :, 1], precision=lax.Precision.HIGHEST) * 0.125)
    scores = jnp.where(key_valid[:, None, None, :], scores, masked)
    attn_probs = low(jax.nn.softmax(scores, axis=-1))
    attended = jnp.einsum('shlm,smhe->slhe', attn_probs, qkv_split[:, :, 2], precision=lax.Precision.HIGHEST)
    attended = low(low_back(attended.reshape(seq_count * length, D)))
    resid_one = flat_rows + low_back(matmul(attended, w_out) + bias_out)
    normed_one = layer_norm(resid_one, gain_one, shift_one)
    pre_gelu = low_back(matmul(low(normed_one), w_in) + bias_in)
    post_gelu = low(jax.nn.gelu(pre_gelu, approximate=False))
    resid_two = normed_one + low_back(matmul(post_gelu, w_back) + bias_back)
    normed_two = layer_norm(resid_two, gain_two, shift_two)
    projected = low_back(matmul(low(normed_two), w_proj))
    unit_rows = projected * lax.rsqrt(lax.optimization_barrier(jnp.sum(projected * projected, -1, keepdims=True)) + epsilon)
    return low(low_back(unit_rows)).reshape(seq_count, length, PROJ)

def group_loss(query_embed, passage_embed, passage_lengths, positive_ids):
    similar = low_back(jnp.einsum('aie,cje->aicj', query_embed, passage_embed, precision=lax.Precision.HIGHEST))
    valid_keys = jnp.arange(PLEN, dtype=jnp.int32)[None, :] < passage_lengths[:, None]
    scaled = jnp.where(valid_keys[None, None], similar / temper, masked)
    soft_max = temper * jax.scipy.special.logsumexp(scaled, axis=-1)
    score_rows = lax.optimization_barrier(jnp.sum(soft_max, axis=1))
    candidates = jnp.arange(PDEV * N_PSG, dtype=jnp.int32)
    picked = lax.optimization_barrier(jnp.sum(jnp.where(candidates[None, :] == positive_ids[:, None], score_rows, 0.0), axis=-1))
    return jax.scipy.special.logsumexp(score_rows, axis=-1) - picked

def reference(query_input, passage_input, lengths, positive, w_qkv, bias_q, bias_v, w_out, bias_out, norm1_gain, norm1_bias, w_in, bias_in, w_back, bias_back, norm2_gain, norm2_bias, w_proj):
    params = tuple((weight.astype(jnp.float32) for weight in (w_qkv, bias_q, bias_v, w_out, bias_out, norm1_gain, norm1_bias, w_in, bias_in, w_back, bias_back, norm2_gain, norm2_bias, w_proj)))
    groups = MB * N_GROUP
    query_valid = jnp.ones((QDEV * N_PSG, QLEN), dtype=bool)
    passage_valid = (jnp.arange(PLEN, dtype=jnp.int32)[None, :] < lengths.reshape(-1)[:, None])[:, None, :]

    def forward(weights, queries, passages):
        query_blocks = queries.reshape(groups, QDEV * N_PSG, QLEN, D)
        query_embed = lax.map(jax.checkpoint(lambda member: encode(weights, member, query_valid)), query_blocks)
        passage_blocks = passages.reshape(MB * PASSAGES, 1, PLEN, D)
        passage_embed = lax.map(jax.checkpoint(lambda packed: encode(weights, packed[0], packed[1])), (passage_blocks, passage_valid))
        passage_embed = passage_embed.reshape(groups, PDEV * N_PSG, PLEN, PROJ)
        losses = lax.map(jax.checkpoint(lambda packed: group_loss(packed[0], packed[1], packed[2], packed[3])), (query_embed, passage_embed, lengths.reshape(groups, PDEV * N_PSG), positive.reshape(groups, QDEV * N_PSG)))
        return (losses.reshape(MB, QUERIES), (query_embed.reshape(MB, QUERIES, QLEN, PROJ), passage_embed.reshape(MB, PASSAGES, PLEN, PROJ)))
    losses, pullback, embeds = jax.vjp(forward, params, query_input.astype(jnp.float32), passage_input.astype(jnp.float32), has_aux=True)
    grad_params, grad_queries, grad_passages = pullback(jnp.ones_like(losses))
    return (losses, embeds[0].astype(jnp.bfloat16), embeds[1].astype(jnp.bfloat16), grad_queries.astype(jnp.bfloat16), grad_passages.astype(jnp.bfloat16), grad_params[0], grad_params[1], grad_params[2], grad_params[3], grad_params[4], grad_params[5], grad_params[6], grad_params[7], grad_params[8], grad_params[9], grad_params[10], grad_params[11], grad_params[12], grad_params[13])
```

```python
import jax
import jax.numpy as jnp
from jax import lax
from jax.experimental import pallas as pl
from jax.experimental.pallas import tpu as pltpu
from jax.sharding import PartitionSpec as P

D = 768
H = 12
HD = 64
PROJ = 128
QLEN = 32
PLEN = 256
MB = 2
PDEV = 1
QDEV = 2


temper = 0.1
epsilon = 1e-06
masked = -1e30


def for_sending(shard):

    def short(part):
        return part.astype(jnp.bfloat16) if part.dtype == jnp.float32 else part

    return jax.tree.map(short, shard)


def dense_dot(left_side, right_side):
    return jnp.dot(left_side, right_side, preferred_element_type=jnp.float32)


def outer_dot(left_side, right_side):
    return lax.dot_general(
        left_side, right_side, (((0,), (0,)), ((), ())), preferred_element_type=jnp.float32
    )


def back_dense(left_side, right_side):
    return lax.dot_general(
        left_side, right_side, (((1,), (1,)), ((), ())), preferred_element_type=jnp.float32
    )


def layer_norm(resid_in, gain_vec, shift_vec):
    row_mean = jnp.mean(resid_in, -1, keepdims=True)
    centred = resid_in - row_mean
    inverse = lax.rsqrt(jnp.mean(centred * centred, -1, keepdims=True) + epsilon)
    normal = centred * inverse
    return (normal * gain_vec.astype(jnp.float32) + shift_vec.astype(jnp.float32), normal, inverse)


def norm_back(grad_out, normal, inverse, gain_vec):
    grad_normal = grad_out * gain_vec.astype(jnp.float32)
    grad_in = inverse * (
        grad_normal
        - jnp.mean(grad_normal, -1, keepdims=True)
        - normal * jnp.mean(grad_normal * normal, -1, keepdims=True)
    )
    return (grad_in, jnp.sum(grad_out * normal, 0), jnp.sum(grad_out, 0))


def attention_scores(qkv_split, key_valid):
    scores = (
        jnp.einsum(
            "slhe,smhe->shlm",
            qkv_split[:, :, 0],
            qkv_split[:, :, 1],
            preferred_element_type=jnp.float32,
        )
        * 0.125
    )
    return jnp.where(key_valid[:, None, None, :], scores, masked)


NFULL = 12
CW = 768
MW = 256
MESH = pl.DeviceIdType.MESH


def reduce_kernel(
    back_ref, in_ref, out_ref, qkv_ref, mini_ref,
    back_o, in_o, out_o, qkv_o, mini_o,
    grad, gmini, core_rv, first_a, first_b, second_b, line_rv, cross_rv, done,
    mcore_rv, mfirst_a, mfirst_b, msecond_b, mline_rv, mcross_rv, mdone,
    load_sem, core_s, core_r, one_s, one_r, two_s, two_r,
    rt_s, rt_r, lf_s, lf_r, last_s, last_r, st_sem, fin_s, fin_r,
):
    g = lax.axis_index("group")
    p = lax.axis_index("psg")
    z, y = g // 2, g % 2
    x, c = p // 2, p % 2
    sib = (g, p + 1 - 2 * c)
    ynb = (g + 1 - 2 * y, p)
    xnb = (g, (p + 2) % 4)
    zup = (g + 2, p)
    zdn = (g - 2, p)

    barrier = pltpu.get_barrier_semaphore()
    for other in (sib, ynb, xnb):
        pl.semaphore_signal(barrier, inc=1, device_id=other, device_id_type=MESH)

    @pl.when(z < 3)
    def _():
        pl.semaphore_signal(barrier, inc=1, device_id=zup, device_id_type=MESH)

    @pl.when(z > 0)
    def _():
        pl.semaphore_signal(barrier, inc=1, device_id=zdn, device_id_type=MESH)

    def loads():
        res = []
        for q in range(4):
            res.append((back_ref.at[:, q], grad.at[q]))
        for q in range(4):
            res.append((in_ref.at[:, :, pl.ds(CW * q, CW)], grad.at[4 + q]))
        res.append((out_ref, grad.at[8]))
        for q in range(3):
            res.append((qkv_ref.at[:, :, pl.ds(CW * q, CW)], grad.at[9 + q]))
        res.append((mini_ref, gmini))
        return [pltpu.make_async_copy(a, b, load_sem.at[i]) for i, (a, b) in enumerate(res)]

    for cp in loads():
        cp.start()
    for cp in loads():
        cp.wait()

    ends = jnp.where(z == 0, 1, 0) + jnp.where(z == 3, 1, 0)
    pl.semaphore_wait(barrier, 5 - ends)

    own = pl.ds(pl.multiple_of(c * 48, 16), 48)
    oth = pl.ds(pl.multiple_of((1 - c) * 48, 16), 48)

    def remote(src, dst, ss, rs, dev):
        return pltpu.make_async_remote_copy(
            src_ref=src, dst_ref=dst, send_sem=ss, recv_sem=rs, device_id=dev, device_id_type=MESH
        )

    class Full:
        width = CW

        def __init__(self, k):
            self.k = k
            self.sem = k
            self.g = grad.at[k]
            self.core_rv = core_rv.at[k]
            self.first_a = first_a.at[k]
            self.first_b = first_b.at[k]
            self.second_b = second_b.at[k]
            self.line_rv = line_rv.at[k]
            self.cross_rv = cross_rv.at[k]
            self.done = done.at[k]

    class Mini:
        width = MW

        def __init__(self):
            self.sem = NFULL
            self.g = gmini
            self.core_rv = mcore_rv
            self.first_a = mfirst_a
            self.first_b = mfirst_b
            self.second_b = msecond_b
            self.line_rv = mline_rv
            self.cross_rv = mcross_rv
            self.done = mdone

    def add_into(dst, src):
        dst[...] = (dst[...].astype(jnp.float32) + src[...].astype(jnp.float32)).astype(
            jnp.bfloat16
        )

    def half(u, xx):
        w = u.width // 2
        return pl.ds(pl.multiple_of(xx * w, 128), w)

    def core_copy(u):
        return remote(u.g.at[:, oth, :], u.core_rv, core_s.at[u.sem], core_r.at[u.sem], sib)

    def core_start(u):
        core_copy(u).start()

    def core_end(u):
        core_copy(u).wait_recv()

        def body(i, carry):
            add_into(u.g.at[i, own, :], u.core_rv.at[i])
            return carry

        lax.fori_loop(0, 8, body, 0)

    def one_a(u):
        v = u.g
        return [
            remote(
                v.at[2 * i + 1 - y, own, :],
                u.first_a.at[i],
                one_s.at[4 * u.sem + i],
                one_r.at[4 * u.sem + i],
                ynb,
            )
            for i in range(4)
        ]

    def one_b(u):
        return remote(
            u.g.at[:, own, half(u, 1 - x)],
            u.first_b,
            one_s.at[4 * u.sem],
            one_r.at[4 * u.sem],
            xnb,
        )

    def one_start(u):
        @pl.when(c == 0)
        def _():
            for cp in one_a(u):
                cp.start()

        @pl.when(c == 1)
        def _():
            one_b(u).start()

    def one_end(u):
        @pl.when(c == 0)
        def _():
            for i, cp in enumerate(one_a(u)):
                cp.wait_recv()
                add_into(u.g.at[2 * i + y, own, :], u.first_a.at[i])

        @pl.when(c == 1)
        def _():
            one_b(u).wait_recv()

            def body(i, carry):
                add_into(u.g.at[i, own, half(u, x)], u.first_b.at[i])
                return carry

            lax.fori_loop(0, 8, body, 0)

    def two_b(u):
        return [
            remote(
                u.g.at[2 * i + 1 - y, own, half(u, x)],
                u.second_b.at[i],
                two_s.at[4 * u.sem + i],
                two_r.at[4 * u.sem + i],
                ynb,
            )
            for i in range(4)
        ]

    def two_start(u):
        @pl.when(c == 1)
        def _():
            for cp in two_b(u):
                cp.start()

    def two_end(u):
        @pl.when(c == 1)
        def _():
            for i, cp in enumerate(two_b(u)):
                cp.wait_recv()
                add_into(u.g.at[2 * i + y, own, half(u, x)], u.second_b.at[i])

    def views(u):
        def part_a(d):
            return u.g.at[2 * d + y, own, :]

        def part_b(d):
            return u.g.at[2 * d + y, own, half(u, x)]

        def rv_a(i):
            return u.line_rv.at[i]

        def rv_b(i):
            return u.line_rv.at[i, :, pl.ds(0, u.width // 2)]

        return ((0, part_a, rv_a), (1, part_b, rv_b))

    def up_copy(u, part, rv, d):
        return remote(part(d), rv(d), rt_s.at[4 * u.sem + d], rt_r.at[4 * u.sem + d], zup)

    def down_copy(u, part, rv, d, at):
        return remote(part(d), rv(at), lf_s.at[4 * u.sem + d], lf_r.at[4 * u.sem + d], zdn)

    def line(u, hop):
        for core, part, rv in views(u):
            if hop <= 3:
                @pl.when((c == core) & (z == hop))
                def _():
                    for d in range(3, hop - 1, -1):
                        if hop > 0:
                            up_copy(u, part, rv, d).wait_recv()
                            add_into(part(d), rv(d))
                        if d > hop:
                            up_copy(u, part, rv, d).start()

                @pl.when((c == core) & (z == 3 - hop))
                def _():
                    for d in range(0, 3 - hop + 1):
                        slot = 4 if d == 3 - hop else d
                        if hop > 0:
                            down_copy(u, part, rv, d, slot).wait_recv()
                            add_into(part(d), rv(slot))
                        if d < 3 - hop:
                            to = 4 if d == 3 - hop - 1 else d
                            down_copy(u, part, rv, d, to).start()

    def last_a(u):
        return remote(
            u.g.at[2 * z + y, own, :], u.cross_rv, last_s.at[u.sem], last_r.at[u.sem], xnb
        )

    def last_b(u):
        return remote(
            u.g.at[2 * z + y, own, half(u, x)],
            u.done.at[:, half(u, x)],
            last_s.at[u.sem],
            last_r.at[u.sem],
            xnb,
        )

    def last_start(u):
        @pl.when(c == 0)
        def _():
            last_a(u).start()

        @pl.when(c == 1)
        def _():
            last_b(u).start()

    def last_end(u):
        @pl.when(c == 0)
        def _():
            last_a(u).wait_recv()
            u.done[...] = (
                u.g[2 * z + y, own, :].astype(jnp.float32) + u.cross_rv[...].astype(jnp.float32)
            ).astype(jnp.bfloat16)

        @pl.when(c == 1)
        def _():
            last_b(u).wait_recv()
            u.done[:, half(u, x)] = u.g[2 * z + y, own, half(u, x)]

    def out_copies(k, u):
        if k < 4:
            dst = back_o.at[pl.ds(pl.multiple_of(96 * k + 48 * c, 16), 48), :]
        elif k < 8:
            dst = in_o.at[own, pl.ds(CW * (k - 4), CW)]
        elif k == 8:
            dst = out_o.at[own, :]
        elif k < 12:
            dst = qkv_o.at[own, pl.ds(CW * (k - 9), CW)]
        else:
            dst = mini_o.at[own, :]
        return (
            pltpu.make_async_copy(u.done, dst, st_sem.at[k]),
            remote(u.done, dst, fin_s.at[k], fin_r.at[k], sib),
        )

    stages = [
        core_start,
        lambda u: (core_end(u), one_start(u)),
        lambda u: (one_end(u), two_start(u)),
        two_end,
        lambda u: line(u, 0),
        lambda u: line(u, 1),
        lambda u: line(u, 2),
        lambda u: (line(u, 3), last_start(u)),
        last_end,
    ]
    depth = len(stages)

    mini = Mini()

    def slot(t, carry):
        for s in range(depth - 1, -1, -1):
            k = t - s

            @pl.when((k >= 0) & (k < NFULL))
            def _():
                stages[s](Full(k))

            @pl.when(k == NFULL)
            def _():
                stages[s](mini)

        return carry

    lax.fori_loop(0, NFULL + depth, slot, 0)
    units = [Full(k) for k in range(NFULL)] + [mini]
    for k, u in enumerate(units):
        for cp in out_copies(k, u):
            cp.start()
    for k, u in enumerate(units):
        here, there = out_copies(k, u)
        here.wait()
        there.wait()
        core_copy(u).wait_send()

        @pl.when(c == 0)
        def _():
            for cp in one_a(u):
                cp.wait_send()
            last_a(u).wait_send()

        @pl.when(c == 1)
        def _():
            one_b(u).wait_send()
            for cp in two_b(u):
                cp.wait_send()
            last_b(u).wait_send()

        for core, part, rv in views(u):
            for d in range(4):
                @pl.when((c == core) & (z < d))
                def _():
                    up_copy(u, part, rv, d).wait_send()

                @pl.when((c == core) & (z > d))
                def _():
                    down_copy(u, part, rv, d, d).wait_send()


def reduce_grads(back, w_in, w_out, w_qkv, mini):
    bf = jnp.bfloat16
    shapes = [(384, 768), (96, 3072), (96, 768), (96, 2304), (96, MW)]

    def bufs(lead, w):
        return [
            pltpu.VMEM(lead + (8, 48, w), bf),
            pltpu.VMEM(lead + (4, 48, w), bf),
            pltpu.VMEM(lead + (8, 48, w // 2), bf),
            pltpu.VMEM(lead + (4, 48, w // 2), bf),
            pltpu.VMEM(lead + (5, 48, w), bf),
            pltpu.VMEM(lead + (48, w), bf),
            pltpu.VMEM(lead + (48, w), bf),
        ]

    n = NFULL + 1
    dma = pltpu.SemaphoreType.DMA
    return pl.pallas_call(
        reduce_kernel,
        out_shape=[jax.ShapeDtypeStruct(s, bf) for s in shapes],
        in_specs=[pl.BlockSpec(memory_space=pl.ANY)] * 5,
        out_specs=[pl.BlockSpec(memory_space=pl.ANY)] * 5,
        scratch_shapes=[pltpu.VMEM((NFULL, 8, 96, CW), bf), pltpu.VMEM((8, 96, MW), bf)]
        + bufs((NFULL,), CW)
        + bufs((), MW)
        + [dma((n,))]
        + [dma((n,)), dma((n,))]
        + [dma((4 * n,))] * 8
        + [dma((n,))] * 5,
        compiler_params=pltpu.CompilerParams(
            collective_id=0, has_side_effects=True, vmem_limit_bytes=60 << 20
        ),
        name="reduce_grads",
    )(
        back.reshape(8, 4, 96, 768),
        w_in.reshape(8, 96, 3072),
        w_out.reshape(8, 96, 768),
        w_qkv.reshape(8, 96, 2304),
        mini.reshape(8, 96, MW),
    )

def reduce_sums(terms):
    (
        g_qkv, g_bq, g_bv, g_out, g_bo, g_n1, g_s1, g_in, g_bi, g_back, g_bb, g_n2, g_s2, g_proj,
    ) = terms
    bf = jnp.bfloat16
    small = jnp.stack([g_bq, g_bv, g_bo, g_n1, g_s1, g_bb, g_n2, g_s2], 1)
    wide = g_bi.reshape(8, 4, 96).transpose(0, 2, 1).reshape(768, 4)
    small = jnp.concatenate([small, wide], 1)
    small = jnp.pad(small, ((0, 0), (0, 128 - small.shape[1])))
    mini = jnp.concatenate([g_proj, small], 1)
    back, w_in, w_out, w_qkv, mini = reduce_grads(
        g_back.astype(bf), g_in.astype(bf), g_out.astype(bf), g_qkv.astype(bf), mini.astype(bf)
    )
    f32 = jnp.float32
    small = mini[:, 128:140].astype(f32).T
    return (
        w_qkv.astype(f32),
        small[0],
        small[1],
        w_out.astype(f32),
        small[2],
        small[3],
        small[4],
        w_in.astype(f32),
        small[8:12].reshape(384),
        back.astype(f32),
        small[5],
        small[6],
        small[7],
        mini[:, :128].astype(f32),
    )


def encode(flat_in, valids, params):
    (
        w_qkv,
        bias_q,
        bias_v,
        w_out,
        bias_out,
        gain_one,
        shift_one,
        w_in,
        bias_in,
        w_back,
        bias_back,
        gain_two,
        shift_two,
        w_proj,
    ) = params
    bias_all = jnp.concatenate([bias_q, jnp.zeros_like(bias_q), bias_v]).astype(jnp.float32)
    qkv_low = (dense_dot(flat_in, w_qkv) + bias_all).astype(jnp.bfloat16)
    log_norms, parts = [], []
    start = 0
    for key_valid in valids:
        seq_count, length = key_valid.shape
        rows = seq_count * length
        qkv_split = qkv_low[start : start + rows].reshape(seq_count, length, 3, H, HD)
        scores = attention_scores(qkv_split, key_valid)
        row_top = jnp.max(scores, -1, keepdims=True)
        shifted_exp = jnp.exp(scores - row_top)
        row_sum = jnp.sum(shifted_exp, -1, keepdims=True)
        log_norms.append(row_top + jnp.log(row_sum))
        attn_probs = (shifted_exp / row_sum).astype(jnp.bfloat16)
        attended = jnp.einsum(
            "shlm,smhe->slhe", attn_probs, qkv_split[:, :, 2], preferred_element_type=jnp.float32
        )
        parts.append(attended.reshape(rows, D).astype(jnp.bfloat16))
        start += rows
    attended = jnp.concatenate(parts, 0)
    resid_one = (
        flat_in.astype(jnp.float32) + dense_dot(attended, w_out) + bias_out.astype(jnp.float32)
    )
    normed_one, normal_one, inverse_one = layer_norm(resid_one, gain_one, shift_one)
    normed_low = normed_one.astype(jnp.bfloat16)
    pre_gelu = dense_dot(normed_low, w_in) + bias_in.astype(jnp.float32)
    post_gelu = jax.nn.gelu(pre_gelu, approximate=False).astype(jnp.bfloat16)
    resid_two = normed_one + dense_dot(post_gelu, w_back) + bias_back.astype(jnp.float32)
    normed_two, normal_two, inverse_two = layer_norm(resid_two, gain_two, shift_two)
    second_low = normed_two.astype(jnp.bfloat16)
    projected = dense_dot(second_low, w_proj)
    inv_length = lax.rsqrt(jnp.sum(projected * projected, -1, keepdims=True) + epsilon)
    unit_rows = projected * inv_length
    saved_state = (
        flat_in,
        qkv_low,
        log_norms,
        attended,
        normal_one,
        inverse_one,
        normed_low,
        pre_gelu,
        post_gelu,
        normal_two,
        inverse_two,
        second_low,
        unit_rows,
        inv_length,
    )
    return (unit_rows.astype(jnp.bfloat16), saved_state)


def encode_back(grad_embed, saved_state, valids, params):
    (
        w_qkv,
        bias_q,
        bias_v,
        w_out,
        bias_out,
        gain_one,
        shift_one,
        w_in,
        bias_in,
        w_back,
        bias_back,
        gain_two,
        shift_two,
        w_proj,
    ) = params
    (
        flat_in,
        qkv_low,
        log_norms,
        attended,
        normal_one,
        inverse_one,
        normed_low,
        pre_gelu,
        post_gelu,
        normal_two,
        inverse_two,
        second_low,
        unit_rows,
        inv_length,
    ) = saved_state
    grad_unit = grad_embed.astype(jnp.float32)
    grad_projected = (
        inv_length * (grad_unit - unit_rows * jnp.sum(grad_unit * unit_rows, -1, keepdims=True))
    ).astype(jnp.bfloat16)
    grad_w_proj = outer_dot(second_low, grad_projected)
    grad_normed_two = back_dense(grad_projected, w_proj)
    grad_resid_two, grad_gain_two, grad_shift_two = norm_back(
        grad_normed_two, normal_two, inverse_two, gain_two
    )
    grad_branch_two = grad_resid_two.astype(jnp.bfloat16)
    grad_w_back = outer_dot(post_gelu, grad_branch_two)
    grad_bias_back = jnp.sum(grad_branch_two.astype(jnp.float32), 0)
    gelu_slope = (
        0.5 * (1.0 + lax.erf(pre_gelu * 0.7071067811865476))
        + pre_gelu * jnp.exp(-0.5 * pre_gelu * pre_gelu) * 0.3989422804014327
    )
    grad_pre_gelu = (back_dense(grad_branch_two, w_back) * gelu_slope).astype(jnp.bfloat16)
    grad_w_in = outer_dot(normed_low, grad_pre_gelu)
    grad_bias_in = jnp.sum(grad_pre_gelu.astype(jnp.float32), 0)
    grad_normed_one = back_dense(grad_pre_gelu, w_in) + grad_resid_two
    grad_resid_one, grad_gain_one, grad_shift_one = norm_back(
        grad_normed_one, normal_one, inverse_one, gain_one
    )
    grad_branch_one = grad_resid_one.astype(jnp.bfloat16)
    grad_w_out = outer_dot(attended, grad_branch_one)
    grad_bias_out = jnp.sum(grad_branch_one.astype(jnp.float32), 0)
    grad_attended_all = back_dense(grad_branch_one, w_out).astype(jnp.bfloat16)
    parts = []
    start = 0
    for key_valid, log_norm in zip(valids, log_norms):
        seq_count, length = key_valid.shape
        rows = seq_count * length
        grad_attended = grad_attended_all[start : start + rows].reshape(seq_count, length, H, HD)
        qkv_split = qkv_low[start : start + rows].reshape(seq_count, length, 3, H, HD)
        start += rows
        scores = attention_scores(qkv_split, key_valid)
        probs_full = jnp.exp(scores - log_norm)
        probs_low = probs_full.astype(jnp.bfloat16)
        grad_values = jnp.einsum(
            "shlm,slhe->smhe", probs_low, grad_attended, preferred_element_type=jnp.float32
        )
        grad_probs = jnp.einsum(
            "slhe,smhe->shlm", grad_attended, qkv_split[:, :, 2], preferred_element_type=jnp.float32
        )
        grad_scores = (
            probs_full * (grad_probs - jnp.sum(probs_full * grad_probs, -1, keepdims=True))
        ).astype(jnp.bfloat16)
        grad_queries = (
            jnp.einsum(
                "shlm,smhe->slhe", grad_scores, qkv_split[:, :, 1], preferred_element_type=jnp.float32
            )
            * 0.125
        )
        grad_keys = (
            jnp.einsum(
                "shlm,slhe->smhe", grad_scores, qkv_split[:, :, 0], preferred_element_type=jnp.float32
            )
            * 0.125
        )
        parts.append(
            jnp.stack([grad_queries, grad_keys, grad_values], 2)
            .reshape(rows, 3 * D)
            .astype(jnp.bfloat16)
        )
    grad_qkv = jnp.concatenate(parts, 0)
    grad_w_qkv = outer_dot(flat_in, grad_qkv)
    grad_bias_all = jnp.sum(grad_qkv.astype(jnp.float32), 0)
    grad_input = (back_dense(grad_qkv, w_qkv) + grad_resid_one).astype(jnp.bfloat16)
    weight_terms = (
        grad_w_qkv,
        grad_bias_all[:D],
        grad_bias_all[2 * D :],
        grad_w_out,
        grad_bias_out,
        grad_gain_one,
        grad_shift_one,
        grad_w_in,
        grad_bias_in,
        grad_w_back,
        grad_bias_back,
        grad_gain_two,
        grad_shift_two,
        grad_w_proj,
    )
    return (grad_input, weight_terms)


def body(
    query_input,
    passage_input,
    lengths,
    positive,
    w_qkv,
    bias_q,
    bias_v,
    w_out,
    bias_out,
    norm1_gain,
    norm1_bias,
    w_in,
    bias_in,
    w_back,
    bias_back,
    norm2_gain,
    norm2_bias,
    w_proj,
):
    params = (
        w_qkv,
        bias_q,
        bias_v,
        w_out,
        bias_out,
        norm1_gain,
        norm1_bias,
        w_in,
        bias_in,
        w_back,
        bias_back,
        norm2_gain,
        norm2_bias,
        w_proj,
    )
    psg_index = lax.axis_index("psg")
    mb, qdev, qlen, _ = query_input.shape
    _, pdev, plen, _ = passage_input.shape
    p_rows = mb * pdev * plen
    query_valid = jnp.ones((mb * qdev, qlen), dtype=bool)
    positions = jnp.arange(plen, dtype=jnp.int32)
    passage_valid = positions[None, :] < lengths.reshape(-1)[:, None]
    valids = (passage_valid, query_valid)
    candidates = psg_index * pdev + jnp.arange(pdev, dtype=jnp.int32)
    all_candidates = jnp.arange(pdev * lax.axis_size("psg"), dtype=jnp.int32)
    flat_in = jnp.concatenate([passage_input.reshape(-1, D), query_input.reshape(-1, D)], 0)
    embed, saved = encode(flat_in, valids, params)
    passage_embed = embed[:p_rows].reshape(mb, pdev, plen, PROJ)
    query_embed = embed[p_rows:].reshape(mb, qdev, qlen, PROJ)
    group_queries = lax.all_gather(query_embed, "psg", axis=1, tiled=True)
    similar = jnp.einsum(
        "maie,mcje->maicj", group_queries, passage_embed, preferred_element_type=jnp.float32
    )
    valid_here = passage_valid.reshape(mb, 1, 1, pdev, plen)
    scaled = jnp.where(valid_here, similar / temper, masked)
    sim_top = jnp.max(scaled, -1, keepdims=True)
    sim_exp = jnp.exp(scaled - sim_top)
    sim_sum = jnp.sum(sim_exp, -1, keepdims=True)
    local_scores = jnp.sum(temper * (sim_top[..., 0] + jnp.log(sim_sum[..., 0])), 2)
    local_hits = (positive[:, :, None] == candidates).astype(jnp.float32)
    all_scores = lax.all_gather(local_scores, "psg", axis=2, tiled=True)
    score_top = jnp.max(all_scores, -1, keepdims=True)
    log_total = score_top[..., 0] + jnp.log(jnp.sum(jnp.exp(all_scores - score_top), -1))
    picked = jnp.sum(jnp.where(all_candidates == positive[:, :, None], all_scores, 0.0), -1)
    group_losses = log_total - picked
    losses = lax.dynamic_slice_in_dim(group_losses, psg_index * qdev, qdev, 1)
    grad_score = jnp.exp(local_scores - log_total[..., None]) - local_hits
    grad_similar = (grad_score[:, :, None, :, None] * (sim_exp / sim_sum)).astype(jnp.bfloat16)
    grad_group = jnp.einsum(
        "maicj,mcje->maie", grad_similar, passage_embed, preferred_element_type=jnp.float32
    )
    grad_passage_embed = jnp.einsum(
        "maicj,maie->mcje", grad_similar, group_queries, preferred_element_type=jnp.float32
    ).astype(jnp.bfloat16)
    grad_query_embed = lax.psum_scatter(
        grad_group.astype(jnp.bfloat16), "psg", scatter_dimension=1, tiled=True
    )
    grad_embed = jnp.concatenate(
        [grad_passage_embed.reshape(-1, PROJ), grad_query_embed.reshape(-1, PROJ)], 0
    )
    grad_in, terms = encode_back(grad_embed, saved, valids, params)
    grad_passage_in = grad_in[:p_rows].reshape(passage_input.shape)
    grad_query_in = grad_in[p_rows:].reshape(query_input.shape)
    if lax.axis_size("group") == 8 and lax.axis_size("psg") == 4:
        finals = reduce_sums(terms)
    else:
        shared = lax.psum_scatter(for_sending(terms), "group", scatter_dimension=0, tiled=True)
        finals = jax.tree.map(
            lambda part: part.astype(jnp.float32), lax.psum(for_sending(shared), "psg")
        )
    return (
        losses,
        query_embed,
        passage_embed,
        grad_query_in,
        grad_passage_in,
        finals[0],
        finals[1],
        finals[2],
        finals[3],
        finals[4],
        finals[5],
        finals[6],
        finals[7],
        finals[8],
        finals[9],
        finals[10],
        finals[11],
        finals[12],
        finals[13],
    )


def solution(mesh):
    in_specs = (
        P(None, ("group", "psg"), None, None),
        P(None, ("group", "psg"), None, None),
        P(None, ("group", "psg")),
        P(None, "group"),
        P(),
        P(),
        P(),
        P(),
        P(),
        P(),
        P(),
        P(),
        P(),
        P(),
        P(),
        P(),
        P(),
        P(),
    )
    out_specs = (
        P(None, ("group", "psg")),
        P(None, ("group", "psg"), None, None),
        P(None, ("group", "psg"), None, None),
        P(None, ("group", "psg"), None, None),
        P(None, ("group", "psg"), None, None),
        P("group", None),
        P("group"),
        P("group"),
        P("group", None),
        P("group"),
        P("group"),
        P("group"),
        P("group", None),
        P("group"),
        P("group", None),
        P("group"),
        P("group"),
        P("group"),
        P("group", None),
    )
    return jax.shard_map(body, mesh=mesh, in_specs=in_specs, out_specs=out_specs, check_vma=False)
```

```python
import functools

import jax
import jax.numpy as jnp
from jax import lax
from jax.experimental import pallas as pl
from jax.experimental.pallas import tpu as pltpu
from jax.sharding import PartitionSpec as P

D = 768
HD = 64
FF = 3072
PROJ = 128
QLEN = 32
PLEN = 256
MB = 2
QDEV = 2
PSG = 4

PR = MB * PLEN
QR = MB * QDEV * QLEN
ROWS = PR + QR
PAIRS = D // 128
NC = 12
CW = 768
MW = 256
SHARDS = 8
SR = D // SHARDS
HALF = SR // 2
CORE_SLOTS = 4
SLOTS = 6

temper = 0.1
epsilon = 1e-06
masked = -1e30

MESH = pl.DeviceIdType.MESH
BF = jnp.bfloat16
F32 = jnp.float32


def dot(a, b):
    return jnp.dot(a, b, preferred_element_type=F32)


def dot_nt(a, b):
    return lax.dot_general(a, b, (((1,), (1,)), ((), ())), preferred_element_type=F32)


def dot_tn(a, b):
    return lax.dot_general(a, b, (((0,), (0,)), ((), ())), preferred_element_type=F32)


def at(i, size):
    return pl.ds(pl.multiple_of(i * size, size), size)


def loop(n, body):
    def step(i, carry):
        body(i)
        return carry

    lax.fori_loop(0, n, step, 0)


def fold(v):
    return jnp.sum(v.reshape(v.shape[0] // 8, 8, v.shape[1]), 0)


def remote(src, dst, ss, rs, dev):
    return pltpu.make_async_remote_copy(
        src_ref=src, dst_ref=dst, send_sem=ss, recv_sem=rs, device_id=dev, device_id_type=MESH
    )


V_BO, V_G1, V_S1, V_BB, V_G2, V_S2, V_BI = 3, 4, 5, 6, 7, 8, 9


def forward(r):
    x, qkv = r["x"], r["qkv"]
    vec = r["vec"]
    lane = lax.broadcasted_iota(jnp.int32, (1, 128), 1)
    masks = [(lane < HD).astype(BF), (lane >= HD).astype(BF)]

    def qkv_tile(j):
        b, n = j // 3, j % 3
        acc = dot(x[...], r["wq"][:, at(j, 256)])
        qkv[b, :, at(n, 256)] = (acc + vec[pl.ds(b, 1), at(n, 256)]).astype(BF)

    loop(9, qkv_tile)

    key_at = lax.broadcasted_iota(jnp.int32, (PLEN, PLEN), 1)
    q_row = lax.broadcasted_iota(jnp.int32, (QR, QR), 0) // QLEN
    q_col = lax.broadcasted_iota(jnp.int32, (QR, QR), 1) // QLEN

    def attend(rows, valid, hp, put):
        cols = at(hp, 128)
        q, k, v = qkv[0, rows, cols], qkv[1, rows, cols], qkv[2, rows, cols]
        total = 0.0
        for h in range(2):
            s = dot_nt(q * (masks[h] * 0.125), k)
            s = jnp.where(valid, s, masked)
            e = jnp.exp(s - jnp.max(s, -1, keepdims=True))
            pr = (e * (1.0 / jnp.sum(e, -1, keepdims=True))).astype(BF)
            put(2 * hp + h, pr)
            total = total + dot(pr, v * masks[h])
        r["att"][rows, cols] = total.astype(BF)

    def pair(hp):
        for m in range(MB):

            def put(h, pr, m=m):
                r["pp"][12 * m + h] = pr

            attend(pl.ds(PLEN * m, PLEN), key_at < r["len"][m, 0], hp, put)

        def put_q(h, pr):
            r["pq"][h] = pr

        attend(pl.ds(PR, QR), q_row == q_col, hp, put_q)

    loop(PAIRS, pair)

    def resid_one(n):
        cols = at(n, 256)
        acc = dot(r["att"][...], r["wo"][:, cols])
        r["n1"][:, cols] = x[:, cols].astype(F32) + acc + vec[V_BO : V_BO + 1, cols]

    loop(3, resid_one)

    def norm(h):
        c = h - jnp.mean(h, -1, keepdims=True)
        inv = lax.rsqrt(jnp.mean(c * c, -1, keepdims=True) + epsilon)
        return c * inv, inv

    def norm_one(i):
        rows = at(i, 64)
        n, inv = norm(r["n1"][rows, :])
        r["n1"][rows, :] = n
        r["i1"][rows, :] = inv
        r["nl"][rows, :] = (n * vec[V_G1 : V_G1 + 1, :] + vec[V_S1 : V_S1 + 1, :]).astype(BF)

    loop(ROWS // 64, norm_one)

    def ffn(j):
        b, n = j // 3, j % 3
        cols = at(n, 256)
        pre = dot(r["nl"][...], r["wi"][:, at(j, 256)]) + vec[pl.ds(V_BI + b, 1), cols]
        cdf = 0.5 * (1.0 + lax.erf(pre * 0.7071067811865476))
        r["slope"][b, :, cols] = (
            cdf + pre * jnp.exp(-0.5 * pre * pre) * 0.3989422804014327
        ).astype(BF)
        post = (pre * cdf).astype(BF)
        full = ROWS // SR
        r["grad"][4 + b, 0:full, :, cols] = post[: full * SR].reshape(full, SR, 256)
        r["grad"][4 + b, full, 0 : ROWS - full * SR, cols] = post[full * SR :]

    loop(FF // 256, ffn)

    def resid_two(n):
        cols = at(n, 256)
        acc = r["n1"][:, cols] * vec[V_G1 : V_G1 + 1, cols] + vec[V_S1 : V_S1 + 1, cols]
        acc = acc + vec[V_BB : V_BB + 1, cols]
        for b in range(4):
            acc = acc + dot(post_block(r, b, pl.ds(0, CW)), r["wb"][b, :, cols])
        r["n2"][:, cols] = acc

    loop(3, resid_two)

    def norm_two(i):
        rows = at(i, 64)
        n, inv = norm(r["n2"][rows, :])
        r["n2"][rows, :] = n
        r["i2"][rows, :] = inv
        r["s2"][rows, :] = (n * vec[V_G2 : V_G2 + 1, :] + vec[V_S2 : V_S2 + 1, :]).astype(BF)

    loop(ROWS // 64, norm_two)
    proj = dot(r["s2"][...], r["wp"][...])
    il = lax.rsqrt(jnp.sum(proj * proj, -1, keepdims=True) + epsilon)
    unit = proj * il
    r["il"][...] = il
    r["unit"][...] = unit
    r["emb"][...] = unit.astype(BF)


def post_block(r, b, cols):
    full = ROWS // SR
    w = cols.size
    top = r["grad"][4 + b, 0:full, :, cols].reshape(full * SR, w)
    return jnp.concatenate([top, r["grad"][4 + b, full, 0 : ROWS - full * SR, cols]], 0)


def maxsim(r, g, p):
    emb = r["emb"]

    def peers(src, buf, ss, rs):
        copies = []
        for o in range(1, PSG):
            to = (p + o) % PSG
            copies.append(remote(src(to), buf.at[p], ss.at[o - 1], rs.at[o - 1], (g, to)))
        return copies

    queries = peers(lambda to: emb.at[pl.ds(PR, QR), :], r["gq"], r["q_s"], r["q_r"])
    for cp in queries:
        cp.start()
    r["gq"][p] = emb[PR:ROWS, :]

    def turn(i):
        b, half = i // 2, i % 2
        t = post_block(r, b, at(half, 384)).T
        for q in range(4):
            r["grad"][8 + q, i, :, 0:ROWS] = t[SR * q : SR * (q + 1)]

    loop(SHARDS, turn)
    for cp in queries:
        cp.wait_recv()

    key_at = lax.broadcasted_iota(jnp.int32, (PSG * QDEV * QLEN, PLEN), 1)
    nq = PSG * QDEV
    half = QDEV * QLEN
    sums = []
    for m in range(MB):
        gq = jnp.concatenate([r["gq"][d, half * m : half * (m + 1), :] for d in range(PSG)], 0)
        s = dot_nt(gq, emb[PLEN * m : PLEN * (m + 1), :])
        e = jnp.where(key_at < r["len"][m, 0], jnp.exp(s * (1.0 / temper)), 0.0)
        total = jnp.sum(e, -1, keepdims=True)
        r["sim"][m] = e
        sums.append(total)
        log = jnp.broadcast_to(jnp.log(total), (nq * QLEN, 128))
        r["sc"][p, nq * m : nq * (m + 1), :] = temper * jnp.sum(log.reshape(nq, QLEN, 128), 1)
    scores = peers(lambda to: r["sc"].at[p], r["sc"], r["s_s"], r["s_r"])
    for cp in scores:
        cp.start()
    for cp in scores:
        cp.wait()
    every = [r["sc"][d] for d in range(PSG)]
    top = functools.reduce(jnp.maximum, every)
    log_total = top + jnp.log(sum(jnp.exp(v - top) for v in every))
    pos = r["pos"][...]
    picked = sum(jnp.where(pos == d, every[d], 0.0) for d in range(PSG))
    r["lo"][...] = log_total - picked
    grad_score = jnp.exp(r["sc"][p] - log_total) - (pos == p).astype(F32)
    for m in range(MB):
        gs = grad_score[nq * m : nq * (m + 1)]
        gs = jnp.broadcast_to(gs[:, None, :], (nq, QLEN, 128)).reshape(nq * QLEN, 128)
        coef = gs * (1.0 / sums[m])
        coef = jnp.concatenate([coef, coef], 1)
        ds = (coef * r["sim"][m]).astype(BF)
        pe = emb[PLEN * m : PLEN * (m + 1), :]
        gg = dot(ds, pe).astype(BF)
        for d in range(PSG):
            r["gg"][d, half * m : half * (m + 1), :] = gg[half * d : half * (d + 1)]
        gq = jnp.concatenate([r["gq"][d, half * m : half * (m + 1), :] for d in range(PSG)], 0)
        r["de"][PLEN * m : PLEN * (m + 1), :] = dot_tn(ds, gq).astype(BF)
    backs = peers(lambda to: r["gg"].at[to], r["gr"], r["g_s"], r["g_r"])
    for cp in backs:
        cp.start()
    r["gr"][p] = r["gg"][p]
    for cp in backs:
        cp.wait()
    for cp in queries:
        cp.wait_send()
    r["de"][PR:ROWS, :] = sum(r["gr"][d].astype(F32) for d in range(PSG)).astype(BF)


def norm_back(grad_out, n, inv, gain):
    gn = grad_out * gain
    return inv * (
        gn - jnp.mean(gn, -1, keepdims=True) - n * jnp.mean(gn * n, -1, keepdims=True)
    )


def head_back(r):
    vec = r["vec"]
    gu = r["de"][...].astype(F32)
    unit = r["unit"][...]
    r["gp"][...] = (r["il"][...] * (gu - unit * jnp.sum(gu * unit, -1, keepdims=True))).astype(BF)

    def body(i, sums):
        rows = at(i, 64)
        g2 = dot_nt(r["gp"][rows, :], r["wp"][...])
        n = r["n2"][rows, :]
        gr = norm_back(g2, n, r["i2"][rows, :], vec[V_G2 : V_G2 + 1, :])
        low = gr.astype(BF)
        r["n2"][rows, :] = gr
        r["gb"][rows, :] = low
        add = (fold(low.astype(F32)), fold(g2 * n), fold(g2))
        return tuple(a + b for a, b in zip(sums, add))

    zero = jnp.zeros((8, D), F32)
    sums = lax.fori_loop(0, ROWS // 64, body, (zero, zero, zero))
    for row, v in zip((5, 6, 7), sums):
        r["sm"][row : row + 1, :] = jnp.sum(v, 0, keepdims=True)


def backward_step(r, t):
    vec, qkv, grad = r["vec"], r["qkv"], r["grad"]
    lane = lax.broadcasted_iota(jnp.int32, (1, 128), 1)
    masks = [(lane < HD).astype(BF), (lane >= HD).astype(BF)]

    def outer(left, right, k, n):
        grad[k, :, :, at(n, 256)] = dot(left, right).astype(BF).reshape(SHARDS, SR, 256)

    def turn(src, n):
        r["lt"][at(n, 256), :] = src[:, at(n, 256)].T

    @pl.when(t < 4)
    def _():
        def tile(n):
            left = grad[8 + t, :, :, 0:ROWS].reshape(CW, ROWS)
            outer(left, r["gb"][:, at(n, 256)], t, n)

        loop(3, tile)

    @pl.when(t == 4)
    def _():
        loop(3, lambda n: turn(r["nl"], n))

    @pl.when((t >= 4) & (t < 8))
    def _():
        b = t - 4

        def tile(n):
            cols = at(n, 256)
            v = dot_nt(r["gb"][...], r["wb"][b, cols, :]) * r["slope"][b, :, cols].astype(F32)
            low = v.astype(BF)
            r["slope"][b, :, cols] = low
            r["sm"][pl.ds(8 + b, 1), cols] = jnp.sum(low.astype(F32), 0, keepdims=True)
            outer(r["lt"][...], low, 4 + b, n)

        loop(3, tile)

    @pl.when(t == 8)
    def _():
        loop(3, lambda n: turn(r["s2"], n))
        v = dot(r["lt"][...], r["gp"][...]).astype(BF)
        r["gmini"][:, :, 0:PROJ] = v.reshape(SHARDS, SR, PROJ)

    @pl.when((t >= 8) & (t < 11))
    def _():
        n = t - 8
        cols = at(n, 256)
        acc = r["n2"][:, cols]
        for b in range(4):
            acc = acc + dot_nt(r["slope"][b], r["wi"][cols, CW * b : CW * (b + 1)])
        r["n2"][:, cols] = acc

    @pl.when(t == 11)
    def _():
        def body(i, sums):
            rows = at(i, 64)
            g1, n = r["n2"][rows, :], r["n1"][rows, :]
            gr = norm_back(g1, n, r["i1"][rows, :], vec[V_G1 : V_G1 + 1, :])
            low = gr.astype(BF)
            r["n1"][rows, :] = gr
            r["gb"][rows, :] = low
            add = (fold(low.astype(F32)), fold(g1 * n), fold(g1))
            return tuple(a + b for a, b in zip(sums, add))

        zero = jnp.zeros((8, D), F32)
        sums = lax.fori_loop(0, ROWS // 64, body, (zero, zero, zero))
        for row, v in zip((2, 3, 4), sums):
            r["sm"][row : row + 1, :] = jnp.sum(v, 0, keepdims=True)
        loop(3, lambda n: turn(r["att"], n))
        loop(3, lambda n: outer(r["lt"][...], r["gb"][:, at(n, 256)], 8, n))

    @pl.when(t == 12)
    def _():
        def tile(n):
            r["att"][:, at(n, 256)] = dot_nt(r["gb"][...], r["wo"][at(n, 256), :]).astype(BF)

        loop(3, tile)
        loop(3, lambda n: turn(r["x"], n))

    def attend_back(rows, hp, take):
        cols = at(hp, 128)
        q, k, v = qkv[0, rows, cols], qkv[1, rows, cols], qkv[2, rows, cols]
        a = r["att"][rows, cols]
        dq = dk = dv = 0.0
        for h in range(2):
            pr = take(2 * hp + h)
            ah = a * masks[h]
            dp = dot_nt(ah, v)
            pf = pr.astype(F32)
            ds = (pf * (dp - jnp.sum(pf * dp, -1, keepdims=True))).astype(BF)
            dq = dq + dot(ds, k * masks[h])
            dk = dk + dot_tn(ds, q * masks[h])
            dv = dv + dot_tn(pr, ah)
        dq = (dq * 0.125).astype(BF)
        dv = dv.astype(BF)
        qkv[0, rows, cols] = dq
        qkv[1, rows, cols] = (dk * 0.125).astype(BF)
        qkv[2, rows, cols] = dv
        return (
            jnp.sum(dq.astype(F32), 0, keepdims=True),
            jnp.sum(dv.astype(F32), 0, keepdims=True),
        )

    @pl.when((t >= 13) & (t < 13 + PAIRS))
    def _():
        hp = t - 13
        cols = at(hp, 128)
        bq, bv = attend_back(pl.ds(PR, QR), hp, lambda h: r["pq"][h])
        for m in range(MB):
            one, two = attend_back(
                pl.ds(PLEN * m, PLEN), hp, lambda h, m=m: r["pp"][12 * m + h]
            )
            bq, bv = bq + one, bv + two
        r["sm"][0:1, cols] = bq
        r["sm"][1:2, cols] = bv

    @pl.when((t == 14) | (t == 16) | (t == 18))
    def _():
        i = (t - 14) // 2
        loop(3, lambda b: outer(r["lt"][...], qkv[b, :, at(i, 256)], 9 + i, b))

    @pl.when(t == 19)
    def _():
        small = r["sm"][...].T
        one = lax.broadcasted_iota(jnp.int32, (SR, 128), 1)
        pad = jnp.zeros((SR, 128 - small.shape[1]), F32)
        for s in range(SHARDS):
            v = jnp.concatenate([small[SR * s : SR * (s + 1)], pad], 1)
            b, base = s // 2, 384 * (s % 2)
            v = jnp.where(one < 8, v, 0.0)
            for q in range(4):
                col = small[base + SR * q : base + SR * (q + 1), 8 + b : 9 + b]
                v = jnp.where(one == 8 + q, col, v)
            r["gmini"][s, :, PROJ:MW] = v.astype(BF)

    @pl.when((t >= 20) & (t < 23))
    def _():
        n = t - 20
        cols = at(n, 256)
        acc = r["n1"][:, cols]
        for b in range(3):
            acc = acc + dot_nt(qkv[b], r["wq"][cols, CW * b : CW * (b + 1)])
        r["gb"][:, cols] = acc.astype(BF)


def chunk_at(u):
    k = jnp.where((u >= 0) & (u < 8), u, -1)
    for step, which in ((11, 8), (14, 9), (16, 10), (18, 11), (19, NC)):
        k = jnp.where(u == step, which, k)
    return k


LAST_ENTER = 19


class Reducer:
    def __init__(self, r, g, p):
        self.r = r
        self.z, self.y = g // 2, g % 2
        self.x, self.c = p // 2, p % 2
        z, y, x, c = self.z, self.y, self.x, self.c
        self.sib = (g, p + 1 - 2 * c)
        self.ynb = (g + 1 - 2 * y, p)
        self.xnb = (g, (p + 2) % 4)
        self.zup = (g + 2, p)
        self.zdn = (g - 2, p)
        self.own = pl.ds(pl.multiple_of(c * HALF, 16), HALF)
        self.oth = pl.ds(pl.multiple_of((1 - c) * HALF, 16), HALF)

    def unit(self, k):
        r = self.r
        u = lambda: None
        u.k = k
        if isinstance(k, int) and k == NC:
            u.width = MW
            u.g = r["gmini"]
            for name in ("core_rv", "first_a", "first_b", "second_b", "line_rv", "cross_rv", "done"):
                setattr(u, name, r["m_" + name])
        else:
            u.width = CW
            u.g = r["grad"].at[k]
            u.core_rv = r["core_rv"].at[k % CORE_SLOTS]
            for name in ("first_a", "first_b", "line_rv"):
                setattr(u, name, r[name].at[k % SLOTS])
            for name in ("second_b", "cross_rv", "done"):
                setattr(u, name, r[name].at[k])
        return u

    def add_into(self, dst, src):
        dst[...] = (dst[...].astype(F32) + src[...].astype(F32)).astype(BF)

    def half(self, u, xx):
        w = u.width // 2
        return pl.ds(pl.multiple_of(xx * w, 128), w)

    def core_copy(self, u):
        r = self.r
        return remote(
            u.g.at[:, self.oth, :], u.core_rv, r["c_s"].at[u.k], r["c_r"].at[u.k], self.sib
        )

    def core_end(self, u):
        self.core_copy(u).wait_recv()
        loop(SHARDS, lambda i: self.add_into(u.g.at[i, self.own, :], u.core_rv.at[i]))

    def one_a(self, u, i):
        r = self.r
        return remote(
            u.g.at[2 * i + 1 - self.y, self.own, :],
            u.first_a.at[i],
            r["one_s"].at[4 * u.k + i],
            r["one_r"].at[4 * u.k + i],
            self.ynb,
        )

    def one_b(self, u):
        r = self.r
        return remote(
            u.g.at[:, self.own, self.half(u, 1 - self.x)],
            u.first_b,
            r["one_s"].at[4 * u.k],
            r["one_r"].at[4 * u.k],
            self.xnb,
        )

    def one_start(self, u):
        @pl.when(self.c == 0)
        def _():
            loop(4, lambda i: self.one_a(u, i).start())

        @pl.when(self.c == 1)
        def _():
            self.one_b(u).start()

    def one_end(self, u):
        @pl.when(self.c == 0)
        def _():
            def body(i):
                self.one_a(u, i).wait_recv()
                self.add_into(u.g.at[2 * i + self.y, self.own, :], u.first_a.at[i])

            loop(4, body)

        @pl.when(self.c == 1)
        def _():
            self.one_b(u).wait_recv()
            mine = self.half(u, self.x)
            loop(
                SHARDS,
                lambda i: self.add_into(u.g.at[i, self.own, mine], u.first_b.at[i]),
            )

    def two_b(self, u, i):
        r = self.r
        return remote(
            u.g.at[2 * i + 1 - self.y, self.own, self.half(u, self.x)],
            u.second_b.at[i],
            r["two_s"].at[4 * u.k + i],
            r["two_r"].at[4 * u.k + i],
            self.ynb,
        )

    def two_start(self, u):
        @pl.when(self.c == 1)
        def _():
            loop(4, lambda i: self.two_b(u, i).start())

    def two_end(self, u):
        @pl.when(self.c == 1)
        def _():
            def body(i):
                self.two_b(u, i).wait_recv()
                self.add_into(
                    u.g.at[2 * i + self.y, self.own, self.half(u, self.x)], u.second_b.at[i]
                )

            loop(4, body)

    def views(self, u):
        def part_a(d):
            return u.g.at[2 * d + self.y, self.own, :]

        def part_b(d):
            return u.g.at[2 * d + self.y, self.own, self.half(u, self.x)]

        def rv_a(i):
            return u.line_rv.at[i]

        def rv_b(i):
            return u.line_rv.at[i, :, pl.ds(0, u.width // 2)]

        return ((0, part_a, rv_a), (1, part_b, rv_b))

    def up_copy(self, u, part, rv, d):
        r, s = self.r, 4 * u.k + d
        return remote(part(d), rv(d), r["up_s"].at[s], r["up_r"].at[s], self.zup)

    def down_copy(self, u, part, rv, d, slot):
        r, s = self.r, 4 * u.k + d
        return remote(part(d), rv(slot), r["dn_s"].at[s], r["dn_r"].at[s], self.zdn)

    def line(self, u, hop):
        z, c = self.z, self.c
        for core, part, rv in self.views(u):

            @pl.when((c == core) & (z == hop))
            def _():
                for d in range(3, hop - 1, -1):
                    if hop > 0:
                        self.up_copy(u, part, rv, d).wait_recv()
                        self.add_into(part(d), rv(d))
                    if d > hop:
                        self.up_copy(u, part, rv, d).start()

            @pl.when((c == core) & (z == 3 - hop))
            def _():
                for d in range(0, 3 - hop + 1):
                    slot = 4 if d == 3 - hop else d
                    if hop > 0:
                        self.down_copy(u, part, rv, d, slot).wait_recv()
                        self.add_into(part(d), rv(slot))
                    if d < 3 - hop:
                        self.down_copy(u, part, rv, d, 4 if d == 2 - hop else d).start()

    def last_a(self, u):
        r = self.r
        return remote(
            u.g.at[2 * self.z + self.y, self.own, :],
            u.cross_rv,
            r["last_s"].at[u.k],
            r["last_r"].at[u.k],
            self.xnb,
        )

    def last_b(self, u):
        r = self.r
        mine = self.half(u, self.x)
        return remote(
            u.g.at[2 * self.z + self.y, self.own, mine],
            u.done.at[:, mine],
            r["last_s"].at[u.k],
            r["last_r"].at[u.k],
            self.xnb,
        )

    def last_start(self, u):
        @pl.when(self.c == 0)
        def _():
            self.last_a(u).start()

        @pl.when(self.c == 1)
        def _():
            self.last_b(u).start()

    def last_end(self, u):
        here = 2 * self.z + self.y

        @pl.when(self.c == 0)
        def _():
            self.last_a(u).wait_recv()
            u.done[...] = (
                u.g[here, self.own, :].astype(F32) + u.cross_rv[...].astype(F32)
            ).astype(BF)

        @pl.when(self.c == 1)
        def _():
            mine = self.half(u, self.x)
            self.last_b(u).wait_recv()
            u.done[:, mine] = u.g[here, self.own, mine]

    def to_outputs(self, u, do):
        r, k, own = self.r, u.k, self.own

        def both(src, dst, i=0):
            s = 3 * k + i
            do(pltpu.make_async_copy(src, dst, r["st_sem"].at[s]))
            do(remote(src, dst, r["fin_s"].at[s], r["fin_r"].at[s], self.sib))

        if isinstance(k, int) and k == NC:
            both(u.done, r["mini_o"].at[own, :])
            return

        @pl.when(k < 4)
        def _():
            rows = pl.ds(pl.multiple_of(SR * k + HALF * self.c, 16), HALF)
            both(u.done, r["back_o"].at[rows, :])

        @pl.when((k >= 4) & (k < 8))
        def _():
            both(u.done, r["in_o"].at[own, at(k - 4, CW)])

        @pl.when(k == 8)
        def _():
            both(u.done, r["out_o"].at[own, :])

        @pl.when(k > 8)
        def _():
            for b in range(3):
                cols = pl.ds(pl.multiple_of(CW * b + 256 * (k - 9), 256), 256)
                both(u.done.at[:, 256 * b : 256 * (b + 1)], r["qkv_o"].at[own, cols], b)

    def stages(self):
        return [
            lambda u: self.core_copy(u).start(),
            lambda u: (self.core_end(u), self.one_start(u)),
            lambda u: (self.one_end(u), self.two_start(u)),
            self.two_end,
            lambda u: self.line(u, 0),
            lambda u: self.line(u, 1),
            lambda u: self.line(u, 2),
            lambda u: (self.line(u, 3), self.last_start(u)),
            lambda u: (self.last_end(u), self.to_outputs(u, lambda cp: cp.start())),
        ]

    def slot(self, t):
        stages = self.stages()
        for s in range(len(stages) - 1, -1, -1):
            k = chunk_at(t - s)

            @pl.when((k >= 0) & (k < NC))
            def _():
                stages[s](self.unit(k))

            @pl.when(k == NC)
            def _():
                stages[s](self.unit(NC))

    def finish(self, u):
        self.to_outputs(u, lambda cp: cp.wait())
        self.core_copy(u).wait_send()

        @pl.when(self.c == 0)
        def _():
            loop(4, lambda i: self.one_a(u, i).wait_send())
            self.last_a(u).wait_send()

        @pl.when(self.c == 1)
        def _():
            self.one_b(u).wait_send()
            loop(4, lambda i: self.two_b(u, i).wait_send())
            self.last_b(u).wait_send()

        for core, part, rv in self.views(u):
            for d in range(4):

                @pl.when((self.c == core) & (self.z < d))
                def _():
                    self.up_copy(u, part, rv, d).wait_send()

                @pl.when((self.c == core) & (self.z > d))
                def _():
                    self.down_copy(u, part, rv, d, d).wait_send()


INPUTS = ("len", "pos", "vec", "xp_h", "xq_h", "wq_h", "wo_h", "wi_h", "wb_h", "wp_h")


def kernel(spread, names, *refs):
    r = dict(zip(names, refs))
    g = lax.axis_index("group")
    p = lax.axis_index("psg")
    barrier = pltpu.get_barrier_semaphore()

    def greet(dev):
        pl.semaphore_signal(barrier, inc=1, device_id=dev, device_id_type=MESH)

    for o in range(1, PSG):
        greet((g, (p + o) % PSG))
    count = PSG - 1
    if spread:
        red = Reducer(r, g, p)
        greet(red.ynb)

        @pl.when(red.z < 3)
        def _():
            greet(red.zup)

        @pl.when(red.z > 0)
        def _():
            greet(red.zdn)

        count = count + 3 - jnp.where(red.z == 0, 1, 0) - jnp.where(red.z == 3, 1, 0)

    pairs = [
        (r["xp_h"], r["x"].at[pl.ds(0, PR), :]),
        (r["xq_h"], r["x"].at[pl.ds(PR, QR), :]),
        (r["wq_h"], r["wq"]),
        (r["wo_h"], r["wo"]),
        (r["wi_h"], r["wi"]),
        (r["wb_h"], r["wb"]),
        (r["wp_h"], r["wp"]),
    ]
    loads = [pltpu.make_async_copy(a, b, r["in_sem"].at[i]) for i, (a, b) in enumerate(pairs)]
    for cp in loads:
        cp.start()
    for cp in loads:
        cp.wait()
    forward(r)
    pl.semaphore_wait(barrier, count)
    maxsim(r, g, p)
    r["loss_o"][...] = jnp.concatenate(
        [r["lo"][pl.ds(PSG * QDEV * m + QDEV * p, QDEV), :] for m in range(MB)], 0
    )
    head_back(r)

    def step(t):
        backward_step(r, t)
        if spread:
            red.slot(t)

    loop(LAST_ENTER + 9 if spread else 23, step)

    outs = [
        (r["emb"].at[pl.ds(0, PR), :], r["ep_o"]),
        (r["emb"].at[pl.ds(PR, QR), :], r["eq_o"]),
        (r["gb"].at[pl.ds(0, PR), :], r["gxp_o"]),
        (r["gb"].at[pl.ds(PR, QR), :], r["gxq_o"]),
    ]
    if not spread:
        outs += [(r["grad"], r["grad_o"]), (r["gmini"], r["mini_o"])]
    stores = [pltpu.make_async_copy(a, b, r["out_sem"].at[i]) for i, (a, b) in enumerate(outs)]
    for cp in stores:
        cp.start()
    for cp in stores:
        cp.wait()
    if spread:
        loop(NC, lambda k: red.finish(red.unit(k)))
        red.finish(red.unit(NC))


def run_step(spread, inputs):
    sds = jax.ShapeDtypeStruct
    outs = {
        "loss_o": sds((MB * QDEV, 128), F32),
        "eq_o": sds((QR, PROJ), BF),
        "ep_o": sds((PR, PROJ), BF),
        "gxq_o": sds((QR, D), BF),
        "gxp_o": sds((PR, D), BF),
    }
    if spread:
        outs |= {
            "back_o": sds((4 * SR, D), BF),
            "in_o": sds((SR, FF), BF),
            "out_o": sds((SR, D), BF),
            "qkv_o": sds((SR, 3 * D), BF),
            "mini_o": sds((SR, MW), BF),
        }
    else:
        outs |= {
            "grad_o": sds((NC, SHARDS, SR, CW), BF),
            "mini_o": sds((SHARDS, SR, MW), BF),
        }
    vm = pltpu.VMEM
    dma = pltpu.SemaphoreType.DMA
    scratch = {
        "x": vm((ROWS, D), BF),
        "wq": vm((D, 3 * D), BF),
        "wo": vm((D, D), BF),
        "wi": vm((D, FF), BF),
        "wb": vm((4, CW, D), BF),
        "wp": vm((D, PROJ), BF),
        "qkv": vm((3, ROWS, D), BF),
        "pp": vm((MB * 12, PLEN, PLEN), BF),
        "pq": vm((12, QR, QR), BF),
        "att": vm((ROWS, D), BF),
        "n1": vm((ROWS, D), F32),
        "n2": vm((ROWS, D), F32),
        "i1": vm((ROWS, 1), F32),
        "i2": vm((ROWS, 1), F32),
        "il": vm((ROWS, 1), F32),
        "nl": vm((ROWS, D), BF),
        "slope": vm((4, ROWS, CW), BF),
        "s2": vm((ROWS, D), BF),
        "unit": vm((ROWS, PROJ), F32),
        "emb": vm((ROWS, PROJ), BF),
        "de": vm((ROWS, PROJ), BF),
        "gp": vm((ROWS, PROJ), BF),
        "gb": vm((ROWS, D), BF),
        "lt": vm((D, ROWS), BF),
        "sm": vm((16, D), F32),
        "gq": vm((PSG, QR, PROJ), BF),
        "sim": vm((MB, PSG * QDEV * QLEN, PLEN), F32),
        "sc": vm((PSG, MB * PSG * QDEV, 128), F32),
        "lo": vm((MB * PSG * QDEV, 128), F32),
        "gg": vm((PSG, QR, PROJ), BF),
        "gr": vm((PSG, QR, PROJ), BF),
        "grad": vm((NC, SHARDS, SR, CW), BF),
        "gmini": vm((SHARDS, SR, MW), BF),
        "in_sem": dma((7,)),
        "out_sem": dma((6,)),
    }
    for name in ("q_s", "q_r", "s_s", "s_r", "g_s", "g_r"):
        scratch[name] = dma((PSG - 1,))
    if spread:
        for lead, slots, w, pre in ((True, (CORE_SLOTS, SLOTS, NC), CW, ""), (False, None, MW, "m_")):
            a, b, c = ((slots[0],), (slots[1],), (slots[2],)) if lead else ((), (), ())
            scratch[pre + "core_rv"] = vm(a + (SHARDS, HALF, w), BF)
            scratch[pre + "first_a"] = vm(b + (4, HALF, w), BF)
            scratch[pre + "first_b"] = vm(b + (SHARDS, HALF, w // 2), BF)
            scratch[pre + "second_b"] = vm(c + (4, HALF, w // 2), BF)
            scratch[pre + "line_rv"] = vm(b + (5, HALF, w), BF)
            scratch[pre + "cross_rv"] = vm(c + (HALF, w), BF)
            scratch[pre + "done"] = vm(c + (HALF, w), BF)
        n = NC + 1
        for name in ("c_s", "c_r", "last_s", "last_r"):
            scratch[name] = dma((n,))
        for name in ("one_s", "one_r", "two_s", "two_r", "up_s", "up_r", "dn_s", "dn_r"):
            scratch[name] = dma((4 * n,))
        for name in ("st_sem", "fin_s", "fin_r"):
            scratch[name] = dma((3 * n,))
    hbm = pl.BlockSpec(memory_space=pl.ANY)
    vmem = pl.BlockSpec(memory_space=pltpu.VMEM)
    smem = pl.BlockSpec(memory_space=pltpu.SMEM)
    names = INPUTS + tuple(outs) + tuple(scratch)
    res = pl.pallas_call(
        functools.partial(kernel, spread, names),
        out_shape=list(outs.values()),
        in_specs=[smem, vmem, vmem] + [hbm] * 7,
        out_specs=[vmem] + [hbm] * (len(outs) - 1),
        scratch_shapes=list(scratch.values()),
        compiler_params=pltpu.CompilerParams(
            collective_id=0, has_side_effects=True, vmem_limit_bytes=64 << 20
        ),
        name="train_step",
    )(*inputs)
    return dict(zip(outs, res))


def body(
    query_input,
    passage_input,
    lengths,
    positive,
    w_qkv,
    bias_q,
    bias_v,
    w_out,
    bias_out,
    norm1_gain,
    norm1_bias,
    w_in,
    bias_in,
    w_back,
    bias_back,
    norm2_gain,
    norm2_bias,
    w_proj,
):
    spread = lax.axis_size("group") == SHARDS
    rows = [
        bias_q,
        jnp.zeros_like(bias_q),
        bias_v,
        bias_out,
        norm1_gain,
        norm1_bias,
        bias_back,
        norm2_gain,
        norm2_bias,
        bias_in,
    ]
    vec = jnp.concatenate(rows).astype(F32).reshape(13, D)
    pos = jnp.broadcast_to(positive.reshape(-1, 1), (positive.size, 128))
    inputs = (
        lengths,
        pos,
        vec,
        passage_input.reshape(PR, D),
        query_input.reshape(QR, D),
        w_qkv,
        w_out,
        w_in,
        w_back.reshape(4, CW, D),
        w_proj,
    )
    o = run_step(spread, inputs)
    if spread:
        small = o["mini_o"][:, PROJ : PROJ + 12].astype(F32).T
        finals = (
            o["qkv_o"],
            small[0],
            small[1],
            o["out_o"],
            small[2],
            small[3],
            small[4],
            o["in_o"],
            small[8:12].reshape(4 * SR),
            o["back_o"],
            small[5],
            small[6],
            small[7],
            o["mini_o"][:, :PROJ],
        )
    else:
        full = o["grad_o"].reshape(NC, SHARDS, SR, CW)
        mini = o["mini_o"].reshape(D, MW)
        small = mini[:, PROJ : PROJ + 8]
        wide = o["mini_o"][:, :, PROJ + 8 : PROJ + 12].transpose(0, 2, 1).reshape(FF)
        halves = full[9:12].reshape(3, D, 3, 256).transpose(1, 2, 0, 3).reshape(D, 3 * D)
        terms = (
            halves,
            small[:, 0],
            small[:, 1],
            full[8].reshape(D, D),
            small[:, 2],
            small[:, 3],
            small[:, 4],
            full[4:8].reshape(4, D, CW).transpose(1, 0, 2).reshape(D, FF),
            wide,
            full[0:4].transpose(1, 0, 2, 3).reshape(FF, D),
            small[:, 5],
            small[:, 6],
            small[:, 7],
            mini[:, :PROJ],
        )
        shared = lax.psum_scatter(terms, "group", scatter_dimension=0, tiled=True)
        finals = lax.psum(shared, "psg")
    return (
        o["loss_o"][:, 0].reshape(MB, QDEV),
        o["eq_o"].reshape(MB, QDEV, QLEN, PROJ),
        o["ep_o"].reshape(MB, -1, PLEN, PROJ),
        o["gxq_o"].reshape(query_input.shape),
        o["gxp_o"].reshape(passage_input.shape),
    ) + tuple(part.astype(F32) for part in finals)


def solution(mesh):
    in_specs = (
        P(None, ("group", "psg"), None, None),
        P(None, ("group", "psg"), None, None),
        P(None, ("group", "psg")),
        P(None, "group"),
        P(),
        P(),
        P(),
        P(),
        P(),
        P(),
        P(),
        P(),
        P(),
        P(),
        P(),
        P(),
        P(),
        P(),
    )
    out_specs = (
        P(None, ("group", "psg")),
        P(None, ("group", "psg"), None, None),
        P(None, ("group", "psg"), None, None),
        P(None, ("group", "psg"), None, None),
        P(None, ("group", "psg"), None, None),
        P("group", None),
        P("group"),
        P("group"),
        P("group", None),
        P("group"),
        P("group"),
        P("group"),
        P("group", None),
        P("group"),
        P("group", None),
        P("group"),
        P("group"),
        P("group"),
        P("group", None),
    )
    return jax.shard_map(body, mesh=mesh, in_specs=in_specs, out_specs=out_specs, check_vma=False)
```

```python
import functools

import jax
import jax.numpy as jnp
from jax import lax
from jax.experimental import pallas as pl
from jax.experimental.pallas import tpu as pltpu
from jax.sharding import PartitionSpec as P

D = 768
HD = 64
FF = 3072
PROJ = 128
QLEN = 32
PLEN = 256
MB = 2
QDEV = 2
PSG = 4

PR = MB * PLEN
QR = MB * QDEV * QLEN
ROWS = PR + QR
PAIRS = D // 128
NC = 12
CW = 768
MW = 256
SHARDS = 8
SR = D // SHARDS
HALF = SR // 2
CORE_SLOTS = 4
SLOTS = 6

temper = 0.1
epsilon = 1e-06
masked = -1e30

MESH = pl.DeviceIdType.MESH
BF = jnp.bfloat16
F32 = jnp.float32


def dot(a, b):
    return jnp.dot(a, b, preferred_element_type=F32)


def dot_nt(a, b):
    return lax.dot_general(a, b, (((1,), (1,)), ((), ())), preferred_element_type=F32)


def dot_tn(a, b):
    return lax.dot_general(a, b, (((0,), (0,)), ((), ())), preferred_element_type=F32)


def at(i, size):
    return pl.ds(pl.multiple_of(i * size, size), size)


def loop(n, body):
    def step(i, carry):
        body(i)
        return carry

    lax.fori_loop(0, n, step, 0)


def fold(v):
    return jnp.sum(v.reshape(v.shape[0] // 8, 8, v.shape[1]), 0)


def remote(src, dst, ss, rs, dev):
    return pltpu.make_async_remote_copy(
        src_ref=src, dst_ref=dst, send_sem=ss, recv_sem=rs, device_id=dev, device_id_type=MESH
    )


V_BO, V_G1, V_S1, V_BB, V_G2, V_S2, V_BI = 3, 4, 5, 6, 7, 8, 9


def forward(r):
    x, qkv = r["x"], r["qkv"]
    vec = r["vec"]
    lane = lax.broadcasted_iota(jnp.int32, (1, 128), 1)
    masks = [(lane < HD).astype(BF), (lane >= HD).astype(BF)]

    def qkv_tile(j):
        b, n = j // 3, j % 3
        acc = dot(x[...], r["wq"][:, at(j, 256)])
        qkv[b, :, at(n, 256)] = (acc + vec[pl.ds(b, 1), at(n, 256)]).astype(BF)

    r["wait"](0, 1, 2)
    loop(9, qkv_tile)

    key_at = lax.broadcasted_iota(jnp.int32, (PLEN, PLEN), 1)
    q_row = lax.broadcasted_iota(jnp.int32, (QR, QR), 0) // QLEN
    q_col = lax.broadcasted_iota(jnp.int32, (QR, QR), 1) // QLEN

    def attend(rows, valid, hp, put):
        cols = at(hp, 128)
        q, k, v = qkv[0, rows, cols], qkv[1, rows, cols], qkv[2, rows, cols]
        total = 0.0
        for h in range(2):
            s = dot_nt(q * (masks[h] * 0.125), k)
            s = jnp.where(valid, s, masked)
            e = jnp.exp(s - jnp.max(s, -1, keepdims=True))
            pr = (e * (1.0 / jnp.sum(e, -1, keepdims=True))).astype(BF)
            put(2 * hp + h, pr)
            total = total + dot(pr, v * masks[h])
        r["att"][rows, cols] = total.astype(BF)

    def pair(hp):
        for m in range(MB):

            def put(h, pr, m=m):
                r["pp"][12 * m + h] = pr

            attend(pl.ds(PLEN * m, PLEN), key_at < r["len"][m], hp, put)

        def put_q(h, pr):
            r["pq"][h] = pr

        attend(pl.ds(PR, QR), q_row == q_col, hp, put_q)

    loop(PAIRS, pair)

    def resid_one(n):
        cols = at(n, 256)
        acc = dot(r["att"][...], r["wo"][:, cols])
        r["n1"][:, cols] = x[:, cols].astype(F32) + acc + vec[V_BO : V_BO + 1, cols]

    r["wait"](3)
    loop(3, resid_one)

    def norm(h):
        c = h - jnp.mean(h, -1, keepdims=True)
        inv = lax.rsqrt(jnp.mean(c * c, -1, keepdims=True) + epsilon)
        return c * inv, inv

    def norm_one(i):
        rows = at(i, 64)
        n, inv = norm(r["n1"][rows, :])
        r["n1"][rows, :] = n
        r["i1"][rows, :] = inv
        r["nl"][rows, :] = (n * vec[V_G1 : V_G1 + 1, :] + vec[V_S1 : V_S1 + 1, :]).astype(BF)

    loop(ROWS // 64, norm_one)

    def ffn(j):
        b, n = j // 3, j % 3
        cols = at(n, 256)
        pre = dot(r["nl"][...], r["wi"][:, at(j, 256)]) + vec[pl.ds(V_BI + b, 1), cols]
        cdf = 0.5 * (1.0 + lax.erf(pre * 0.7071067811865476))
        r["slope"][b, :, cols] = (
            cdf + pre * jnp.exp(-0.5 * pre * pre) * 0.3989422804014327
        ).astype(BF)
        post = (pre * cdf).astype(BF)
        r["grad"][4 + b, 0:3, :, :, cols] = post[: 6 * SR].reshape(3, 2, SR, 256)
        r["grad"][4 + b, 3, 0, 0 : ROWS - 6 * SR, cols] = post[6 * SR :]

    r["wait"](4)
    loop(FF // 256, ffn)

    def resid_two(n):
        cols = at(n, 256)
        acc = r["n1"][:, cols] * vec[V_G1 : V_G1 + 1, cols] + vec[V_S1 : V_S1 + 1, cols]
        acc = acc + vec[V_BB : V_BB + 1, cols]
        for b in range(4):
            acc = acc + dot(post_block(r, b, pl.ds(0, CW)), r["wb"][b, :, cols])
        r["n2"][:, cols] = acc

    r["wait"](5)
    loop(3, resid_two)

    def norm_two(i):
        rows = at(i, 64)
        n, inv = norm(r["n2"][rows, :])
        r["n2"][rows, :] = n
        r["i2"][rows, :] = inv
        r["s2"][rows, :] = (n * vec[V_G2 : V_G2 + 1, :] + vec[V_S2 : V_S2 + 1, :]).astype(BF)

    loop(ROWS // 64, norm_two)
    r["wait"](6)
    proj = dot(r["s2"][...], r["wp"][...])
    il = lax.rsqrt(jnp.sum(proj * proj, -1, keepdims=True) + epsilon)
    unit = proj * il
    r["il"][...] = il
    r["unit"][...] = unit
    r["emb"][...] = unit.astype(BF)


def post_block(r, b, cols):
    top = r["grad"][4 + b, 0:3, :, :, cols].reshape(6 * SR, cols.size)
    return jnp.concatenate([top, r["grad"][4 + b, 3, 0, 0 : ROWS - 6 * SR, cols]], 0)


def maxsim(r, g, p):
    emb = r["emb"]

    def peers(src, buf, ss, rs):
        copies = []
        for o in range(1, PSG):
            to = (p + o) % PSG
            copies.append(remote(src(to), buf.at[p], ss.at[o - 1], rs.at[o - 1], (g, to)))
        return copies

    queries = peers(lambda to: emb.at[pl.ds(PR, QR), :], r["gq"], r["q_s"], r["q_r"])
    for cp in queries:
        cp.start()
    r["gq"][p] = emb[PR:ROWS, :]

    def turn(i):
        b, half = i // 2, i % 2
        t = post_block(r, b, at(half, 384)).T
        for q in range(4):
            r["grad"][8 + q, b, half, :, 0:ROWS] = t[SR * q : SR * (q + 1)]

    loop(SHARDS, turn)
    for cp in queries:
        cp.wait_recv()

    key_at = lax.broadcasted_iota(jnp.int32, (PSG * QDEV * QLEN, PLEN), 1)
    nq = PSG * QDEV
    half = QDEV * QLEN
    sums = []
    for m in range(MB):
        gq = jnp.concatenate([r["gq"][d, half * m : half * (m + 1), :] for d in range(PSG)], 0)
        s = dot_nt(gq, emb[PLEN * m : PLEN * (m + 1), :])
        e = jnp.where(key_at < r["len"][m], jnp.exp(s * (1.0 / temper)), 0.0)
        total = jnp.sum(e, -1, keepdims=True)
        r["sim"][m] = e
        sums.append(total)
        log = jnp.broadcast_to(jnp.log(total), (nq * QLEN, 128))
        r["sc"][p, nq * m : nq * (m + 1), :] = temper * jnp.sum(log.reshape(nq, QLEN, 128), 1)
    scores = peers(lambda to: r["sc"].at[p], r["sc"], r["s_s"], r["s_r"])
    for cp in scores:
        cp.start()
    for cp in scores:
        cp.wait()
    every = [r["sc"][d] for d in range(PSG)]
    top = functools.reduce(jnp.maximum, every)
    log_total = top + jnp.log(sum(jnp.exp(v - top) for v in every))
    row = lax.broadcasted_iota(jnp.int32, (MB * nq, 128), 0)
    pos = jnp.zeros((MB * nq, 128), jnp.int32)
    for m in range(MB):
        for q in range(nq):
            pos = jnp.where(row == nq * m + q, r["pos"][m, q], pos)
    picked = sum(jnp.where(pos == d, every[d], 0.0) for d in range(PSG))
    r["lo"][...] = log_total - picked
    grad_score = jnp.exp(r["sc"][p] - log_total) - (pos == p).astype(F32)
    for m in range(MB):
        gs = grad_score[nq * m : nq * (m + 1)]
        gs = jnp.broadcast_to(gs[:, None, :], (nq, QLEN, 128)).reshape(nq * QLEN, 128)
        coef = gs * (1.0 / sums[m])
        coef = jnp.concatenate([coef, coef], 1)
        ds = (coef * r["sim"][m]).astype(BF)
        pe = emb[PLEN * m : PLEN * (m + 1), :]
        gg = dot(ds, pe).astype(BF)
        for d in range(PSG):
            r["gg"][d, half * m : half * (m + 1), :] = gg[half * d : half * (d + 1)]
        gq = jnp.concatenate([r["gq"][d, half * m : half * (m + 1), :] for d in range(PSG)], 0)
        r["de"][PLEN * m : PLEN * (m + 1), :] = dot_tn(ds, gq).astype(BF)
    backs = peers(lambda to: r["gg"].at[to], r["gr"], r["g_s"], r["g_r"])
    for cp in backs:
        cp.start()
    r["gr"][p] = r["gg"][p]
    for cp in backs:
        cp.wait()
    for cp in queries:
        cp.wait_send()
    r["de"][PR:ROWS, :] = sum(r["gr"][d].astype(F32) for d in range(PSG)).astype(BF)


def norm_back(grad_out, n, inv, gain):
    gn = grad_out * gain
    return inv * (
        gn - jnp.mean(gn, -1, keepdims=True) - n * jnp.mean(gn * n, -1, keepdims=True)
    )


def head_back(r):
    vec = r["vec"]
    gu = r["de"][...].astype(F32)
    unit = r["unit"][...]
    r["gp"][...] = (r["il"][...] * (gu - unit * jnp.sum(gu * unit, -1, keepdims=True))).astype(BF)

    def body(i, sums):
        rows = at(i, 64)
        g2 = dot_nt(r["gp"][rows, :], r["wp"][...])
        n = r["n2"][rows, :]
        gr = norm_back(g2, n, r["i2"][rows, :], vec[V_G2 : V_G2 + 1, :])
        low = gr.astype(BF)
        r["n2"][rows, :] = gr
        r["gb"][rows, :] = low
        add = (fold(low.astype(F32)), fold(g2 * n), fold(g2))
        return tuple(a + b for a, b in zip(sums, add))

    zero = jnp.zeros((8, D), F32)
    sums = lax.fori_loop(0, ROWS // 64, body, (zero, zero, zero))
    for row, v in zip((5, 6, 7), sums):
        r["sm"][row : row + 1, :] = jnp.sum(v, 0, keepdims=True)


def backward_step(r, t):
    vec, qkv, grad = r["vec"], r["qkv"], r["grad"]
    lane = lax.broadcasted_iota(jnp.int32, (1, 128), 1)
    masks = [(lane < HD).astype(BF), (lane >= HD).astype(BF)]

    def outer(left, right, k, n):
        grad[k, :, :, :, at(n, 256)] = dot(left, right).astype(BF).reshape(4, 2, SR, 256)

    def turn(src, n):
        r["lt"][at(n, 256), :] = src[:, at(n, 256)].T

    @pl.when(t < 4)
    def _():
        def tile(n):
            left = grad[8 + t, :, :, :, 0:ROWS].reshape(CW, ROWS)
            outer(left, r["gb"][:, at(n, 256)], t, n)

        loop(3, tile)

    @pl.when(t == 4)
    def _():
        loop(3, lambda n: turn(r["nl"], n))

    @pl.when((t >= 4) & (t < 8))
    def _():
        b = t - 4

        def tile(n):
            cols = at(n, 256)
            v = dot_nt(r["gb"][...], r["wb"][b, cols, :]) * r["slope"][b, :, cols].astype(F32)
            low = v.astype(BF)
            r["slope"][b, :, cols] = low
            r["sm"][pl.ds(8 + b, 1), cols] = jnp.sum(low.astype(F32), 0, keepdims=True)
            outer(r["lt"][...], low, 4 + b, n)

        loop(3, tile)

    @pl.when(t == 8)
    def _():
        loop(3, lambda n: turn(r["s2"], n))
        v = dot(r["lt"][...], r["gp"][...]).astype(BF)
        r["gmini"][:, :, :, 0:PROJ] = v.reshape(4, 2, SR, PROJ)

    @pl.when((t >= 8) & (t < 11))
    def _():
        n = t - 8
        cols = at(n, 256)
        acc = r["n2"][:, cols]
        for b in range(4):
            acc = acc + dot_nt(r["slope"][b], r["wi"][cols, CW * b : CW * (b + 1)])
        r["n2"][:, cols] = acc

    @pl.when(t == 11)
    def _():
        def body(i, sums):
            rows = at(i, 64)
            g1, n = r["n2"][rows, :], r["n1"][rows, :]
            gr = norm_back(g1, n, r["i1"][rows, :], vec[V_G1 : V_G1 + 1, :])
            low = gr.astype(BF)
            r["n1"][rows, :] = gr
            r["gb"][rows, :] = low
            add = (fold(low.astype(F32)), fold(g1 * n), fold(g1))
            return tuple(a + b for a, b in zip(sums, add))

        zero = jnp.zeros((8, D), F32)
        sums = lax.fori_loop(0, ROWS // 64, body, (zero, zero, zero))
        for row, v in zip((2, 3, 4), sums):
            r["sm"][row : row + 1, :] = jnp.sum(v, 0, keepdims=True)
        loop(3, lambda n: turn(r["att"], n))
        loop(3, lambda n: outer(r["lt"][...], r["gb"][:, at(n, 256)], 8, n))

    @pl.when(t == 12)
    def _():
        def tile(n):
            r["att"][:, at(n, 256)] = dot_nt(r["gb"][...], r["wo"][at(n, 256), :]).astype(BF)

        loop(3, tile)
        loop(3, lambda n: turn(r["x"], n))

    def attend_back(rows, hp, take):
        cols = at(hp, 128)
        q, k, v = qkv[0, rows, cols], qkv[1, rows, cols], qkv[2, rows, cols]
        a = r["att"][rows, cols]
        dq = dk = dv = 0.0
        for h in range(2):
            pr = take(2 * hp + h)
            ah = a * masks[h]
            dp = dot_nt(ah, v)
            pf = pr.astype(F32)
            ds = (pf * (dp - jnp.sum(pf * dp, -1, keepdims=True))).astype(BF)
            dq = dq + dot(ds, k * masks[h])
            dk = dk + dot_tn(ds, q * masks[h])
            dv = dv + dot_tn(pr, ah)
        dq = (dq * 0.125).astype(BF)
        dv = dv.astype(BF)
        qkv[0, rows, cols] = dq
        qkv[1, rows, cols] = (dk * 0.125).astype(BF)
        qkv[2, rows, cols] = dv
        return (
            jnp.sum(dq.astype(F32), 0, keepdims=True),
            jnp.sum(dv.astype(F32), 0, keepdims=True),
        )

    @pl.when((t >= 13) & (t < 13 + PAIRS))
    def _():
        hp = t - 13
        cols = at(hp, 128)
        bq, bv = attend_back(pl.ds(PR, QR), hp, lambda h: r["pq"][h])
        for m in range(MB):
            one, two = attend_back(
                pl.ds(PLEN * m, PLEN), hp, lambda h, m=m: r["pp"][12 * m + h]
            )
            bq, bv = bq + one, bv + two
        r["sm"][0:1, cols] = bq
        r["sm"][1:2, cols] = bv

    @pl.when((t == 14) | (t == 16) | (t == 18))
    def _():
        i = (t - 14) // 2
        loop(3, lambda b: outer(r["lt"][...], qkv[b, :, at(i, 256)], 9 + i, b))

    @pl.when(t == 19)
    def _():
        small = r["sm"][...].T
        one = lax.broadcasted_iota(jnp.int32, (SR, 128), 1)
        pad = jnp.zeros((SR, 128 - small.shape[1]), F32)
        for s in range(SHARDS):
            v = jnp.concatenate([small[SR * s : SR * (s + 1)], pad], 1)
            b, base = s // 2, 384 * (s % 2)
            v = jnp.where(one < 8, v, 0.0)
            for q in range(4):
                col = small[base + SR * q : base + SR * (q + 1), 8 + b : 9 + b]
                v = jnp.where(one == 8 + q, col, v)
            r["gmini"][s // 2, s % 2, :, PROJ:MW] = v.astype(BF)

    @pl.when((t >= 20) & (t < 23))
    def _():
        n = t - 20
        cols = at(n, 256)
        acc = r["n1"][:, cols]
        for b in range(3):
            acc = acc + dot_nt(qkv[b], r["wq"][cols, CW * b : CW * (b + 1)])
        r["gb"][:, cols] = acc.astype(BF)


def slot_of(t):
    k = jnp.where(t < 8, t, -1)
    for step, which in ((11, 8), (14, 9), (16, 10), (18, 11)):
        k = jnp.where(t == step, which, k)
    return jnp.where(t >= LAST_ENTER, t - LAST_ENTER + NC, k)


LAST_ENTER = 19


class Reducer:
    def __init__(self, r, g, p):
        self.r = r
        self.p = p
        self.z, self.y = g // 2, g % 2
        self.x, self.c = p // 2, p % 2
        z, y, x, c = self.z, self.y, self.x, self.c
        self.sib = (g, p + 1 - 2 * c)
        self.ynb = (g + 1 - 2 * y, p)
        self.xnb = (g, (p + 2) % 4)
        self.line = [(2 * ((z + o) % 4) + y, p) for o in range(1, 4)]
        self.own = pl.ds(pl.multiple_of(c * HALF, 16), HALF)
        self.oth = pl.ds(pl.multiple_of((1 - c) * HALF, 16), HALF)

    def unit(self, k, core):
        r = self.r
        u = lambda: None
        u.k, u.core = k, core
        if isinstance(k, int) and k == NC:
            u.width = MW
            u.g = r["gmini"]
            u.cs, u.s = CORE_SLOTS, SLOTS
            for name in ("core_rv", "first_a", "first_b", "second_b", "line_rv", "cross_rv", "done"):
                setattr(u, name, r["m_" + name])
        else:
            u.width = CW
            u.g = r["grad"].at[k]
            u.cs, u.s = k % CORE_SLOTS, k % SLOTS
            u.core_rv = r["core_rv"].at[u.cs]
            for name in ("first_a", "first_b", "line_rv"):
                setattr(u, name, r[name].at[u.s])
            for name in ("second_b", "cross_rv", "done"):
                setattr(u, name, r[name].at[k])
        return u

    def add_into(self, dst, src):
        dst[...] = (dst[...].astype(F32) + src[...].astype(F32)).astype(BF)

    def half(self, u, xx):
        w = u.width // 2
        return pl.ds(pl.multiple_of(xx * w, 128), w)

    def core_copy(self, u):
        r = self.r
        return remote(
            u.g.at[:, :, self.oth, :], u.core_rv, r["c_s"].at[u.cs], r["c_r"].at[u.cs], self.sib
        )

    def core_end(self, u):
        self.core_copy(u).wait()
        loop(
            SHARDS,
            lambda i: self.add_into(
                u.g.at[i // 2, i % 2, self.own, :], u.core_rv.at[i // 2, i % 2]
            ),
        )

    def one_copy(self, u):
        r = self.r
        sems = r["one_s"].at[u.s], r["one_r"].at[u.s]
        if u.core == 0:
            return remote(u.g.at[:, 1 - self.y, self.own, :], u.first_a, *sems, self.ynb)
        away = self.half(u, 1 - self.x)
        return remote(u.g.at[:, :, self.own, away], u.first_b, *sems, self.xnb)

    def one_start(self, u):
        self.one_copy(u).start()

    def one_end(self, u):
        self.one_copy(u).wait()
        if u.core == 0:
            loop(
                4, lambda i: self.add_into(u.g.at[i, self.y, self.own, :], u.first_a.at[i])
            )
        else:
            mine = self.half(u, self.x)
            loop(
                SHARDS,
                lambda i: self.add_into(
                    u.g.at[i // 2, i % 2, self.own, mine], u.first_b.at[i // 2, i % 2]
                ),
            )

    def two_copy(self, u):
        r = self.r
        return remote(
            u.g.at[:, 1 - self.y, self.own, self.half(u, self.x)],
            u.second_b,
            r["two_s"].at[u.s],
            r["two_r"].at[u.s],
            self.ynb,
        )

    def two_start(self, u):
        self.two_copy(u).start()

    def two_end(self, u):
        self.two_copy(u).wait()
        mine = self.half(u, self.x)
        loop(
            4, lambda i: self.add_into(u.g.at[i, self.y, self.own, mine], u.second_b.at[i])
        )

    def part(self, u, d):
        cols = slice(None) if u.core == 0 else self.half(u, self.x)
        return u.g.at[d, self.y, self.own, cols]

    def landing(self, u, i):
        return u.line_rv.at[i, :, pl.ds(0, u.width // (1 + u.core))]

    def line_copy(self, u, o):
        r, d = self.r, (self.z + o) % 4
        return remote(
            self.part(u, d),
            self.landing(u, 3 - o),
            r["z_s"].at[3 * u.s + 3 - o],
            r["z_r"].at[3 * u.s + 3 - o],
            (2 * d + self.y, self.p),
        )

    def line_start(self, u):
        for o in (2, 1, 3):
            self.line_copy(u, o).start()

    def line_end(self, u):
        mine = self.part(u, self.z)
        for o in range(1, 4):
            self.line_copy(u, o).wait()
        total = mine[...].astype(F32)
        for i in range(3):
            total = total + self.landing(u, i)[...].astype(F32)
        mine[...] = total.astype(BF)

    def last_copy(self, u):
        r = self.r
        sems = r["last_s"].at[u.s], r["last_r"].at[u.s]
        to = u.cross_rv if u.core == 0 else u.done.at[:, self.half(u, self.x)]
        return remote(self.part(u, self.z), to, *sems, self.xnb)

    def last_start(self, u):
        self.last_copy(u).start()

    def last_end(self, u):
        self.last_copy(u).wait()
        mine = self.part(u, self.z)[...]
        if u.core == 0:
            u.done[...] = (mine.astype(F32) + u.cross_rv[...].astype(F32)).astype(BF)
        else:
            u.done[:, self.half(u, self.x)] = mine

    def to_outputs(self, u, do):
        r, k, own = self.r, u.k, self.own

        def both(dst):
            do(pltpu.make_async_copy(u.done, dst, r["st_sem"].at[k]))
            do(remote(u.done, dst, r["fin_s"].at[k], r["fin_r"].at[k], self.sib))

        if isinstance(k, int) and k == NC:
            both(r["mini_o"].at[own, :])
            return

        @pl.when(k < 4)
        def _():
            both(r["back_o"].at[pl.ds(pl.multiple_of(SR * k + HALF * self.c, 16), HALF), :])

        @pl.when((k >= 4) & (k < 8))
        def _():
            both(r["in_o"].at[own, at(k - 4, CW)])

        @pl.when(k == 8)
        def _():
            both(r["out_o"].at[own, :])

        @pl.when(k > 8)
        def _():
            both(r["qkv_o"].at[own, at(k - 9, CW)])

    def stages(self, core):
        out = lambda u: self.to_outputs(u, lambda cp: cp.start())
        core_start = lambda u: self.core_copy(u).start()
        if core == 0:
            return {
                0: [core_start],
                1: [self.core_end, self.one_start],
                3: [self.one_end, self.line_start],
                5: [self.line_end, self.last_start],
                7: [self.last_end, out],
            }
        return {
            0: [core_start],
            1: [self.core_end, self.one_start],
            3: [self.one_end, self.two_start],
            5: [self.two_end, self.line_start],
            7: [self.line_end, self.last_start],
            9: [self.last_end, out],
        }

    def slot(self, t):
        for core in range(2):

            @pl.when(self.c == core)
            def _():
                stages = self.stages(core)
                for s in sorted(stages, reverse=True):
                    k = t - s

                    @pl.when((k >= 0) & (k < NC))
                    def _():
                        for do in stages[s]:
                            do(self.unit(k, core))

                    @pl.when(k == NC)
                    def _():
                        for do in stages[s]:
                            do(self.unit(NC, core))

    def finish(self, k):
        self.to_outputs(self.unit(k, 0), lambda cp: cp.wait())


INPUTS = ("len", "pos", "vec", "xp_h", "xq_h", "wq_h", "wo_h", "wi_h", "wb_h", "wp_h")


def kernel(spread, names, *refs):
    r = dict(zip(names, refs))
    g = lax.axis_index("group")
    p = lax.axis_index("psg")
    barrier = pltpu.get_barrier_semaphore()

    def greet(dev):
        pl.semaphore_signal(barrier, inc=1, device_id=dev, device_id_type=MESH)

    for o in range(1, PSG):
        greet((g, (p + o) % PSG))
    count = PSG - 1
    if spread:
        red = Reducer(r, g, p)
        for dev in [red.ynb] + red.line:
            greet(dev)
        count = count + 4

    pairs = [
        (r["xp_h"], r["x"].at[pl.ds(0, PR), :]),
        (r["xq_h"], r["x"].at[pl.ds(PR, QR), :]),
        (r["wq_h"], r["wq"]),
        (r["wo_h"], r["wo"]),
        (r["wi_h"], r["wi"]),
        (r["wb_h"], r["wb"]),
        (r["wp_h"], r["wp"]),
    ]
    loads = [pltpu.make_async_copy(a, b, r["in_sem"].at[i]) for i, (a, b) in enumerate(pairs)]
    for cp in loads:
        cp.start()
    r["wait"] = lambda *which: [loads[i].wait() for i in which]
    forward(r)
    pl.semaphore_wait(barrier, count)
    maxsim(r, g, p)
    lane = lax.broadcasted_iota(jnp.int32, (1, 128), 1)
    for m in range(MB):
        v = jnp.zeros((1, 128), F32)
        for q in range(QDEV):
            v = jnp.where(lane == q, r["lo"][pl.ds(PSG * QDEV * m + QDEV * p + q, 1), :], v)
        r["loss_o"][m : m + 1, :] = v
    head_back(r)

    def step(t):
        backward_step(r, t)
        if spread:
            now = slot_of(t)

            @pl.when(now >= 0)
            def _():
                red.slot(now)


    loop(LAST_ENTER + 10 if spread else 23, step)

    outs = [
        (r["emb"].at[pl.ds(0, PR), :], r["ep_o"]),
        (r["emb"].at[pl.ds(PR, QR), :], r["eq_o"]),
        (r["gb"].at[pl.ds(0, PR), :], r["gxp_o"]),
        (r["gb"].at[pl.ds(PR, QR), :], r["gxq_o"]),
    ]
    if not spread:
        outs += [(r["grad"], r["grad_o"]), (r["gmini"], r["mini_o"])]
    stores = [pltpu.make_async_copy(a, b, r["out_sem"].at[i]) for i, (a, b) in enumerate(outs)]
    for cp in stores:
        cp.start()
    for cp in stores:
        cp.wait()
    if spread:
        loop(NC, red.finish)
        red.finish(NC)


def run_step(spread, inputs):
    sds = jax.ShapeDtypeStruct
    outs = {
        "loss_o": sds((MB, 128), F32),
        "eq_o": sds((QR, PROJ), BF),
        "ep_o": sds((PR, PROJ), BF),
        "gxq_o": sds((QR, D), BF),
        "gxp_o": sds((PR, D), BF),
    }
    if spread:
        outs |= {
            "back_o": sds((4 * SR, D), BF),
            "in_o": sds((SR, FF), BF),
            "out_o": sds((SR, D), BF),
            "qkv_o": sds((SR, 3 * D), BF),
            "mini_o": sds((SR, MW), BF),
        }
    else:
        outs |= {
            "grad_o": sds((NC, 4, 2, SR, CW), BF),
            "mini_o": sds((4, 2, SR, MW), BF),
        }
    vm = pltpu.VMEM
    dma = pltpu.SemaphoreType.DMA
    scratch = {
        "x": vm((ROWS, D), BF),
        "wq": vm((D, 3 * D), BF),
        "wo": vm((D, D), BF),
        "wi": vm((D, FF), BF),
        "wb": vm((4, CW, D), BF),
        "wp": vm((D, PROJ), BF),
        "qkv": vm((3, ROWS, D), BF),
        "pp": vm((MB * 12, PLEN, PLEN), BF),
        "pq": vm((12, QR, QR), BF),
        "att": vm((ROWS, D), BF),
        "n1": vm((ROWS, D), F32),
        "n2": vm((ROWS, D), F32),
        "i1": vm((ROWS, 1), F32),
        "i2": vm((ROWS, 1), F32),
        "il": vm((ROWS, 1), F32),
        "nl": vm((ROWS, D), BF),
        "slope": vm((4, ROWS, CW), BF),
        "s2": vm((ROWS, D), BF),
        "unit": vm((ROWS, PROJ), F32),
        "emb": vm((ROWS, PROJ), BF),
        "de": vm((ROWS, PROJ), BF),
        "gp": vm((ROWS, PROJ), BF),
        "gb": vm((ROWS, D), BF),
        "lt": vm((D, ROWS), BF),
        "sm": vm((16, D), F32),
        "gq": vm((PSG, QR, PROJ), BF),
        "sim": vm((MB, PSG * QDEV * QLEN, PLEN), F32),
        "sc": vm((PSG, MB * PSG * QDEV, 128), F32),
        "lo": vm((MB * PSG * QDEV, 128), F32),
        "gg": vm((PSG, QR, PROJ), BF),
        "gr": vm((PSG, QR, PROJ), BF),
        "grad": vm((NC, 4, 2, SR, CW), BF),
        "gmini": vm((4, 2, SR, MW), BF),
        "in_sem": dma((7,)),
        "out_sem": dma((6,)),
    }
    for name in ("q_s", "q_r", "s_s", "s_r", "g_s", "g_r"):
        scratch[name] = dma((PSG - 1,))
    if spread:
        for lead, slots, w, pre in ((True, (CORE_SLOTS, SLOTS, NC), CW, ""), (False, None, MW, "m_")):
            a, b, c = ((slots[0],), (slots[1],), (slots[2],)) if lead else ((), (), ())
            scratch[pre + "core_rv"] = vm(a + (4, 2, HALF, w), BF)
            scratch[pre + "first_a"] = vm(b + (4, HALF, w), BF)
            scratch[pre + "first_b"] = vm(b + (4, 2, HALF, w // 2), BF)
            scratch[pre + "second_b"] = vm(c + (4, HALF, w // 2), BF)
            scratch[pre + "line_rv"] = vm(b + (3, HALF, w), BF)
            scratch[pre + "cross_rv"] = vm(c + (HALF, w), BF)
            scratch[pre + "done"] = vm(c + (HALF, w), BF)
        for name in ("c_s", "c_r"):
            scratch[name] = dma((CORE_SLOTS + 1,))
        for name in ("one_s", "one_r", "two_s", "two_r", "last_s", "last_r"):
            scratch[name] = dma((SLOTS + 1,))
        for name in ("z_s", "z_r"):
            scratch[name] = dma((3 * (SLOTS + 1),))
        for name in ("st_sem", "fin_s", "fin_r"):
            scratch[name] = dma((NC + 1,))
    hbm = pl.BlockSpec(memory_space=pl.ANY)
    vmem = pl.BlockSpec(memory_space=pltpu.VMEM)
    smem = pl.BlockSpec(memory_space=pltpu.SMEM)
    names = INPUTS + tuple(outs) + tuple(scratch)
    res = pl.pallas_call(
        functools.partial(kernel, spread, names),
        out_shape=list(outs.values()),
        in_specs=[smem, smem, vmem] + [hbm] * 7,
        out_specs=[vmem] + [hbm] * (len(outs) - 1),
        scratch_shapes=list(scratch.values()),
        compiler_params=pltpu.CompilerParams(
            collective_id=0, has_side_effects=True, vmem_limit_bytes=64 << 20
        ),
        name="train_step",
    )(*inputs)
    return dict(zip(outs, res))


WIDE = ("eq_o", "ep_o", "gxq_o", "gxp_o")
GRADS = ("qkv_o", "out_o", "in_o", "back_o")


def finish_kernel(*refs):
    names = ("loss", "mini") + GRADS + WIDE
    n = len(names)
    i = dict(zip(names, refs[:n]))
    o = dict(zip(("loss",) + WIDE + GRADS + ("proj", "small"), refs[n:]))
    o["loss"][...] = i["loss"][:, 0:QDEV]

    def move(v):
        def cast(j):
            o[v][at(j, 32), :] = i[v][at(j, 32), :].astype(o[v].dtype)

        loop(i[v].shape[0] // 32, cast)

    for v in GRADS[1:] + WIDE:
        move(v)
    for b in range(3):
        for n in range(3):
            to = slice(CW * b + 256 * n, CW * b + 256 * (n + 1))
            of = slice(CW * n + 256 * b, CW * n + 256 * (b + 1))
            o["qkv_o"][:, to] = i["qkv_o"][:, of].astype(F32)
    o["proj"][...] = i["mini"][:, 0:PROJ].astype(F32)
    o["small"][...] = i["mini"][:, PROJ:MW].astype(F32).T[0:16, 0:SR]


def finish_step(o):
    sds = jax.ShapeDtypeStruct
    like = lambda v, t: sds(o[v].shape, t)
    outs = [sds((MB, QDEV), F32)]
    outs += [like(v, BF) for v in WIDE] + [like(v, F32) for v in GRADS]
    outs += [sds((SR, PROJ), F32), sds((16, SR), F32)]
    vmem = pl.BlockSpec(memory_space=pltpu.VMEM)
    res = pl.pallas_call(
        finish_kernel,
        out_shape=outs,
        in_specs=[vmem] * 10,
        out_specs=[vmem] * 11,
        name="finish",
    )(o["loss_o"], o["mini_o"], *[o[v] for v in GRADS], *[o[v] for v in WIDE])
    moved = dict(zip(("loss_o",) + WIDE, res[:5]))
    qkv, w_out, w_in, back, proj, v = res[5:]
    return moved, (
        qkv, v[0], v[1], w_out, v[2], v[3], v[4], w_in, v[8:12].reshape(4 * SR),
        back, v[5], v[6], v[7], proj,
    )


def body(
    query_input,
    passage_input,
    lengths,
    positive,
    w_qkv,
    bias_q,
    bias_v,
    w_out,
    bias_out,
    norm1_gain,
    norm1_bias,
    w_in,
    bias_in,
    w_back,
    bias_back,
    norm2_gain,
    norm2_bias,
    w_proj,
):
    spread = lax.axis_size("group") == SHARDS
    vec, row = 0.0, 0
    for v in (
        bias_q, None, bias_v, bias_out, norm1_gain, norm1_bias, bias_back, norm2_gain, norm2_bias, bias_in,
    ):
        if v is None:
            row += D
            continue
        vec = vec + jnp.pad(v.astype(F32), (row, 13 * D - row - v.shape[0]))
        row += v.shape[0]
    vec = vec.reshape(13, D)
    inputs = (
        lengths.reshape(MB),
        positive,
        vec,
        passage_input.reshape(PR, D),
        query_input.reshape(QR, D),
        w_qkv,
        w_out,
        w_in,
        w_back.reshape(4, CW, D),
        w_proj,
    )
    o = run_step(spread, inputs)
    if spread:
        o, finals = finish_step(o)
    else:
        full = o["grad_o"].reshape(NC, SHARDS, SR, CW)
        mini = o["mini_o"].reshape(D, MW)
        small = mini[:, PROJ : PROJ + 8]
        wide = o["mini_o"].reshape(SHARDS, SR, MW)[:, :, PROJ + 8 : PROJ + 12].transpose(0, 2, 1).reshape(FF)
        halves = full[9:12].reshape(3, D, 3, 256).transpose(1, 2, 0, 3).reshape(D, 3 * D)
        terms = (
            halves,
            small[:, 0],
            small[:, 1],
            full[8].reshape(D, D),
            small[:, 2],
            small[:, 3],
            small[:, 4],
            full[4:8].reshape(4, D, CW).transpose(1, 0, 2).reshape(D, FF),
            wide,
            full[0:4].transpose(1, 0, 2, 3).reshape(FF, D),
            small[:, 5],
            small[:, 6],
            small[:, 7],
            mini[:, :PROJ],
        )
        shared = lax.psum_scatter(terms, "group", scatter_dimension=0, tiled=True)
        finals = lax.psum(shared, "psg")
    return (
        o["loss_o"][:, :QDEV],
        o["eq_o"].reshape(MB, QDEV, QLEN, PROJ),
        o["ep_o"].reshape(MB, -1, PLEN, PROJ),
        o["gxq_o"].reshape(query_input.shape),
        o["gxp_o"].reshape(passage_input.shape),
    ) + tuple(part.astype(F32) for part in finals)


def solution(mesh):
    in_specs = (
        P(None, ("group", "psg"), None, None),
        P(None, ("group", "psg"), None, None),
        P(None, ("group", "psg")),
        P(None, "group"),
        P(),
        P(),
        P(),
        P(),
        P(),
        P(),
        P(),
        P(),
        P(),
        P(),
        P(),
        P(),
        P(),
        P(),
    )
    out_specs = (
        P(None, ("group", "psg")),
        P(None, ("group", "psg"), None, None),
        P(None, ("group", "psg"), None, None),
        P(None, ("group", "psg"), None, None),
        P(None, ("group", "psg"), None, None),
        P("group", None),
        P("group"),
        P("group"),
        P("group", None),
        P("group"),
        P("group"),
        P("group"),
        P("group", None),
        P("group"),
        P("group", None),
        P("group"),
        P("group"),
        P("group"),
        P("group", None),
    )
    return jax.shard_map(body, mesh=mesh, in_specs=in_specs, out_specs=out_specs, check_vma=False)
```

```python
import functools

import jax
import jax.numpy as jnp
from jax import lax
from jax.experimental import pallas as pl
from jax.experimental.pallas import tpu as pltpu
from jax.sharding import PartitionSpec as P

D = 768
HD = 64
FF = 3072
PROJ = 128
QLEN = 32
PLEN = 256
MB = 2
QDEV = 2
PSG = 4

PR = MB * PLEN
QR = MB * QDEV * QLEN
ROWS = PR + QR
PAIRS = D // 128
NC = 12
CW = 768
MW = 256
SHARDS = 8
SR = D // SHARDS
HALF = SR // 2
CORE_SLOTS = 2
SLOTS = 6
LINE_SLOTS = 6

temper = 0.1
epsilon = 1e-06
masked = -1e30

MESH = pl.DeviceIdType.MESH
BF = jnp.bfloat16
F32 = jnp.float32


def dot(a, b):
    return jnp.dot(a, b, preferred_element_type=F32)


def dot_nt(a, b):
    return lax.dot_general(a, b, (((1,), (1,)), ((), ())), preferred_element_type=F32)


def dot_tn(a, b):
    return lax.dot_general(a, b, (((0,), (0,)), ((), ())), preferred_element_type=F32)


def at(i, size):
    return pl.ds(i * size if isinstance(i, int) else pl.multiple_of(i * size, size), size)


def loop(n, body, unroll=1):
    def step(i, carry):
        body(i)
        return carry

    lax.fori_loop(0, n, step, 0, unroll=unroll)


def fold(v):
    return jnp.sum(v.reshape(v.shape[0] // 8, 8, v.shape[1]), 0)


def remote(src, dst, ss, rs, dev):
    return pltpu.make_async_remote_copy(
        src_ref=src, dst_ref=dst, send_sem=ss, recv_sem=rs, device_id=dev, device_id_type=MESH
    )


V_BO, V_G1, V_S1, V_BB, V_G2, V_S2, V_BI = 3, 4, 5, 6, 7, 8, 9


def forward(r, send_queries):
    x, qkv = r["x"], r["qkv"]
    vec = r["vec"]
    lane = lax.broadcasted_iota(jnp.int32, (1, 128), 1)
    masks = [(lane < HD).astype(BF), (lane >= HD).astype(BF)]

    def qkv_tile(j):
        b, n = j // 3, j % 3
        acc = dot(x[...], r["wq"][:, at(j, 256)])
        qkv[b, :, at(n, 256)] = (acc + vec[pl.ds(b, 1), at(n, 256)]).astype(BF)

    r["wait"](0, 1, 2)
    loop(9, qkv_tile, 3)

    key_at = lax.broadcasted_iota(jnp.int32, (PLEN, PLEN), 0)
    q_row = lax.broadcasted_iota(jnp.int32, (QR, QR), 0) // QLEN
    q_col = lax.broadcasted_iota(jnp.int32, (QR, QR), 1) // QLEN

    def pair(hp):
        cols = at(hp, 128)
        segs = [(pl.ds(PLEN * m, PLEN), key_at < r["len"][m]) for m in range(MB)]
        segs.append((pl.ds(PR, QR), q_row == q_col))
        scores = []
        for rows, valid in segs:
            q, k = qkv[0, rows, cols], qkv[1, rows, cols]
            for h in range(2):
                scores.append(jnp.where(valid, dot_nt(k, q * (masks[h] * 0.125)), masked))
        probs = []
        for i, sc in enumerate(scores):
            e = jnp.exp(sc - jnp.max(sc, 0, keepdims=True))
            pr = (e * (1.0 / jnp.sum(e, 0, keepdims=True))).astype(BF)
            m, h = i // 2, i % 2
            if m < MB:
                r["pp"][12 * m + 2 * hp + h] = pr
            else:
                r["pq"][2 * hp + h] = pr
            probs.append(pr)
        for m, (rows, _) in enumerate(segs):
            vt = qkv[2, rows, cols].T
            parts = [
                dot(vt[HD * h : HD * (h + 1)], probs[2 * m + h]).astype(BF) for h in range(2)
            ]
            r["att"][rows, cols] = jnp.concatenate(parts, 0).T

    loop(PAIRS, pair)

    def resid_one(n):
        cols = at(n, 256)
        acc = dot(r["att"][...], r["wo"][:, cols])
        r["n2"][:, cols] = x[:, cols].astype(F32) + acc + vec[V_BO : V_BO + 1, cols]

    r["wait"](3)
    loop(3, resid_one, 3)

    def norm(h):
        c = h - jnp.mean(h, -1, keepdims=True)
        inv = lax.rsqrt(jnp.mean(c * c, -1, keepdims=True) + epsilon)
        return c * inv, inv

    def norm_one(i):
        rows = at(i, 64)
        n, inv = norm(r["n2"][rows, :])
        r["n1"][rows, :] = n
        r["i1"][rows, :] = inv
        r["nl"][rows, :] = (n * vec[V_G1 : V_G1 + 1, :] + vec[V_S1 : V_S1 + 1, :]).astype(BF)

    loop(ROWS // 64, norm_one, 5)

    def ffn(b):
        tiles = []
        for n in range(3):
            bias = vec[pl.ds(V_BI + b, 1), at(n, 256)]
            tiles.append(dot(r["nl"][...], r["wi"][:, at(3 * b + n, 256)]) + bias)
        for n, pre in enumerate(tiles):
            cols = at(n, 256)
            cdf = 0.5 * (1.0 + lax.erf(pre * 0.7071067811865476))
            r["slope"][b, :, cols] = (
                cdf + pre * jnp.exp(-0.5 * pre * pre) * 0.3989422804014327
            ).astype(BF)
            post = (pre * cdf).astype(BF)
            r["grad"][4 + b, 0:3, :, :, cols] = post[: 6 * SR].reshape(3, 2, SR, 256)
            r["grad"][4 + b, 3, 0, 0 : ROWS - 6 * SR, cols] = post[6 * SR :]

    r["wait"](4)
    loop(4, ffn)

    def resid_two(n):
        cols = at(n, 256)
        acc = r["n1"][:, cols] * vec[V_G1 : V_G1 + 1, cols] + vec[V_S1 : V_S1 + 1, cols]
        acc = acc + vec[V_BB : V_BB + 1, cols]
        for b in range(4):
            acc = acc + dot(post_block(r, b, pl.ds(0, CW)), r["wb"][b, :, cols])
        r["n2"][:, cols] = acc

    r["wait"](5)
    loop(3, resid_two, 3)

    def norm_two(i):
        rows = at(i, 128)
        n, inv = norm(r["n2"][rows, :])
        r["n2"][rows, :] = n
        r["i2"][rows, :] = inv
        r["s2"][rows, :] = (n * vec[V_G2 : V_G2 + 1, :] + vec[V_S2 : V_S2 + 1, :]).astype(BF)

    r["wait"](6)

    def project(rows):
        proj = dot(r["s2"][rows, :], r["wp"][...])
        il = lax.rsqrt(jnp.sum(proj * proj, -1, keepdims=True) + epsilon)
        unit = proj * il
        r["il"][rows, :] = il
        r["unit"][rows, :] = unit
        r["emb"][rows, :] = unit.astype(BF)

    norm_two(PR // 128)
    project(pl.ds(PR, QR))
    send_queries()
    for i in range(PR // 128):
        norm_two(i)
    project(pl.ds(0, PR))


def post_block(r, b, cols):
    top = r["grad"][4 + b, 0:3, :, :, cols].reshape(6 * SR, cols.size)
    return jnp.concatenate([top, r["grad"][4 + b, 3, 0, 0 : ROWS - 6 * SR, cols]], 0)


def peers(r, g, p, src, buf, ss, rs):
    copies = []
    for o in range(1, PSG):
        to = (p + o) % PSG
        copies.append(remote(src(to), buf.at[p], ss.at[o - 1], rs.at[o - 1], (g, to)))
    return copies


def query_copies(r, g, p):
    src = r["emb"].at[pl.ds(PR, QR), :]
    return peers(r, g, p, lambda to: src, r["gq"], r["q_s"], r["q_r"])


def turn_post(r, i):
    b, half = i // 2, i % 2
    t = post_block(r, b, at(half, 384)).T
    for q in range(4):
        r["grad"][8 + q, b, half, :, 0:ROWS] = t[SR * q : SR * (q + 1)]


def maxsim(r, g, p):
    emb = r["emb"]
    queries = query_copies(r, g, p)
    r["gq"][p] = emb[PR:ROWS, :]
    for cp in queries:
        cp.wait()

    key_at = lax.broadcasted_iota(jnp.int32, (PSG * QDEV * QLEN, PLEN), 1)
    nq = PSG * QDEV
    half = QDEV * QLEN
    sums = []
    for m in range(MB):
        gq = jnp.concatenate([r["gq"][d, half * m : half * (m + 1), :] for d in range(PSG)], 0)
        s = dot_nt(gq, emb[PLEN * m : PLEN * (m + 1), :])
        e = jnp.where(key_at < r["len"][m], jnp.exp(s * (1.0 / temper)), 0.0)
        total = jnp.sum(e, -1, keepdims=True)
        r["sim"][m] = e
        sums.append(total)
        log = jnp.broadcast_to(jnp.log(total), (nq * QLEN, 128))
        r["sc"][p, nq * m : nq * (m + 1), :] = temper * jnp.sum(log.reshape(nq, QLEN, 128), 1)
    scores = peers(r, g, p, lambda to: r["sc"].at[p], r["sc"], r["s_s"], r["s_r"])
    for cp in scores:
        cp.start()
    loop(6, lambda i: turn_post(r, i))
    for cp in scores:
        cp.wait()
    every = [r["sc"][d] for d in range(PSG)]
    top = functools.reduce(jnp.maximum, every)
    log_total = top + jnp.log(sum(jnp.exp(v - top) for v in every))
    row = lax.broadcasted_iota(jnp.int32, (MB * nq, 128), 0)
    pos = jnp.zeros((MB * nq, 128), jnp.int32)
    for m in range(MB):
        for q in range(nq):
            pos = jnp.where(row == nq * m + q, r["pos"][m, q], pos)
    picked = sum(jnp.where(pos == d, every[d], 0.0) for d in range(PSG))
    r["lo"][...] = log_total - picked
    grad_score = jnp.exp(r["sc"][p] - log_total) - (pos == p).astype(F32)
    for m in range(MB):
        gs = grad_score[nq * m : nq * (m + 1)]
        gs = jnp.broadcast_to(gs[:, None, :], (nq, QLEN, 128)).reshape(nq * QLEN, 128)
        coef = gs * (1.0 / sums[m])
        coef = jnp.concatenate([coef, coef], 1)
        ds = (coef * r["sim"][m]).astype(BF)
        pe = emb[PLEN * m : PLEN * (m + 1), :]
        gg = dot(ds, pe).astype(BF)
        for d in range(PSG):
            r["gg"][d, half * m : half * (m + 1), :] = gg[half * d : half * (d + 1)]
        gq = jnp.concatenate([r["gq"][d, half * m : half * (m + 1), :] for d in range(PSG)], 0)
        r["de"][PLEN * m : PLEN * (m + 1), :] = dot_tn(ds, gq).astype(BF)
    backs = peers(r, g, p, lambda to: r["gg"].at[to], r["gr"], r["g_s"], r["g_r"])
    for cp in backs:
        cp.start()
    r["gr"][p] = r["gg"][p]
    loop(2, lambda i: turn_post(r, 6 + i))
    sums = head_back(r, 0, PR)
    for cp in backs:
        cp.wait()
    r["de"][PR:ROWS, :] = sum(r["gr"][d].astype(F32) for d in range(PSG)).astype(BF)
    for row, one, two in zip((5, 6, 7), sums, head_back(r, PR, QR)):
        r["sm"][row : row + 1, :] = jnp.sum(one + two, 0, keepdims=True)


def norm_back(grad_out, n, inv, gain):
    gn = grad_out * gain
    return inv * (
        gn - jnp.mean(gn, -1, keepdims=True) - n * jnp.mean(gn * n, -1, keepdims=True)
    )


def head_back(r, first, count):
    vec = r["vec"]
    some = pl.ds(first, count)
    gu = r["de"][some, :].astype(F32)
    unit = r["unit"][some, :]
    along = jnp.sum(gu * unit, -1, keepdims=True)
    r["gp"][some, :] = (r["il"][some, :] * (gu - unit * along)).astype(BF)
    sums = None
    for i in range(count // 128):
        rows = pl.ds(first + 128 * i, 128)
        g2 = dot_nt(r["gp"][rows, :], r["wp"][...])
        n = r["n2"][rows, :]
        gr = norm_back(g2, n, r["i2"][rows, :], vec[V_G2 : V_G2 + 1, :])
        low = gr.astype(BF)
        r["n2"][rows, :] = gr
        r["gb"][rows, :] = low
        add = (fold(low.astype(F32)), fold(g2 * n), fold(g2))
        sums = add if sums is None else tuple(a + b for a, b in zip(sums, add))
    return sums


def backward_step(r, t):
    vec, qkv, grad = r["vec"], r["qkv"], r["grad"]
    lane = lax.broadcasted_iota(jnp.int32, (1, 128), 1)
    masks = [(lane < HD).astype(BF), (lane >= HD).astype(BF)]

    def outer(left, right, k, n):
        grad[k, :, :, :, at(n, 256)] = dot(left, right).astype(BF).reshape(4, 2, SR, 256)

    def turn(src, n):
        r["lt"][at(n, 256), :] = src[:, at(n, 256)].T

    @pl.when(t < 4)
    def _():
        def tile(n):
            left = grad[8 + t, :, :, :, 0:ROWS].reshape(CW, ROWS)
            outer(left, r["gb"][:, at(n, 256)], t, n)

        loop(3, tile, 3)

    @pl.when(t == 4)
    def _():
        loop(3, lambda n: turn(r["nl"], n), 3)

    @pl.when((t >= 4) & (t < 8))
    def _():
        b = t - 4

        def tile(n):
            cols = at(n, 256)
            v = dot_nt(r["gb"][...], r["wb"][b, cols, :]) * r["slope"][b, :, cols].astype(F32)
            low = v.astype(BF)
            r["slope"][b, :, cols] = low
            r["sm"][pl.ds(8 + b, 1), cols] = jnp.sum(low.astype(F32), 0, keepdims=True)
            outer(r["lt"][...], low, 4 + b, n)

        loop(3, tile, 3)

    @pl.when(t == 8)
    def _():
        loop(3, lambda n: turn(r["s2"], n), 3)
        v = dot(r["lt"][...], r["gp"][...]).astype(BF)
        r["gmini"][:, :, :, 0:PROJ] = v.reshape(4, 2, SR, PROJ)

    @pl.when((t >= 8) & (t < 11))
    def _():
        n = t - 8
        cols = at(n, 256)
        acc = r["n2"][:, cols]
        for b in range(4):
            acc = acc + dot_nt(r["slope"][b], r["wi"][cols, CW * b : CW * (b + 1)])
        r["n2"][:, cols] = acc

    @pl.when(t == 11)
    def _():
        def body(i, sums):
            rows = at(i, 64)
            g1, n = r["n2"][rows, :], r["n1"][rows, :]
            gr = norm_back(g1, n, r["i1"][rows, :], vec[V_G1 : V_G1 + 1, :])
            low = gr.astype(BF)
            r["n1"][rows, :] = gr
            r["gb"][rows, :] = low
            add = (fold(low.astype(F32)), fold(g1 * n), fold(g1))
            return tuple(a + b for a, b in zip(sums, add))

        zero = jnp.zeros((8, D), F32)
        sums = lax.fori_loop(0, ROWS // 64, body, (zero, zero, zero), unroll=5)
        for row, v in zip((2, 3, 4), sums):
            r["sm"][row : row + 1, :] = jnp.sum(v, 0, keepdims=True)
        loop(3, lambda n: turn(r["att"], n), 3)
        loop(3, lambda n: outer(r["lt"][...], r["gb"][:, at(n, 256)], 8, n), 3)

    @pl.when(t == 12)
    def _():
        def tile(n):
            r["att"][:, at(n, 256)] = dot_nt(r["gb"][...], r["wo"][at(n, 256), :]).astype(BF)

        loop(3, tile, 3)
        loop(3, lambda n: turn(r["x"], n), 3)

    @pl.when((t >= 13) & (t < 13 + PAIRS))
    def _():
        hp = t - 13
        cols = at(hp, 128)
        segs = [(pl.ds(PLEN * m, PLEN), r["pp"], 12 * m) for m in range(MB)]
        segs.append((pl.ds(PR, QR), r["pq"], 0))
        work = []
        for rows, p_ref, first in segs:
            q, k, v = qkv[0, rows, cols], qkv[1, rows, cols], qkv[2, rows, cols]
            a = r["att"][rows, cols]
            for h in range(2):
                ah = a * masks[h]
                work.append((q * masks[h], ah, p_ref[first + 2 * hp + h], dot_nt(v, ah)))
        grads = []
        for qh, ah, pr, dp in work:
            pf = pr.astype(F32)
            ds = (pf * (dp - jnp.sum(pf * dp, 0, keepdims=True))).astype(BF)
            grads.append(ds)
        bq = bv = 0.0
        for m, (rows, _, _) in enumerate(segs):
            kt = qkv[1, rows, cols].T
            dk = dv = 0.0
            parts = []
            for h in range(2):
                qh, ah, pr, _ = work[2 * m + h]
                ds = grads[2 * m + h]
                parts.append((dot(kt[HD * h : HD * (h + 1)], ds) * 0.125).astype(BF))
                dk = dk + dot(ds, qh)
                dv = dv + dot(pr, ah)
            dq = jnp.concatenate(parts, 0).T
            dv = dv.astype(BF)
            qkv[0, rows, cols] = dq
            qkv[1, rows, cols] = (dk * 0.125).astype(BF)
            qkv[2, rows, cols] = dv
            bq = bq + jnp.sum(dq.astype(F32), 0, keepdims=True)
            bv = bv + jnp.sum(dv.astype(F32), 0, keepdims=True)
        r["sm"][0:1, cols] = bq
        r["sm"][1:2, cols] = bv

    @pl.when((t == 14) | (t == 16) | (t == 18))
    def _():
        i = (t - 14) // 2
        loop(3, lambda b: outer(r["lt"][...], qkv[b, :, at(i, 256)], 9 + i, b), 3)

    @pl.when(t == 19)
    def _():
        small = r["sm"][...].T
        one = lax.broadcasted_iota(jnp.int32, (SR, 128), 1)
        pad = jnp.zeros((SR, 128 - small.shape[1]), F32)
        for s in range(SHARDS):
            v = jnp.concatenate([small[SR * s : SR * (s + 1)], pad], 1)
            b, base = s // 2, 384 * (s % 2)
            v = jnp.where(one < 8, v, 0.0)
            for q in range(4):
                col = small[base + SR * q : base + SR * (q + 1), 8 + b : 9 + b]
                v = jnp.where(one == 8 + q, col, v)
            r["gmini"][s // 2, s % 2, :, PROJ:MW] = v.astype(BF)

    @pl.when((t >= 20) & (t < 23))
    def _():
        n = t - 20
        cols = at(n, 256)
        acc = r["n1"][:, cols]
        for b in range(3):
            acc = acc + dot_nt(qkv[b], r["wq"][cols, CW * b : CW * (b + 1)])
        r["gb"][:, cols] = acc.astype(BF)


def slot_of(t):
    k = jnp.where(t < 8, t, -1)
    for step, which in ((11, 8), (14, 9), (16, 10), (18, 11)):
        k = jnp.where(t == step, which, k)
    return jnp.where(t >= LAST_ENTER, t - LAST_ENTER + NC, k)


LAST_ENTER = 19


class Reducer:
    def __init__(self, r, g, p):
        self.r = r
        self.p = p
        self.z, self.y = g // 2, g % 2
        self.x, self.c = p // 2, p % 2
        z, y, x, c = self.z, self.y, self.x, self.c
        self.sib = (g, p + 1 - 2 * c)
        self.ynb = (g + 1 - 2 * y, p)
        self.xnb = (g, (p + 2) % 4)
        self.outer = (z == 0) | (z == 3)
        self.line = [(2 * ((z + o) % 4) + y, p) for o in range(1, 4)]
        self.own = pl.ds(pl.multiple_of(c * HALF, 16), HALF)
        self.oth = pl.ds(pl.multiple_of((1 - c) * HALF, 16), HALF)

    def unit(self, k, core):
        r = self.r
        u = lambda: None
        u.k, u.core = k, core
        if isinstance(k, int) and k == NC:
            u.width = MW
            u.g = r["gmini"]
            u.cs, u.s, u.ls = CORE_SLOTS, SLOTS, LINE_SLOTS
            for name in ("core_rv", "first_a", "first_b", "second_b", "line_rv", "cross_rv", "done"):
                setattr(u, name, r["m_" + name])
        else:
            u.width = CW
            u.g = r["grad"].at[k]
            u.cs, u.s, u.ls = k % CORE_SLOTS, k % SLOTS, k % LINE_SLOTS
            u.core_rv = r["core_rv"].at[u.cs]
            for name in ("first_a", "first_b", "second_b", "cross_rv"):
                setattr(u, name, r[name].at[u.s])
            u.line_rv = r["line_rv"].at[u.ls]
            u.done = r["done"].at[k]
        return u

    def add_into(self, dst, src):
        dst[...] = (dst[...].astype(F32) + src[...].astype(F32)).astype(BF)

    def half(self, u, xx):
        w = u.width // 2
        return pl.ds(pl.multiple_of(xx * w, 128), w)

    def core_copy(self, u):
        r = self.r
        return remote(
            u.g.at[:, :, self.oth, :], u.core_rv, r["c_s"].at[u.cs], r["c_r"].at[u.cs], self.sib
        )

    def core_end(self, u):
        self.core_copy(u).wait()
        loop(
            SHARDS,
            lambda i: self.add_into(
                u.g.at[i // 2, i % 2, self.own, :], u.core_rv.at[i // 2, i % 2]
            ),
        )

    def one_copy(self, u):
        r = self.r
        sems = r["one_s"].at[u.s], r["one_r"].at[u.s]
        if u.core == 0:
            return remote(u.g.at[:, 1 - self.y, self.own, :], u.first_a, *sems, self.ynb)
        away = self.half(u, 1 - self.x)
        return remote(u.g.at[:, :, self.own, away], u.first_b, *sems, self.xnb)

    def one_start(self, u):
        self.one_copy(u).start()

    def one_end(self, u):
        self.one_copy(u).wait()
        if u.core == 0:
            loop(
                4, lambda i: self.add_into(u.g.at[i, self.y, self.own, :], u.first_a.at[i])
            )
        else:
            mine = self.half(u, self.x)
            loop(
                SHARDS,
                lambda i: self.add_into(
                    u.g.at[i // 2, i % 2, self.own, mine], u.first_b.at[i // 2, i % 2]
                ),
            )

    def two_copy(self, u):
        r = self.r
        return remote(
            u.g.at[:, 1 - self.y, self.own, self.half(u, self.x)],
            u.second_b,
            r["two_s"].at[u.s],
            r["two_r"].at[u.s],
            self.ynb,
        )

    def two_start(self, u):
        self.two_copy(u).start()

    def two_end(self, u):
        self.two_copy(u).wait()
        mine = self.half(u, self.x)
        loop(
            4, lambda i: self.add_into(u.g.at[i, self.y, self.own, mine], u.second_b.at[i])
        )

    def part(self, u, d):
        cols = slice(None) if u.core == 0 else self.half(u, self.x)
        return u.g.at[d, self.y, self.own, cols]

    def seen(self, i):
        return jnp.where(self.z < 2, i, 3 - i)

    def landing(self, u, i):
        return u.line_rv.at[i, :, pl.ds(0, u.width // (1 + u.core))]

    def line_copy(self, u, i, slot, send):
        r, d = self.r, self.seen(i)
        to = self.seen(jnp.where(self.outer, 1, i))
        return remote(
            self.part(u, d),
            self.landing(u, slot),
            r["z_s"].at[4 * u.ls + send],
            r["z_r"].at[4 * u.ls + slot],
            (2 * to + self.y, self.p),
        )

    def out_copies(self, u):
        return [self.line_copy(u, i, i - 1, i - 1) for i in (3, 2, 1)]

    def own_copy(self, u):
        return self.line_copy(u, 0, 0, 3)

    def in_copies(self, u):
        return [self.line_copy(u, 3, 1, 1), self.line_copy(u, 2, 3, 0)]

    def arrived(self, u, slot):
        self.line_copy(u, 0, slot, 0).wait_recv()
        return self.landing(u, slot)

    def line_one(self, u):
        @pl.when(self.outer)
        def _():
            for cp in self.out_copies(u):
                cp.start()

        @pl.when(jnp.logical_not(self.outer))
        def _():
            self.own_copy(u).start()

    def line_two(self, u):
        @pl.when(self.outer)
        def _():
            self.add_into(self.part(u, self.z), self.arrived(u, 0))
            for cp in self.out_copies(u):
                cp.wait_send()

        @pl.when(jnp.logical_not(self.outer))
        def _():
            for i in (3, 2, 1):
                self.add_into(self.part(u, self.seen(i)), self.arrived(u, i - 1))
                if i > 1:
                    self.in_copies(u)[3 - i].start()
            self.own_copy(u).wait_send()

    def line_end(self, u):
        mine = self.part(u, self.z)

        @pl.when(self.outer)
        def _():
            self.add_into(mine, self.arrived(u, 1))

        @pl.when(jnp.logical_not(self.outer))
        def _():
            self.add_into(mine, self.arrived(u, 3))
            for cp in self.in_copies(u):
                cp.wait_send()

    def last_copy(self, u):
        r = self.r
        sems = r["last_s"].at[u.s], r["last_r"].at[u.s]
        to = u.cross_rv if u.core == 0 else u.done.at[:, self.half(u, self.x)]
        return remote(self.part(u, self.z), to, *sems, self.xnb)

    def last_start(self, u):
        self.last_copy(u).start()

    def last_end(self, u):
        self.last_copy(u).wait()
        mine = self.part(u, self.z)[...]
        if u.core == 0:
            u.done[...] = (mine.astype(F32) + u.cross_rv[...].astype(F32)).astype(BF)
        else:
            u.done[:, self.half(u, self.x)] = mine

    def to_outputs(self, u, do):
        r, k, own = self.r, u.k, self.own

        def both(dst):
            do(pltpu.make_async_copy(u.done, dst, r["st_sem"].at[k]))
            do(remote(u.done, dst, r["fin_s"].at[k], r["fin_r"].at[k], self.sib))

        if isinstance(k, int) and k == NC:
            both(r["mini_o"].at[own, :])
            return

        @pl.when(k < 4)
        def _():
            both(r["back_o"].at[pl.ds(pl.multiple_of(SR * k + HALF * self.c, 16), HALF), :])

        @pl.when((k >= 4) & (k < 8))
        def _():
            both(r["in_o"].at[own, at(k - 4, CW)])

        @pl.when(k == 8)
        def _():
            both(r["out_o"].at[own, :])

        @pl.when(k > 8)
        def _():
            both(r["qkv_o"].at[own, at(k - 9, CW)])

    def stages(self, core):
        out = lambda u: self.to_outputs(u, lambda cp: cp.start())
        core_start = lambda u: self.core_copy(u).start()
        if core == 0:
            return {
                0: [core_start],
                1: [self.core_end, self.one_start],
                4: [self.one_end, self.line_one],
                6: [self.line_two],
                8: [self.line_end, self.last_start],
                10: [self.last_end, out],
            }
        return {
            0: [core_start],
            1: [self.core_end, self.one_start],
            4: [self.one_end, self.two_start],
            6: [self.two_end, self.line_one],
            8: [self.line_two],
            10: [self.line_end, self.last_start],
            12: [self.last_end, out],
        }

    def slot(self, t):
        for core in range(2):

            @pl.when(self.c == core)
            def _():
                stages = self.stages(core)
                for s in sorted(stages, reverse=True):
                    k = t - s

                    @pl.when((k >= 0) & (k < NC))
                    def _():
                        for do in stages[s]:
                            do(self.unit(k, core))

                    @pl.when(k == NC)
                    def _():
                        for do in stages[s]:
                            do(self.unit(NC, core))

    def finish(self, k):
        self.to_outputs(self.unit(k, 0), lambda cp: cp.wait())


VECTORS = ("v_bq", "v_bv", "v_bo", "v_g1", "v_s1", "v_bb", "v_g2", "v_s2", "v_bi")
INPUTS = ("len", "pos") + VECTORS + ("xp_h", "xq_h", "wq_h", "wo_h", "wi_h", "wb_h", "wp_h")


def kernel(spread, names, *refs):
    r = dict(zip(names, refs))
    g = lax.axis_index("group")
    p = lax.axis_index("psg")
    barrier = pltpu.get_barrier_semaphore()

    def greet(dev):
        pl.semaphore_signal(barrier, inc=1, device_id=dev, device_id_type=MESH)

    for o in range(1, PSG):
        greet((g, (p + o) % PSG))
    count = PSG - 1
    if spread:
        red = Reducer(r, g, p)
        for dev in [red.ynb] + red.line:
            greet(dev)
        count = count + 4

    pairs = [
        (r["xp_h"], r["x"].at[pl.ds(0, PR), :]),
        (r["xq_h"], r["x"].at[pl.ds(PR, QR), :]),
        (r["wq_h"], r["wq"]),
        (r["wo_h"], r["wo"]),
        (r["wi_h"], r["wi"]),
        (r["wb_h"], r["wb"]),
        (r["wp_h"], r["wp"]),
    ]
    row = 0
    for name in VECTORS:
        v = r[name][...].astype(F32)
        n = v.shape[0] // D
        for i in range(n):
            r["vec"][row + i : row + i + 1, :] = v[D * i : D * (i + 1)].reshape(1, D)
        row += n
        if name == "v_bq":
            r["vec"][row : row + 1, :] = jnp.zeros((1, D), F32)
            row += 1
    loads = [pltpu.make_async_copy(a, b, r["in_sem"].at[i]) for i, (a, b) in enumerate(pairs)]
    for cp in loads[:3]:
        cp.start()

    def wait(*which):
        for i in which:
            loads[i].wait()
        if 2 in which:
            for cp in loads[3:]:
                cp.start()

    r["wait"] = wait

    def send_queries():
        pl.semaphore_wait(barrier, count)
        for cp in query_copies(r, g, p):
            cp.start()

    forward(r, send_queries)
    maxsim(r, g, p)
    lane = lax.broadcasted_iota(jnp.int32, (1, 128), 1)
    for m in range(MB):
        v = jnp.zeros((1, 128), F32)
        for q in range(QDEV):
            v = jnp.where(lane == q, r["lo"][pl.ds(PSG * QDEV * m + QDEV * p + q, 1), :], v)
        r["loss_o"][m : m + 1, :] = v

    def step(t):
        backward_step(r, t)
        if spread:
            now = slot_of(t)

            @pl.when(now >= 0)
            def _():
                red.slot(now)


    loop(LAST_ENTER + 13 if spread else 23, step)

    outs = [
        (r["emb"].at[pl.ds(0, PR), :], r["ep_o"]),
        (r["emb"].at[pl.ds(PR, QR), :], r["eq_o"]),
        (r["gb"].at[pl.ds(0, PR), :], r["gxp_o"]),
        (r["gb"].at[pl.ds(PR, QR), :], r["gxq_o"]),
    ]
    if not spread:
        outs += [(r["grad"], r["grad_o"]), (r["gmini"], r["mini_o"])]
    stores = [pltpu.make_async_copy(a, b, r["out_sem"].at[i]) for i, (a, b) in enumerate(outs)]
    for cp in stores:
        cp.start()
    for cp in stores:
        cp.wait()
    if spread:
        loop(NC, red.finish)
        red.finish(NC)


def run_step(spread, inputs):
    sds = jax.ShapeDtypeStruct
    outs = {
        "loss_o": sds((MB, 128), F32),
        "eq_o": sds((QR, PROJ), BF),
        "ep_o": sds((PR, PROJ), BF),
        "gxq_o": sds((QR, D), BF),
        "gxp_o": sds((PR, D), BF),
    }
    if spread:
        outs |= {
            "back_o": sds((4 * SR, D), BF),
            "in_o": sds((SR, FF), BF),
            "out_o": sds((SR, D), BF),
            "qkv_o": sds((SR, 3 * D), BF),
            "mini_o": sds((SR, MW), BF),
        }
    else:
        outs |= {
            "grad_o": sds((NC, 4, 2, SR, CW), BF),
            "mini_o": sds((4, 2, SR, MW), BF),
        }
    vm = pltpu.VMEM
    dma = pltpu.SemaphoreType.DMA
    scratch = {
        "vec": vm((16, D), F32),
        "x": vm((ROWS, D), BF),
        "wq": vm((D, 3 * D), BF),
        "wo": vm((D, D), BF),
        "wi": vm((D, FF), BF),
        "wb": vm((4, CW, D), BF),
        "wp": vm((D, PROJ), BF),
        "qkv": vm((3, ROWS, D), BF),
        "pp": vm((MB * 12, PLEN, PLEN), BF),
        "pq": vm((12, QR, QR), BF),
        "att": vm((ROWS, D), BF),
        "n1": vm((ROWS, D), F32),
        "n2": vm((ROWS, D), F32),
        "i1": vm((ROWS, 1), F32),
        "i2": vm((ROWS, 1), F32),
        "il": vm((ROWS, 1), F32),
        "nl": vm((ROWS, D), BF),
        "slope": vm((4, ROWS, CW), BF),
        "s2": vm((ROWS, D), BF),
        "unit": vm((ROWS, PROJ), F32),
        "emb": vm((ROWS, PROJ), BF),
        "de": vm((ROWS, PROJ), BF),
        "gp": vm((ROWS, PROJ), BF),
        "gb": vm((ROWS, D), BF),
        "lt": vm((D, ROWS), BF),
        "sm": vm((16, D), F32),
        "gq": vm((PSG, QR, PROJ), BF),
        "sim": vm((MB, PSG * QDEV * QLEN, PLEN), F32),
        "sc": vm((PSG, MB * PSG * QDEV, 128), F32),
        "lo": vm((MB * PSG * QDEV, 128), F32),
        "gg": vm((PSG, QR, PROJ), BF),
        "gr": vm((PSG, QR, PROJ), BF),
        "grad": vm((NC, 4, 2, SR, CW), BF),
        "gmini": vm((4, 2, SR, MW), BF),
        "in_sem": dma((7,)),
        "out_sem": dma((6,)),
    }
    for name in ("q_s", "q_r", "s_s", "s_r", "g_s", "g_r"):
        scratch[name] = dma((PSG - 1,))
    if spread:
        for lead, slots, w, pre in ((True, (CORE_SLOTS, SLOTS, NC), CW, ""), (False, None, MW, "m_")):
            a, b, c = ((slots[0],), (slots[1],), (slots[2],)) if lead else ((), (), ())
            scratch[pre + "core_rv"] = vm(a + (4, 2, HALF, w), BF)
            scratch[pre + "first_a"] = vm(b + (4, HALF, w), BF)
            scratch[pre + "first_b"] = vm(b + (4, 2, HALF, w // 2), BF)
            scratch[pre + "second_b"] = vm(b + (4, HALF, w // 2), BF)
            scratch[pre + "line_rv"] = vm((LINE_SLOTS,) * len(b) + (4, HALF, w), BF)
            scratch[pre + "cross_rv"] = vm(b + (HALF, w), BF)
            scratch[pre + "done"] = vm(c + (HALF, w), BF)
        for name in ("c_s", "c_r"):
            scratch[name] = dma((CORE_SLOTS + 1,))
        for name in ("one_s", "one_r", "two_s", "two_r", "last_s", "last_r"):
            scratch[name] = dma((SLOTS + 1,))
        for name in ("z_s", "z_r"):
            scratch[name] = dma((4 * (LINE_SLOTS + 1),))
        for name in ("st_sem", "fin_s", "fin_r"):
            scratch[name] = dma((NC + 1,))
    hbm = pl.BlockSpec(memory_space=pl.ANY)
    vmem = pl.BlockSpec(memory_space=pltpu.VMEM)
    smem = pl.BlockSpec(memory_space=pltpu.SMEM)
    names = INPUTS + tuple(outs) + tuple(scratch)
    res = pl.pallas_call(
        functools.partial(kernel, spread, names),
        out_shape=list(outs.values()),
        in_specs=[smem, smem] + [vmem] * len(VECTORS) + [hbm] * 7,
        out_specs=[vmem] + [hbm] * (len(outs) - 1),
        scratch_shapes=list(scratch.values()),
        compiler_params=pltpu.CompilerParams(
            collective_id=0, has_side_effects=True, vmem_limit_bytes=64 << 20
        ),
        name="train_step",
    )(*inputs)
    return dict(zip(outs, res))


WIDE = ("eq_o", "ep_o", "gxq_o", "gxp_o")
GRADS = ("qkv_o", "out_o", "in_o", "back_o")


def finish_kernel(*refs):
    names = ("loss", "mini") + GRADS + WIDE
    n = len(names)
    i = dict(zip(names, refs[:n]))
    o = dict(zip(("loss",) + WIDE + GRADS + ("proj", "bias_in"), refs[n:]))
    o["loss"][...] = i["loss"][:, 0:QDEV]

    def move(v):
        def cast(j):
            o[v][at(j, 32), :] = i[v][at(j, 32), :].astype(o[v].dtype)

        loop(i[v].shape[0] // 32, cast)

    for v in GRADS[1:] + WIDE:
        move(v)
    for b in range(3):
        for n in range(3):
            to = slice(CW * b + 256 * n, CW * b + 256 * (n + 1))
            of = slice(CW * n + 256 * b, CW * n + 256 * (b + 1))
            o["qkv_o"][:, to] = i["qkv_o"][:, of].astype(F32)
    o["proj"][...] = i["mini"][:, 0:PROJ].astype(F32)
    small = i["mini"][:, PROJ:MW].astype(F32).T
    for j, ref in enumerate(refs[-8:]):
        ref[...] = small[j, 0:SR]
    o["bias_in"][...] = jnp.concatenate([small[8 + q : 9 + q, 0:SR] for q in range(4)], 1)[0]


def finish_step(o):
    sds = jax.ShapeDtypeStruct
    like = lambda v, t: sds(o[v].shape, t)
    outs = [sds((MB, QDEV), F32)]
    outs += [like(v, BF) for v in WIDE] + [like(v, F32) for v in GRADS]
    outs += [sds((SR, PROJ), F32), sds((4 * SR,), F32)] + [sds((SR,), F32)] * 8
    vmem = pl.BlockSpec(memory_space=pltpu.VMEM)
    res = pl.pallas_call(
        finish_kernel,
        out_shape=outs,
        in_specs=[vmem] * 10,
        out_specs=[vmem] * 19,
        name="finish",
    )(o["loss_o"], o["mini_o"], *[o[v] for v in GRADS], *[o[v] for v in WIDE])
    moved = dict(zip(("loss_o",) + WIDE, res[:5]))
    qkv, w_out, w_in, back, proj, bias_in = res[5:11]
    v = res[11:]
    return moved, (
        qkv, v[0], v[1], w_out, v[2], v[3], v[4], w_in, bias_in,
        back, v[5], v[6], v[7], proj,
    )


def body(
    query_input,
    passage_input,
    lengths,
    positive,
    w_qkv,
    bias_q,
    bias_v,
    w_out,
    bias_out,
    norm1_gain,
    norm1_bias,
    w_in,
    bias_in,
    w_back,
    bias_back,
    norm2_gain,
    norm2_bias,
    w_proj,
):
    spread = lax.axis_size("group") == SHARDS
    inputs = (
        lengths.reshape(MB),
        positive,
        bias_q,
        bias_v,
        bias_out,
        norm1_gain,
        norm1_bias,
        bias_back,
        norm2_gain,
        norm2_bias,
        bias_in,
        passage_input.reshape(PR, D),
        query_input.reshape(QR, D),
        w_qkv,
        w_out,
        w_in,
        w_back.reshape(4, CW, D),
        w_proj,
    )
    o = run_step(spread, inputs)
    if spread:
        o, finals = finish_step(o)
    else:
        full = o["grad_o"].reshape(NC, SHARDS, SR, CW)
        mini = o["mini_o"].reshape(D, MW)
        small = mini[:, PROJ : PROJ + 8]
        wide = o["mini_o"].reshape(SHARDS, SR, MW)[:, :, PROJ + 8 : PROJ + 12].transpose(0, 2, 1).reshape(FF)
        halves = full[9:12].reshape(3, D, 3, 256).transpose(1, 2, 0, 3).reshape(D, 3 * D)
        terms = (
            halves,
            small[:, 0],
            small[:, 1],
            full[8].reshape(D, D),
            small[:, 2],
            small[:, 3],
            small[:, 4],
            full[4:8].reshape(4, D, CW).transpose(1, 0, 2).reshape(D, FF),
            wide,
            full[0:4].transpose(1, 0, 2, 3).reshape(FF, D),
            small[:, 5],
            small[:, 6],
            small[:, 7],
            mini[:, :PROJ],
        )
        shared = lax.psum_scatter(terms, "group", scatter_dimension=0, tiled=True)
        finals = lax.psum(shared, "psg")
    return (
        o["loss_o"][:, :QDEV],
        o["eq_o"].reshape(MB, QDEV, QLEN, PROJ),
        o["ep_o"].reshape(MB, -1, PLEN, PROJ),
        o["gxq_o"].reshape(query_input.shape),
        o["gxp_o"].reshape(passage_input.shape),
    ) + tuple(part.astype(F32) for part in finals)


def solution(mesh):
    in_specs = (
        P(None, ("group", "psg"), None, None),
        P(None, ("group", "psg"), None, None),
        P(None, ("group", "psg")),
        P(None, "group"),
        P(),
        P(),
        P(),
        P(),
        P(),
        P(),
        P(),
        P(),
        P(),
        P(),
        P(),
        P(),
        P(),
        P(),
    )
    out_specs = (
        P(None, ("group", "psg")),
        P(None, ("group", "psg"), None, None),
        P(None, ("group", "psg"), None, None),
        P(None, ("group", "psg"), None, None),
        P(None, ("group", "psg"), None, None),
        P("group", None),
        P("group"),
        P("group"),
        P("group", None),
        P("group"),
        P("group"),
        P("group"),
        P("group", None),
        P("group"),
        P("group", None),
        P("group"),
        P("group"),
        P("group"),
        P("group", None),
    )
    return jax.shard_map(body, mesh=mesh, in_specs=in_specs, out_specs=out_specs, check_vma=False)
```

```python
import functools

import jax
import jax.numpy as jnp
from jax import lax
from jax.experimental import pallas as pl
from jax.experimental.pallas import tpu as pltpu
from jax.sharding import PartitionSpec as P

D = 768
HD = 64
FF = 3072
PROJ = 128
QLEN = 32
PLEN = 256
MB = 2
QDEV = 2
PSG = 4

PR = MB * PLEN
QR = MB * QDEV * QLEN
ROWS = PR + QR
PAIRS = D // 128
NC = 12
CW = 768
MW = 256
SHARDS = 8
SR = D // SHARDS
HALF = SR // 2
CORE_SLOTS = 2
SLOTS = 6
LINE_SLOTS = 6

temper = 0.1
epsilon = 1e-06
masked = -1e30

MESH = pl.DeviceIdType.MESH
BF = jnp.bfloat16
F32 = jnp.float32


def dot(a, b):
    return jnp.dot(a, b, preferred_element_type=F32)


def dot_nt(a, b):
    return lax.dot_general(a, b, (((1,), (1,)), ((), ())), preferred_element_type=F32)


def dot_tn(a, b):
    return lax.dot_general(a, b, (((0,), (0,)), ((), ())), preferred_element_type=F32)


def at(i, size):
    return pl.ds(i * size if isinstance(i, int) else pl.multiple_of(i * size, size), size)


def loop(n, body, unroll=1):
    def step(i, carry):
        body(i)
        return carry

    lax.fori_loop(0, n, step, 0, unroll=unroll)


def fold(v):
    return jnp.sum(v.reshape(v.shape[0] // 8, 8, v.shape[1]), 0)


def remote(src, dst, ss, rs, dev):
    return pltpu.make_async_remote_copy(
        src_ref=src, dst_ref=dst, send_sem=ss, recv_sem=rs, device_id=dev, device_id_type=MESH
    )


V_BO, V_G1, V_S1, V_BB, V_G2, V_S2, V_BI = 3, 4, 5, 6, 7, 8, 9


def forward(r, send_queries):
    x, qkv = r["x"], r["qkv"]
    vec = r["vec"]
    lane = lax.broadcasted_iota(jnp.int32, (1, 128), 1)
    masks = [(lane < HD).astype(BF), (lane >= HD).astype(BF)]

    def qkv_tile(j):
        b, n = j // 3, j % 3
        acc = dot(x[...], r["wq"][:, at(j, 256)])
        qkv[b, :, at(n, 256)] = (acc + vec[pl.ds(b, 1), at(n, 256)]).astype(BF)

    r["wait"](0, 1, 2)
    loop(9, qkv_tile, 3)

    key_at = lax.broadcasted_iota(jnp.int32, (PLEN, PLEN), 0)
    q_row = lax.broadcasted_iota(jnp.int32, (QR, QR), 0) // QLEN
    q_col = lax.broadcasted_iota(jnp.int32, (QR, QR), 1) // QLEN

    def pair(hp):
        cols = at(hp, 128)
        segs = [(pl.ds(PLEN * m, PLEN), key_at < r["len"][m]) for m in range(MB)]
        segs.append((pl.ds(PR, QR), q_row == q_col))
        scores = []
        for rows, valid in segs:
            q, k = qkv[0, rows, cols], qkv[1, rows, cols]
            for h in range(2):
                scores.append(jnp.where(valid, dot_nt(k, q * (masks[h] * 0.125)), masked))
        probs = []
        for i, sc in enumerate(scores):
            e = jnp.exp(sc - jnp.max(sc, 0, keepdims=True))
            pr = (e * (1.0 / jnp.sum(e, 0, keepdims=True))).astype(BF)
            m, h = i // 2, i % 2
            if m < MB:
                r["pp"][12 * m + 2 * hp + h] = pr
            else:
                r["pq"][2 * hp + h] = pr
            probs.append(pr)
        for m, (rows, _) in enumerate(segs):
            vt = qkv[2, rows, cols].T
            parts = [
                dot(vt[HD * h : HD * (h + 1)], probs[2 * m + h]).astype(BF) for h in range(2)
            ]
            r["att"][rows, cols] = jnp.concatenate(parts, 0).T

    loop(PAIRS, pair, 3)

    def resid_one(n):
        cols = at(n, 256)
        acc = dot(r["att"][...], r["wo"][:, cols])
        r["n2"][:, cols] = x[:, cols].astype(F32) + acc + vec[V_BO : V_BO + 1, cols]

    r["wait"](3)
    loop(3, resid_one, 3)

    def norm(h):
        c = h - jnp.mean(h, -1, keepdims=True)
        inv = lax.rsqrt(jnp.mean(c * c, -1, keepdims=True) + epsilon)
        return c * inv, inv

    def norm_one(i):
        rows = at(i, 64)
        n, inv = norm(r["n2"][rows, :])
        r["n1"][rows, :] = n
        r["i1"][rows, :] = inv
        r["nl"][rows, :] = (n * vec[V_G1 : V_G1 + 1, :] + vec[V_S1 : V_S1 + 1, :]).astype(BF)

    loop(ROWS // 64, norm_one, 5)

    def ffn(b):
        tiles = []
        for n in range(3):
            bias = vec[pl.ds(V_BI + b, 1), at(n, 256)]
            tiles.append(dot(r["nl"][...], r["wi"][:, at(3 * b + n, 256)]) + bias)
        for n, pre in enumerate(tiles):
            cols = at(n, 256)
            cdf = 0.5 * (1.0 + lax.erf(pre * 0.7071067811865476))
            r["slope"][b, :, cols] = (
                cdf + pre * jnp.exp(-0.5 * pre * pre) * 0.3989422804014327
            ).astype(BF)
            post = (pre * cdf).astype(BF)
            r["grad"][4 + b, 0:3, :, :, cols] = post[: 6 * SR].reshape(3, 2, SR, 256)
            r["grad"][4 + b, 3, 0, 0 : ROWS - 6 * SR, cols] = post[6 * SR :]

    r["wait"](4)
    loop(4, ffn)

    def resid_two(n):
        cols = at(n, 256)
        acc = r["n1"][:, cols] * vec[V_G1 : V_G1 + 1, cols] + vec[V_S1 : V_S1 + 1, cols]
        acc = acc + vec[V_BB : V_BB + 1, cols]
        for b in range(4):
            acc = acc + dot(post_block(r, b, pl.ds(0, CW)), r["wb"][b, :, cols])
        r["n2"][:, cols] = acc

    r["wait"](5)
    loop(3, resid_two, 3)

    def norm_two(i):
        rows = at(i, 128)
        n, inv = norm(r["n2"][rows, :])
        r["n2"][rows, :] = n
        r["i2"][rows, :] = inv
        r["s2"][rows, :] = (n * vec[V_G2 : V_G2 + 1, :] + vec[V_S2 : V_S2 + 1, :]).astype(BF)

    r["wait"](6)

    def project(rows):
        proj = dot(r["s2"][rows, :], r["wp"][...])
        il = lax.rsqrt(jnp.sum(proj * proj, -1, keepdims=True) + epsilon)
        unit = proj * il
        r["il"][rows, :] = il
        r["unit"][rows, :] = unit
        r["emb"][rows, :] = unit.astype(BF)

    norm_two(PR // 128)
    project(pl.ds(PR, QR))
    send_queries()
    for i in range(PR // 128):
        norm_two(i)
    project(pl.ds(0, PR))


def post_block(r, b, cols):
    top = r["grad"][4 + b, 0:3, :, :, cols].reshape(6 * SR, cols.size)
    return jnp.concatenate([top, r["grad"][4 + b, 3, 0, 0 : ROWS - 6 * SR, cols]], 0)


def peers(r, g, p, src, buf, ss, rs):
    copies = []
    for o in range(1, PSG):
        to = (p + o) % PSG
        copies.append(remote(src(to), buf.at[p], ss.at[o - 1], rs.at[o - 1], (g, to)))
    return copies


def query_copies(r, g, p):
    src = r["emb"].at[pl.ds(PR, QR), :]
    return peers(r, g, p, lambda to: src, r["gq"], r["q_s"], r["q_r"])


def turn_post(r, i):
    b, half = i // 2, i % 2
    t = post_block(r, b, at(half, 384)).T
    for q in range(4):
        r["grad"][8 + q, b, half, :, 0:ROWS] = t[SR * q : SR * (q + 1)]


def maxsim(r, g, p):
    emb = r["emb"]
    queries = query_copies(r, g, p)
    r["gq"][p] = emb[PR:ROWS, :]
    for cp in queries:
        cp.wait()

    key_at = lax.broadcasted_iota(jnp.int32, (PSG * QDEV * QLEN, PLEN), 1)
    nq = PSG * QDEV
    half = QDEV * QLEN
    sums = []
    for m in range(MB):
        gq = jnp.concatenate([r["gq"][d, half * m : half * (m + 1), :] for d in range(PSG)], 0)
        s = dot_nt(gq, emb[PLEN * m : PLEN * (m + 1), :])
        e = jnp.where(key_at < r["len"][m], jnp.exp(s * (1.0 / temper)), 0.0)
        total = jnp.sum(e, -1, keepdims=True)
        r["sim"][m] = e
        sums.append(total)
        log = jnp.broadcast_to(jnp.log(total), (nq * QLEN, 128))
        r["sc"][p, nq * m : nq * (m + 1), :] = temper * jnp.sum(log.reshape(nq, QLEN, 128), 1)
    scores = peers(r, g, p, lambda to: r["sc"].at[p], r["sc"], r["s_s"], r["s_r"])
    for cp in scores:
        cp.start()
    loop(6, lambda i: turn_post(r, i))
    for cp in scores:
        cp.wait()
    every = [r["sc"][d] for d in range(PSG)]
    top = functools.reduce(jnp.maximum, every)
    log_total = top + jnp.log(sum(jnp.exp(v - top) for v in every))
    row = lax.broadcasted_iota(jnp.int32, (MB * nq, 128), 0)
    pos = jnp.zeros((MB * nq, 128), jnp.int32)
    for m in range(MB):
        for q in range(nq):
            pos = jnp.where(row == nq * m + q, r["pos"][m, q], pos)
    picked = sum(jnp.where(pos == d, every[d], 0.0) for d in range(PSG))
    r["lo"][...] = log_total - picked
    grad_score = jnp.exp(r["sc"][p] - log_total) - (pos == p).astype(F32)
    for m in range(MB):
        gs = grad_score[nq * m : nq * (m + 1)]
        gs = jnp.broadcast_to(gs[:, None, :], (nq, QLEN, 128)).reshape(nq * QLEN, 128)
        coef = gs * (1.0 / sums[m])
        coef = jnp.concatenate([coef, coef], 1)
        ds = (coef * r["sim"][m]).astype(BF)
        pe = emb[PLEN * m : PLEN * (m + 1), :]
        gg = dot(ds, pe).astype(BF)
        for d in range(PSG):
            r["gg"][d, half * m : half * (m + 1), :] = gg[half * d : half * (d + 1)]
        gq = jnp.concatenate([r["gq"][d, half * m : half * (m + 1), :] for d in range(PSG)], 0)
        r["de"][PLEN * m : PLEN * (m + 1), :] = dot_tn(ds, gq).astype(BF)
    backs = peers(r, g, p, lambda to: r["gg"].at[to], r["gr"], r["g_s"], r["g_r"])
    for cp in backs:
        cp.start()
    r["gr"][p] = r["gg"][p]
    loop(2, lambda i: turn_post(r, 6 + i))
    sums = head_back(r, 0, PR)
    for cp in backs:
        cp.wait()
    r["de"][PR:ROWS, :] = sum(r["gr"][d].astype(F32) for d in range(PSG)).astype(BF)
    for row, one, two in zip((5, 6, 7), sums, head_back(r, PR, QR)):
        r["sm"][row : row + 1, :] = jnp.sum(one + two, 0, keepdims=True)


def norm_back(grad_out, n, inv, gain):
    gn = grad_out * gain
    return inv * (
        gn - jnp.mean(gn, -1, keepdims=True) - n * jnp.mean(gn * n, -1, keepdims=True)
    )


def head_back(r, first, count):
    vec = r["vec"]
    some = pl.ds(first, count)
    gu = r["de"][some, :].astype(F32)
    unit = r["unit"][some, :]
    along = jnp.sum(gu * unit, -1, keepdims=True)
    r["gp"][some, :] = (r["il"][some, :] * (gu - unit * along)).astype(BF)
    sums = None
    for i in range(count // 128):
        rows = pl.ds(first + 128 * i, 128)
        g2 = dot_nt(r["gp"][rows, :], r["wp"][...])
        n = r["n2"][rows, :]
        gr = norm_back(g2, n, r["i2"][rows, :], vec[V_G2 : V_G2 + 1, :])
        low = gr.astype(BF)
        r["n2"][rows, :] = gr
        r["gb"][rows, :] = low
        add = (fold(low.astype(F32)), fold(g2 * n), fold(g2))
        sums = add if sums is None else tuple(a + b for a, b in zip(sums, add))
    return sums


def backward_step(r, t):
    vec, qkv, grad = r["vec"], r["qkv"], r["grad"]
    lane = lax.broadcasted_iota(jnp.int32, (1, 128), 1)
    masks = [(lane < HD).astype(BF), (lane >= HD).astype(BF)]

    def outer(left, right, k, n):
        grad[k, :, :, :, at(n, 256)] = dot(left, right).astype(BF).reshape(4, 2, SR, 256)

    def turn(src, n):
        r["lt"][at(n, 256), :] = src[:, at(n, 256)].T

    @pl.when(t < 4)
    def _():
        def tile(n):
            left = grad[8 + t, :, :, :, 0:ROWS].reshape(CW, ROWS)
            outer(left, r["gb"][:, at(n, 256)], t, n)

        loop(3, tile, 3)

    @pl.when(t == 4)
    def _():
        loop(3, lambda n: turn(r["nl"], n), 3)

    @pl.when((t >= 4) & (t < 8))
    def _():
        b = t - 4

        def tile(n):
            cols = at(n, 256)
            v = dot_nt(r["gb"][...], r["wb"][b, cols, :]) * r["slope"][b, :, cols].astype(F32)
            low = v.astype(BF)
            r["slope"][b, :, cols] = low
            r["sm"][pl.ds(8 + b, 1), cols] = jnp.sum(low.astype(F32), 0, keepdims=True)
            outer(r["lt"][...], low, 4 + b, n)

        loop(3, tile, 3)

    @pl.when(t == 8)
    def _():
        loop(3, lambda n: turn(r["s2"], n), 3)
        v = dot(r["lt"][...], r["gp"][...]).astype(BF)
        r["gmini"][:, :, :, 0:PROJ] = v.reshape(4, 2, SR, PROJ)

    @pl.when((t >= 8) & (t < 11))
    def _():
        n = t - 8
        cols = at(n, 256)
        acc = r["n2"][:, cols]
        for b in range(4):
            acc = acc + dot_nt(r["slope"][b], r["wi"][cols, CW * b : CW * (b + 1)])
        r["n2"][:, cols] = acc

    @pl.when(t == 11)
    def _():
        def body(i, sums):
            rows = at(i, 64)
            g1, n = r["n2"][rows, :], r["n1"][rows, :]
            gr = norm_back(g1, n, r["i1"][rows, :], vec[V_G1 : V_G1 + 1, :])
            low = gr.astype(BF)
            r["n1"][rows, :] = gr
            r["gb"][rows, :] = low
            add = (fold(low.astype(F32)), fold(g1 * n), fold(g1))
            return tuple(a + b for a, b in zip(sums, add))

        zero = jnp.zeros((8, D), F32)
        sums = lax.fori_loop(0, ROWS // 64, body, (zero, zero, zero), unroll=5)
        for row, v in zip((2, 3, 4), sums):
            r["sm"][row : row + 1, :] = jnp.sum(v, 0, keepdims=True)
        loop(3, lambda n: turn(r["att"], n), 3)
        loop(3, lambda n: outer(r["lt"][...], r["gb"][:, at(n, 256)], 8, n), 3)

    @pl.when(t == 12)
    def _():
        def tile(n):
            r["att"][:, at(n, 256)] = dot_nt(r["gb"][...], r["wo"][at(n, 256), :]).astype(BF)

        loop(3, tile, 3)
        loop(3, lambda n: turn(r["x"], n), 3)

    @pl.when((t >= 13) & (t < 13 + PAIRS))
    def _():
        hp = t - 13
        cols = at(hp, 128)
        segs = [(pl.ds(PLEN * m, PLEN), r["pp"], 12 * m) for m in range(MB)]
        segs.append((pl.ds(PR, QR), r["pq"], 0))
        work = []
        for rows, p_ref, first in segs:
            q, k, v = qkv[0, rows, cols], qkv[1, rows, cols], qkv[2, rows, cols]
            a = r["att"][rows, cols]
            for h in range(2):
                ah = a * masks[h]
                work.append((q * masks[h], ah, p_ref[first + 2 * hp + h], dot_nt(v, ah)))
        grads = []
        for qh, ah, pr, dp in work:
            pf = pr.astype(F32)
            ds = (pf * (dp - jnp.sum(pf * dp, 0, keepdims=True))).astype(BF)
            grads.append(ds)
        bq = bv = 0.0
        for m, (rows, _, _) in enumerate(segs):
            kt = qkv[1, rows, cols].T
            dk = dv = 0.0
            parts = []
            for h in range(2):
                qh, ah, pr, _ = work[2 * m + h]
                ds = grads[2 * m + h]
                parts.append((dot(kt[HD * h : HD * (h + 1)], ds) * 0.125).astype(BF))
                dk = dk + dot(ds, qh)
                dv = dv + dot(pr, ah)
            dq = jnp.concatenate(parts, 0).T
            dv = dv.astype(BF)
            qkv[0, rows, cols] = dq
            qkv[1, rows, cols] = (dk * 0.125).astype(BF)
            qkv[2, rows, cols] = dv
            bq = bq + jnp.sum(dq.astype(F32), 0, keepdims=True)
            bv = bv + jnp.sum(dv.astype(F32), 0, keepdims=True)
        r["sm"][0:1, cols] = bq
        r["sm"][1:2, cols] = bv

    @pl.when((t == 14) | (t == 16) | (t == 18))
    def _():
        i = (t - 14) // 2
        loop(3, lambda b: outer(r["lt"][...], qkv[b, :, at(i, 256)], 9 + i, b), 3)

    @pl.when(t == 19)
    def _():
        small = r["sm"][...].T
        one = lax.broadcasted_iota(jnp.int32, (SR, 128), 1)
        pad = jnp.zeros((SR, 128 - small.shape[1]), F32)
        for s in range(SHARDS):
            v = jnp.concatenate([small[SR * s : SR * (s + 1)], pad], 1)
            b, base = s // 2, 384 * (s % 2)
            v = jnp.where(one < 8, v, 0.0)
            for q in range(4):
                col = small[base + SR * q : base + SR * (q + 1), 8 + b : 9 + b]
                v = jnp.where(one == 8 + q, col, v)
            r["gmini"][s // 2, s % 2, :, PROJ:MW] = v.astype(BF)

    @pl.when((t >= 20) & (t < 23))
    def _():
        n = t - 20
        cols = at(n, 256)
        acc = r["n1"][:, cols]
        for b in range(3):
            acc = acc + dot_nt(qkv[b], r["wq"][cols, CW * b : CW * (b + 1)])
        r["gb"][:, cols] = acc.astype(BF)


def slot_of(t):
    k = jnp.where(t < 8, t, -1)
    for step, which in ((11, 8), (14, 9), (16, 10), (18, 11)):
        k = jnp.where(t == step, which, k)
    return jnp.where(t >= LAST_ENTER, t - LAST_ENTER + NC, k)


LAST_ENTER = 19


class Reducer:
    def __init__(self, r, g, p):
        self.r = r
        self.p = p
        self.z, self.y = g // 2, g % 2
        self.x, self.c = p // 2, p % 2
        z, y, x, c = self.z, self.y, self.x, self.c
        self.sib = (g, p + 1 - 2 * c)
        self.ynb = (g + 1 - 2 * y, p)
        self.xnb = (g, (p + 2) % 4)
        self.outer = (z == 0) | (z == 3)
        self.line = [(2 * ((z + o) % 4) + y, p) for o in range(1, 4)]
        self.own = pl.ds(pl.multiple_of(c * HALF, 16), HALF)
        self.oth = pl.ds(pl.multiple_of((1 - c) * HALF, 16), HALF)

    def unit(self, k, kind):
        r = self.r
        u = lambda: None
        u.k, u.core, u.kind = k, min(kind, 1), kind
        if isinstance(k, int) and k == NC:
            u.width = MW
            u.g = r["gmini"]
            u.cs, u.s, u.ls = CORE_SLOTS, SLOTS, LINE_SLOTS
            for name in ("core_rv", "first_a", "first_b", "second_b", "line_rv", "cross_rv", "done"):
                setattr(u, name, r["m_" + name])
        else:
            u.width = CW
            u.g = r["grad"].at[k]
            u.cs, u.s, u.ls = k % CORE_SLOTS, k % SLOTS, k % LINE_SLOTS
            u.core_rv = r["core_rv"].at[u.cs]
            for name in ("first_a", "first_b", "second_b", "cross_rv"):
                setattr(u, name, r[name].at[u.s])
            u.line_rv = r["line_rv"].at[u.ls]
            u.done = r["done"].at[k]
        return u

    def add_into(self, dst, src):
        dst[...] = (dst[...].astype(F32) + src[...].astype(F32)).astype(BF)

    def half(self, u, xx):
        w = u.width // 2
        return pl.ds(pl.multiple_of(xx * w, 128), w)

    def core_copy(self, u):
        r = self.r
        return remote(
            u.g.at[:, :, self.oth, :], u.core_rv, r["c_s"].at[u.cs], r["c_r"].at[u.cs], self.sib
        )

    def core_end(self, u):
        self.core_copy(u).wait()
        loop(
            SHARDS,
            lambda i: self.add_into(
                u.g.at[i // 2, i % 2, self.own, :], u.core_rv.at[i // 2, i % 2]
            ),
        )

    def one_copy(self, u):
        r = self.r
        sems = r["one_s"].at[u.s], r["one_r"].at[u.s]
        if u.core == 0:
            return remote(u.g.at[:, 1 - self.y, self.own, :], u.first_a, *sems, self.ynb)
        away = self.half(u, 1 - self.x)
        return remote(u.g.at[:, :, self.own, away], u.first_b, *sems, self.xnb)

    def one_start(self, u):
        self.one_copy(u).start()

    def one_end(self, u):
        self.one_copy(u).wait()
        if u.core == 0:
            loop(
                4, lambda i: self.add_into(u.g.at[i, self.y, self.own, :], u.first_a.at[i])
            )
        else:
            mine = self.half(u, self.x)
            loop(
                SHARDS,
                lambda i: self.add_into(
                    u.g.at[i // 2, i % 2, self.own, mine], u.first_b.at[i // 2, i % 2]
                ),
            )

    def two_copy(self, u):
        r = self.r
        return remote(
            u.g.at[:, 1 - self.y, self.own, self.half(u, self.x)],
            u.second_b,
            r["two_s"].at[u.s],
            r["two_r"].at[u.s],
            self.ynb,
        )

    def two_start(self, u):
        self.two_copy(u).start()

    def two_end(self, u):
        self.two_copy(u).wait()
        mine = self.half(u, self.x)
        loop(
            4, lambda i: self.add_into(u.g.at[i, self.y, self.own, mine], u.second_b.at[i])
        )

    def part(self, u, d, y=None):
        cols = slice(None) if u.core == 0 else self.half(u, self.x)
        return u.g.at[d, self.y if y is None else y, self.own, cols]

    def lanes(self, u):
        return ((0, 0), (1, 1)) if u.kind == 2 else ((None, 0),)

    def seen(self, i):
        return jnp.where(self.z < 2, i, 3 - i)

    def landing(self, u, i, j):
        w = u.width // (1 + u.core)
        return u.line_rv.at[i, :, pl.ds(j * w, w)]

    def line_copy(self, u, i, slot, send, y, j):
        r, d = self.r, self.seen(i)
        to = self.seen(jnp.where(self.outer, 1, i))
        return remote(
            self.part(u, d, y),
            self.landing(u, slot, j),
            r["z_s"].at[8 * u.ls + 2 * send + j],
            r["z_r"].at[8 * u.ls + 2 * slot + j],
            (2 * to + self.y, self.p),
        )

    def out_copies(self, u):
        return [self.line_copy(u, i, i - 1, i - 1, *w) for i in (3, 2, 1) for w in self.lanes(u)]

    def own_copies(self, u):
        return [self.line_copy(u, 0, 0, 3, *w) for w in self.lanes(u)]

    def in_copies(self, u, i):
        return [self.line_copy(u, i, 1 if i == 3 else 3, 3 - i, *w) for w in self.lanes(u)]

    def take(self, u, d, slot):
        for y, j in self.lanes(u):
            self.line_copy(u, 0, slot, 0, y, j).wait_recv()
            self.add_into(self.part(u, d, y), self.landing(u, slot, j))

    def line_one(self, u):
        @pl.when(self.outer)
        def _():
            for cp in self.out_copies(u):
                cp.start()

        @pl.when(jnp.logical_not(self.outer))
        def _():
            for cp in self.own_copies(u):
                cp.start()

    def line_two(self, u):
        @pl.when(self.outer)
        def _():
            self.take(u, self.z, 0)
            for cp in self.out_copies(u):
                cp.wait_send()

        @pl.when(jnp.logical_not(self.outer))
        def _():
            for i in (3, 2, 1):
                self.take(u, self.seen(i), i - 1)
                if i > 1:
                    for cp in self.in_copies(u, i):
                        cp.start()
            for cp in self.own_copies(u):
                cp.wait_send()

    def line_end(self, u):
        @pl.when(self.outer)
        def _():
            self.take(u, self.z, 1)

        @pl.when(jnp.logical_not(self.outer))
        def _():
            self.take(u, self.z, 3)
            for i in (3, 2):
                for cp in self.in_copies(u, i):
                    cp.wait_send()

    def late_copy(self, u):
        r = self.r
        return remote(
            self.part(u, self.z, 1 - self.y),
            u.second_b.at[0],
            r["two_s"].at[u.s],
            r["two_r"].at[u.s],
            self.ynb,
        )

    def late_start(self, u):
        self.late_copy(u).start()

    def late_end(self, u):
        self.late_copy(u).wait()
        self.add_into(self.part(u, self.z), u.second_b.at[0])

    def last_copy(self, u):
        r = self.r
        sems = r["last_s"].at[u.s], r["last_r"].at[u.s]
        to = u.cross_rv if u.core == 0 else u.done.at[:, self.half(u, self.x)]
        return remote(self.part(u, self.z), to, *sems, self.xnb)

    def last_start(self, u):
        self.last_copy(u).start()

    def last_end(self, u):
        self.last_copy(u).wait()
        mine = self.part(u, self.z)[...]
        if u.core == 0:
            u.done[...] = (mine.astype(F32) + u.cross_rv[...].astype(F32)).astype(BF)
        else:
            u.done[:, self.half(u, self.x)] = mine

    def to_outputs(self, u, do):
        r, k, own = self.r, u.k, self.own

        def both(dst):
            do(pltpu.make_async_copy(u.done, dst, r["st_sem"].at[k]))
            do(remote(u.done, dst, r["fin_s"].at[k], r["fin_r"].at[k], self.sib))

        if isinstance(k, int) and k == NC:
            both(r["mini_o"].at[own, :])
            return

        @pl.when(k < 4)
        def _():
            both(r["back_o"].at[pl.ds(pl.multiple_of(SR * k + HALF * self.c, 16), HALF), :])

        @pl.when((k >= 4) & (k < 8))
        def _():
            both(r["in_o"].at[own, at(k - 4, CW)])

        @pl.when(k == 8)
        def _():
            both(r["out_o"].at[own, :])

        @pl.when(k > 8)
        def _():
            both(r["qkv_o"].at[own, at(k - 9, CW)])

    def stages(self, kind):
        out = lambda u: self.to_outputs(u, lambda cp: cp.start())
        core_start = lambda u: self.core_copy(u).start()
        if kind == 0:
            return {
                0: [core_start],
                1: [self.core_end, self.one_start],
                4: [self.one_end, self.line_one],
                6: [self.line_two],
                8: [self.line_end, self.last_start],
                10: [self.last_end, out],
            }
        if kind == 1:
            return {
                0: [core_start],
                1: [self.core_end, self.one_start],
                4: [self.one_end, self.two_start],
                6: [self.two_end, self.line_one],
                8: [self.line_two],
                10: [self.line_end, self.last_start],
                12: [self.last_end, out],
            }
        return {
            0: [core_start],
            1: [self.core_end, self.one_start],
            4: [self.one_end, self.line_one],
            6: [self.line_two],
            8: [self.line_end, self.late_start],
            10: [self.late_end, self.last_start],
            12: [self.last_end, out],
        }

    def slot(self, t):
        for core in range(2):

            @pl.when(self.c == core)
            def _():
                kinds = (1, 2) if core else (0,)
                stages = {kind: self.stages(kind) for kind in kinds}
                for s in sorted(stages[kinds[0]], reverse=True):
                    k = t - s
                    valid = (k >= 0) & (k < NC)
                    alike = len(kinds) == 1 or s in (0, 1)
                    for kind in kinds[:1] if alike else kinds:
                        now = valid if alike else valid & (k % 2 == kind - 1)

                        @pl.when(now)
                        def _():
                            for do in stages[kind][s]:
                                do(self.unit(k, kind))

                    @pl.when(k == NC)
                    def _():
                        for do in stages[kinds[0]][s]:
                            do(self.unit(NC, kinds[0]))

    def finish(self, k):
        self.to_outputs(self.unit(k, 0), lambda cp: cp.wait())


VECTORS = ("v_bq", "v_bv", "v_bo", "v_g1", "v_s1", "v_bb", "v_g2", "v_s2", "v_bi")
INPUTS = ("len", "pos") + VECTORS + ("xp_h", "xq_h", "wq_h", "wo_h", "wi_h", "wb_h", "wp_h")


def kernel(spread, names, *refs):
    r = dict(zip(names, refs))
    g = lax.axis_index("group")
    p = lax.axis_index("psg")
    barrier = pltpu.get_barrier_semaphore()

    def greet(dev):
        pl.semaphore_signal(barrier, inc=1, device_id=dev, device_id_type=MESH)

    for o in range(1, PSG):
        greet((g, (p + o) % PSG))
    count = PSG - 1
    if spread:
        red = Reducer(r, g, p)
        for dev in [red.ynb] + red.line:
            greet(dev)
        count = count + 4

    pairs = [
        (r["xp_h"], r["x"].at[pl.ds(0, PR), :]),
        (r["xq_h"], r["x"].at[pl.ds(PR, QR), :]),
        (r["wq_h"], r["wq"]),
        (r["wo_h"], r["wo"]),
        (r["wi_h"], r["wi"]),
        (r["wb_h"], r["wb"]),
        (r["wp_h"], r["wp"]),
    ]
    row = 0
    for name in VECTORS:
        v = r[name][...].astype(F32)
        n = v.shape[0] // D
        for i in range(n):
            r["vec"][row + i : row + i + 1, :] = v[D * i : D * (i + 1)].reshape(1, D)
        row += n
        if name == "v_bq":
            r["vec"][row : row + 1, :] = jnp.zeros((1, D), F32)
            row += 1
    loads = [pltpu.make_async_copy(a, b, r["in_sem"].at[i]) for i, (a, b) in enumerate(pairs)]
    for cp in loads[:3]:
        cp.start()

    def wait(*which):
        for i in which:
            loads[i].wait()
        if 2 in which:
            for cp in loads[3:]:
                cp.start()

    r["wait"] = wait

    def send_queries():
        pl.semaphore_wait(barrier, count)
        for cp in query_copies(r, g, p):
            cp.start()

    forward(r, send_queries)
    maxsim(r, g, p)
    lane = lax.broadcasted_iota(jnp.int32, (1, 128), 1)
    for m in range(MB):
        v = jnp.zeros((1, 128), F32)
        for q in range(QDEV):
            v = jnp.where(lane == q, r["lo"][pl.ds(PSG * QDEV * m + QDEV * p + q, 1), :], v)
        r["loss_o"][m : m + 1, :] = v

    outs = [
        (r["emb"].at[pl.ds(0, PR), :], r["ep_o"]),
        (r["emb"].at[pl.ds(PR, QR), :], r["eq_o"]),
        (r["gb"].at[pl.ds(0, PR), :], r["gxp_o"]),
        (r["gb"].at[pl.ds(PR, QR), :], r["gxq_o"]),
    ]
    if not spread:
        outs += [(r["grad"], r["grad_o"]), (r["gmini"], r["mini_o"])]
    stores = [pltpu.make_async_copy(a, b, r["out_sem"].at[i]) for i, (a, b) in enumerate(outs)]

    def step(t):
        backward_step(r, t)

        @pl.when(t == 22)
        def _():
            for cp in stores:
                cp.start()

        if spread:
            now = slot_of(t)

            @pl.when(now >= 0)
            def _():
                red.slot(now)


    loop(LAST_ENTER + 13 if spread else 23, step)

    for cp in stores:
        cp.wait()
    if spread:
        loop(NC, red.finish)
        red.finish(NC)


def run_step(spread, inputs):
    sds = jax.ShapeDtypeStruct
    outs = {
        "loss_o": sds((MB, 128), F32),
        "eq_o": sds((QR, PROJ), BF),
        "ep_o": sds((PR, PROJ), BF),
        "gxq_o": sds((QR, D), BF),
        "gxp_o": sds((PR, D), BF),
    }
    if spread:
        outs |= {
            "back_o": sds((4 * SR, D), BF),
            "in_o": sds((SR, FF), BF),
            "out_o": sds((SR, D), BF),
            "qkv_o": sds((SR, 3 * D), BF),
            "mini_o": sds((SR, MW), BF),
        }
    else:
        outs |= {
            "grad_o": sds((NC, 4, 2, SR, CW), BF),
            "mini_o": sds((4, 2, SR, MW), BF),
        }
    vm = pltpu.VMEM
    dma = pltpu.SemaphoreType.DMA
    scratch = {
        "vec": vm((16, D), F32),
        "x": vm((ROWS, D), BF),
        "wq": vm((D, 3 * D), BF),
        "wo": vm((D, D), BF),
        "wi": vm((D, FF), BF),
        "wb": vm((4, CW, D), BF),
        "wp": vm((D, PROJ), BF),
        "qkv": vm((3, ROWS, D), BF),
        "pp": vm((MB * 12, PLEN, PLEN), BF),
        "pq": vm((12, QR, QR), BF),
        "att": vm((ROWS, D), BF),
        "n1": vm((ROWS, D), F32),
        "n2": vm((ROWS, D), F32),
        "i1": vm((ROWS, 1), F32),
        "i2": vm((ROWS, 1), F32),
        "il": vm((ROWS, 1), F32),
        "nl": vm((ROWS, D), BF),
        "slope": vm((4, ROWS, CW), BF),
        "s2": vm((ROWS, D), BF),
        "unit": vm((ROWS, PROJ), F32),
        "emb": vm((ROWS, PROJ), BF),
        "de": vm((ROWS, PROJ), BF),
        "gp": vm((ROWS, PROJ), BF),
        "gb": vm((ROWS, D), BF),
        "lt": vm((D, ROWS), BF),
        "sm": vm((16, D), F32),
        "gq": vm((PSG, QR, PROJ), BF),
        "sim": vm((MB, PSG * QDEV * QLEN, PLEN), F32),
        "sc": vm((PSG, MB * PSG * QDEV, 128), F32),
        "lo": vm((MB * PSG * QDEV, 128), F32),
        "gg": vm((PSG, QR, PROJ), BF),
        "gr": vm((PSG, QR, PROJ), BF),
        "grad": vm((NC, 4, 2, SR, CW), BF),
        "gmini": vm((4, 2, SR, MW), BF),
        "in_sem": dma((7,)),
        "out_sem": dma((6,)),
    }
    for name in ("q_s", "q_r", "s_s", "s_r", "g_s", "g_r"):
        scratch[name] = dma((PSG - 1,))
    if spread:
        for lead, slots, w, pre in ((True, (CORE_SLOTS, SLOTS, NC), CW, ""), (False, None, MW, "m_")):
            a, b, c = ((slots[0],), (slots[1],), (slots[2],)) if lead else ((), (), ())
            scratch[pre + "core_rv"] = vm(a + (4, 2, HALF, w), BF)
            scratch[pre + "first_a"] = vm(b + (4, HALF, w), BF)
            scratch[pre + "first_b"] = vm(b + (4, 2, HALF, w // 2), BF)
            scratch[pre + "second_b"] = vm(b + (4, HALF, w // 2), BF)
            scratch[pre + "line_rv"] = vm((LINE_SLOTS,) * len(b) + (4, HALF, w), BF)
            scratch[pre + "cross_rv"] = vm(b + (HALF, w), BF)
            scratch[pre + "done"] = vm(c + (HALF, w), BF)
        for name in ("c_s", "c_r"):
            scratch[name] = dma((CORE_SLOTS + 1,))
        for name in ("one_s", "one_r", "two_s", "two_r", "last_s", "last_r"):
            scratch[name] = dma((SLOTS + 1,))
        for name in ("z_s", "z_r"):
            scratch[name] = dma((8 * (LINE_SLOTS + 1),))
        for name in ("st_sem", "fin_s", "fin_r"):
            scratch[name] = dma((NC + 1,))
    hbm = pl.BlockSpec(memory_space=pl.ANY)
    vmem = pl.BlockSpec(memory_space=pltpu.VMEM)
    smem = pl.BlockSpec(memory_space=pltpu.SMEM)
    names = INPUTS + tuple(outs) + tuple(scratch)
    res = pl.pallas_call(
        functools.partial(kernel, spread, names),
        out_shape=list(outs.values()),
        in_specs=[smem, smem] + [vmem] * len(VECTORS) + [hbm] * 7,
        out_specs=[vmem] + [hbm] * (len(outs) - 1),
        scratch_shapes=list(scratch.values()),
        compiler_params=pltpu.CompilerParams(
            collective_id=0, has_side_effects=True, vmem_limit_bytes=64 << 20
        ),
        name="train_step",
    )(*inputs)
    return dict(zip(outs, res))


WIDE = ("eq_o", "ep_o", "gxq_o", "gxp_o")
GRADS = ("qkv_o", "out_o", "in_o", "back_o")


def finish_kernel(*refs):
    names = ("loss", "mini") + GRADS + WIDE
    n = len(names)
    i = dict(zip(names, refs[:n]))
    o = dict(zip(("loss",) + WIDE + GRADS + ("proj", "bias_in"), refs[n:]))
    o["loss"][...] = i["loss"][:, 0:QDEV]

    def move(v):
        def cast(j):
            o[v][at(j, 32), :] = i[v][at(j, 32), :].astype(o[v].dtype)

        loop(i[v].shape[0] // 32, cast)

    for v in GRADS[1:] + WIDE:
        move(v)
    for b in range(3):
        for n in range(3):
            to = slice(CW * b + 256 * n, CW * b + 256 * (n + 1))
            of = slice(CW * n + 256 * b, CW * n + 256 * (b + 1))
            o["qkv_o"][:, to] = i["qkv_o"][:, of].astype(F32)
    o["proj"][...] = i["mini"][:, 0:PROJ].astype(F32)
    small = i["mini"][:, PROJ:MW].astype(F32).T
    for j, ref in enumerate(refs[-8:]):
        ref[...] = small[j, 0:SR]
    o["bias_in"][...] = jnp.concatenate([small[8 + q : 9 + q, 0:SR] for q in range(4)], 1)[0]


def finish_step(o):
    sds = jax.ShapeDtypeStruct
    like = lambda v, t: sds(o[v].shape, t)
    outs = [sds((MB, QDEV), F32)]
    outs += [like(v, BF) for v in WIDE] + [like(v, F32) for v in GRADS]
    outs += [sds((SR, PROJ), F32), sds((4 * SR,), F32)] + [sds((SR,), F32)] * 8
    vmem = pl.BlockSpec(memory_space=pltpu.VMEM)
    res = pl.pallas_call(
        finish_kernel,
        out_shape=outs,
        in_specs=[vmem] * 10,
        out_specs=[vmem] * 19,
        name="finish",
    )(o["loss_o"], o["mini_o"], *[o[v] for v in GRADS], *[o[v] for v in WIDE])
    moved = dict(zip(("loss_o",) + WIDE, res[:5]))
    qkv, w_out, w_in, back, proj, bias_in = res[5:11]
    v = res[11:]
    return moved, (
        qkv, v[0], v[1], w_out, v[2], v[3], v[4], w_in, bias_in,
        back, v[5], v[6], v[7], proj,
    )


def body(
    query_input,
    passage_input,
    lengths,
    positive,
    w_qkv,
    bias_q,
    bias_v,
    w_out,
    bias_out,
    norm1_gain,
    norm1_bias,
    w_in,
    bias_in,
    w_back,
    bias_back,
    norm2_gain,
    norm2_bias,
    w_proj,
):
    spread = lax.axis_size("group") == SHARDS
    inputs = (
        lengths.reshape(MB),
        positive,
        bias_q,
        bias_v,
        bias_out,
        norm1_gain,
        norm1_bias,
        bias_back,
        norm2_gain,
        norm2_bias,
        bias_in,
        passage_input.reshape(PR, D),
        query_input.reshape(QR, D),
        w_qkv,
        w_out,
        w_in,
        w_back.reshape(4, CW, D),
        w_proj,
    )
    o = run_step(spread, inputs)
    if spread:
        o, finals = finish_step(o)
    else:
        full = o["grad_o"].reshape(NC, SHARDS, SR, CW)
        mini = o["mini_o"].reshape(D, MW)
        small = mini[:, PROJ : PROJ + 8]
        wide = o["mini_o"].reshape(SHARDS, SR, MW)[:, :, PROJ + 8 : PROJ + 12].transpose(0, 2, 1).reshape(FF)
        halves = full[9:12].reshape(3, D, 3, 256).transpose(1, 2, 0, 3).reshape(D, 3 * D)
        terms = (
            halves,
            small[:, 0],
            small[:, 1],
            full[8].reshape(D, D),
            small[:, 2],
            small[:, 3],
            small[:, 4],
            full[4:8].reshape(4, D, CW).transpose(1, 0, 2).reshape(D, FF),
            wide,
            full[0:4].transpose(1, 0, 2, 3).reshape(FF, D),
            small[:, 5],
            small[:, 6],
            small[:, 7],
            mini[:, :PROJ],
        )
        shared = lax.psum_scatter(terms, "group", scatter_dimension=0, tiled=True)
        finals = lax.psum(shared, "psg")
    return (
        o["loss_o"][:, :QDEV],
        o["eq_o"].reshape(MB, QDEV, QLEN, PROJ),
        o["ep_o"].reshape(MB, -1, PLEN, PROJ),
        o["gxq_o"].reshape(query_input.shape),
        o["gxp_o"].reshape(passage_input.shape),
    ) + tuple(part.astype(F32) for part in finals)


def solution(mesh):
    in_specs = (
        P(None, ("group", "psg"), None, None),
        P(None, ("group", "psg"), None, None),
        P(None, ("group", "psg")),
        P(None, "group"),
        P(),
        P(),
        P(),
        P(),
        P(),
        P(),
        P(),
        P(),
        P(),
        P(),
        P(),
        P(),
        P(),
        P(),
    )
    out_specs = (
        P(None, ("group", "psg")),
        P(None, ("group", "psg"), None, None),
        P(None, ("group", "psg"), None, None),
        P(None, ("group", "psg"), None, None),
        P(None, ("group", "psg"), None, None),
        P("group", None),
        P("group"),
        P("group"),
        P("group", None),
        P("group"),
        P("group"),
        P("group"),
        P("group", None),
        P("group"),
        P("group", None),
        P("group"),
        P("group"),
        P("group"),
        P("group", None),
    )
    return jax.shard_map(body, mesh=mesh, in_specs=in_specs, out_specs=out_specs, check_vma=False)
```

```python
import functools

import jax
import jax.numpy as jnp
from jax import lax
from jax.experimental import pallas as pl
from jax.experimental.pallas import tpu as pltpu
from jax.sharding import PartitionSpec as P

D = 768
HD = 64
FF = 3072
PROJ = 128
QLEN = 32
PLEN = 256
MB = 2
QDEV = 2
PSG = 4

PR = MB * PLEN
QR = MB * QDEV * QLEN
ROWS = PR + QR
PAIRS = D // 128
NC = 12
CW = 768
MW = 256
SHARDS = 8
SR = D // SHARDS
HALF = SR // 2
CORE_SLOTS = 2
SLOTS = 6
LINE_SLOTS = 6

temper = 0.1
epsilon = 1e-06
masked = -1e30

MESH = pl.DeviceIdType.MESH
BF = jnp.bfloat16
F32 = jnp.float32


def dot(a, b):
    return jnp.dot(a, b, preferred_element_type=F32)


def dot_nt(a, b):
    return lax.dot_general(a, b, (((1,), (1,)), ((), ())), preferred_element_type=F32)


def dot_tn(a, b):
    return lax.dot_general(a, b, (((0,), (0,)), ((), ())), preferred_element_type=F32)


def at(i, size):
    return pl.ds(i * size if isinstance(i, int) else pl.multiple_of(i * size, size), size)


def loop(n, body, unroll=1):
    def step(i, carry):
        body(i)
        return carry

    lax.fori_loop(0, n, step, 0, unroll=unroll)


def fold(v):
    return jnp.sum(v.reshape(v.shape[0] // 8, 8, v.shape[1]), 0)


def remote(src, dst, ss, rs, dev):
    return pltpu.make_async_remote_copy(
        src_ref=src, dst_ref=dst, send_sem=ss, recv_sem=rs, device_id=dev, device_id_type=MESH
    )


V_BO, V_G1, V_S1, V_BB, V_G2, V_S2, V_BI = 3, 4, 5, 6, 7, 8, 9


def forward(r, send_queries):
    x, qkv = r["x"], r["qkv"]
    vec = r["vec"]
    lane = lax.broadcasted_iota(jnp.int32, (1, 128), 1)
    masks = [(lane < HD).astype(BF), (lane >= HD).astype(BF)]

    def qkv_tile(j):
        b, n = j // 3, j % 3
        acc = dot(x[...], r["wq"][:, at(j, 256)])
        qkv[b, :, at(n, 256)] = (acc + vec[pl.ds(b, 1), at(n, 256)]).astype(BF)

    r["wait"](0, 1, 2)
    for j in range(9):
        qkv_tile(j)

    key_at = lax.broadcasted_iota(jnp.int32, (PLEN, PLEN), 0)
    q_row = lax.broadcasted_iota(jnp.int32, (QR, QR), 0) // QLEN
    q_col = lax.broadcasted_iota(jnp.int32, (QR, QR), 1) // QLEN

    def pair(hp):
        cols = at(hp, 128)
        segs = [(pl.ds(PLEN * m, PLEN), key_at < r["len"][m]) for m in range(MB)]
        segs.append((pl.ds(PR, QR), q_row == q_col))
        scores = []
        for rows, valid in segs:
            q, k = qkv[0, rows, cols], qkv[1, rows, cols]
            for h in range(2):
                scores.append(jnp.where(valid, dot_nt(k, q * (masks[h] * 0.125)), masked))
        probs = []
        for i, sc in enumerate(scores):
            e = jnp.exp(sc - jnp.max(sc, 0, keepdims=True))
            pr = (e * (1.0 / jnp.sum(e, 0, keepdims=True))).astype(BF)
            m, h = i // 2, i % 2
            if m < MB:
                r["pp"][12 * m + 2 * hp + h] = pr
            else:
                r["pq"][2 * hp + h] = pr
            probs.append(pr)
        for m, (rows, _) in enumerate(segs):
            vt = qkv[2, rows, cols].T
            parts = [
                dot(vt[HD * h : HD * (h + 1)], probs[2 * m + h]).astype(BF) for h in range(2)
            ]
            r["att"][rows, cols] = jnp.concatenate(parts, 0).T

    loop(PAIRS, pair, 3)

    def resid_one(n):
        cols = at(n, 256)
        acc = dot(r["att"][...], r["wo"][:, cols])
        r["n2"][:, cols] = x[:, cols].astype(F32) + acc + vec[V_BO : V_BO + 1, cols]

    r["wait"](3)
    for n in range(3):
        resid_one(n)

    def norm(h):
        c = h - jnp.mean(h, -1, keepdims=True)
        inv = lax.rsqrt(jnp.mean(c * c, -1, keepdims=True) + epsilon)
        return c * inv, inv

    def norm_one(i):
        rows = at(i, 128)
        n, inv = norm(r["n2"][rows, :])
        r["n1"][rows, :] = n
        r["i1"][rows, :] = inv
        r["nl"][rows, :] = (n * vec[V_G1 : V_G1 + 1, :] + vec[V_S1 : V_S1 + 1, :]).astype(BF)

    for i in range(ROWS // 128):
        norm_one(i)

    def ffn(b):
        tiles = []
        for n in range(3):
            bias = vec[pl.ds(V_BI + b, 1), at(n, 256)]
            tiles.append(dot(r["nl"][...], r["wi"][:, at(3 * b + n, 256)]) + bias)
        for n, pre in enumerate(tiles):
            cols = at(n, 256)
            cdf = 0.5 * (1.0 + lax.erf(pre * 0.7071067811865476))
            r["slope"][b, :, cols] = (
                cdf + pre * jnp.exp(-0.5 * pre * pre) * 0.3989422804014327
            ).astype(BF)
            post = (pre * cdf).astype(BF)
            r["grad"][4 + b, 0:3, :, :, cols] = post[: 6 * SR].reshape(3, 2, SR, 256)
            r["grad"][4 + b, 3, 0, 0 : ROWS - 6 * SR, cols] = post[6 * SR :]

    r["wait"](4)
    for b in range(4):
        ffn(b)

    def resid_two(n):
        cols = at(n, 256)
        acc = r["n1"][:, cols] * vec[V_G1 : V_G1 + 1, cols] + vec[V_S1 : V_S1 + 1, cols]
        acc = acc + vec[V_BB : V_BB + 1, cols]
        for b in range(4):
            acc = acc + dot(post_block(r, b, pl.ds(0, CW)), r["wb"][b, :, cols])
        r["n2"][:, cols] = acc

    r["wait"](5)
    for n in range(3):
        resid_two(n)

    def norm_two(i):
        rows = at(i, 128)
        n, inv = norm(r["n2"][rows, :])
        r["n2"][rows, :] = n
        r["i2"][rows, :] = inv
        r["s2"][rows, :] = (n * vec[V_G2 : V_G2 + 1, :] + vec[V_S2 : V_S2 + 1, :]).astype(BF)

    r["wait"](6)

    def project(rows):
        proj = dot(r["s2"][rows, :], r["wp"][...])
        il = lax.rsqrt(jnp.sum(proj * proj, -1, keepdims=True) + epsilon)
        unit = proj * il
        r["il"][rows, :] = il
        r["unit"][rows, :] = unit
        r["emb"][rows, :] = unit.astype(BF)

    norm_two(PR // 128)
    project(pl.ds(PR, QR))
    send_queries()
    for i in range(PR // 128):
        norm_two(i)
    project(pl.ds(0, PR))


def post_block(r, b, cols):
    top = r["grad"][4 + b, 0:3, :, :, cols].reshape(6 * SR, cols.size)
    return jnp.concatenate([top, r["grad"][4 + b, 3, 0, 0 : ROWS - 6 * SR, cols]], 0)


def peers(r, g, p, src, buf, ss, rs):
    copies = []
    for o in range(1, PSG):
        to = (p + o) % PSG
        copies.append(remote(src(to), buf.at[p], ss.at[o - 1], rs.at[o - 1], (g, to)))
    return copies


def query_copies(r, g, p):
    src = r["emb"].at[pl.ds(PR, QR), :]
    return peers(r, g, p, lambda to: src, r["gq"], r["q_s"], r["q_r"])


def turn_post(r, i):
    b, half = i // 2, i % 2
    t = post_block(r, b, at(half, 384)).T
    for q in range(4):
        r["grad"][8 + q, b, half, :, 0:ROWS] = t[SR * q : SR * (q + 1)]


def maxsim(r, g, p):
    emb = r["emb"]
    queries = query_copies(r, g, p)
    r["gq"][p] = emb[PR:ROWS, :]
    for cp in queries:
        cp.wait()

    key_at = lax.broadcasted_iota(jnp.int32, (PSG * QDEV * QLEN, PLEN), 1)
    nq = PSG * QDEV
    half = QDEV * QLEN
    sums = []
    for m in range(MB):
        gq = jnp.concatenate([r["gq"][d, half * m : half * (m + 1), :] for d in range(PSG)], 0)
        s = dot_nt(gq, emb[PLEN * m : PLEN * (m + 1), :])
        e = jnp.where(key_at < r["len"][m], jnp.exp(s * (1.0 / temper)), 0.0)
        total = jnp.sum(e, -1, keepdims=True)
        r["sim"][m] = e
        sums.append(total)
        log = jnp.broadcast_to(jnp.log(total), (nq * QLEN, 128))
        r["sc"][p, nq * m : nq * (m + 1), :] = temper * jnp.sum(log.reshape(nq, QLEN, 128), 1)
    scores = peers(r, g, p, lambda to: r["sc"].at[p], r["sc"], r["s_s"], r["s_r"])
    for cp in scores:
        cp.start()
    loop(6, lambda i: turn_post(r, i))
    for cp in scores:
        cp.wait()
    every = [r["sc"][d] for d in range(PSG)]
    top = functools.reduce(jnp.maximum, every)
    log_total = top + jnp.log(sum(jnp.exp(v - top) for v in every))
    row = lax.broadcasted_iota(jnp.int32, (MB * nq, 128), 0)
    pos = jnp.zeros((MB * nq, 128), jnp.int32)
    for m in range(MB):
        for q in range(nq):
            pos = jnp.where(row == nq * m + q, r["pos"][m, q], pos)
    picked = sum(jnp.where(pos == d, every[d], 0.0) for d in range(PSG))
    r["lo"][...] = log_total - picked
    grad_score = jnp.exp(r["sc"][p] - log_total) - (pos == p).astype(F32)
    for m in range(MB):
        gs = grad_score[nq * m : nq * (m + 1)]
        gs = jnp.broadcast_to(gs[:, None, :], (nq, QLEN, 128)).reshape(nq * QLEN, 128)
        coef = gs * (1.0 / sums[m])
        coef = jnp.concatenate([coef, coef], 1)
        ds = (coef * r["sim"][m]).astype(BF)
        pe = emb[PLEN * m : PLEN * (m + 1), :]
        gg = dot(ds, pe).astype(BF)
        for d in range(PSG):
            r["gg"][d, half * m : half * (m + 1), :] = gg[half * d : half * (d + 1)]
        gq = jnp.concatenate([r["gq"][d, half * m : half * (m + 1), :] for d in range(PSG)], 0)
        r["de"][PLEN * m : PLEN * (m + 1), :] = dot_tn(ds, gq).astype(BF)
    backs = peers(r, g, p, lambda to: r["gg"].at[to], r["gr"], r["g_s"], r["g_r"])
    for cp in backs:
        cp.start()
    r["gr"][p] = r["gg"][p]
    loop(2, lambda i: turn_post(r, 6 + i))
    sums = head_back(r, 0, PR)
    for cp in backs:
        cp.wait()
    r["de"][PR:ROWS, :] = sum(r["gr"][d].astype(F32) for d in range(PSG)).astype(BF)
    for row, one, two in zip((5, 6, 7), sums, head_back(r, PR, QR)):
        r["sm"][row : row + 1, :] = jnp.sum(one + two, 0, keepdims=True)


def norm_back(grad_out, n, inv, gain):
    gn = grad_out * gain
    return inv * (
        gn - jnp.mean(gn, -1, keepdims=True) - n * jnp.mean(gn * n, -1, keepdims=True)
    )


def head_back(r, first, count):
    vec = r["vec"]
    some = pl.ds(first, count)
    gu = r["de"][some, :].astype(F32)
    unit = r["unit"][some, :]
    along = jnp.sum(gu * unit, -1, keepdims=True)
    r["gp"][some, :] = (r["il"][some, :] * (gu - unit * along)).astype(BF)
    sums = None
    for i in range(count // 128):
        rows = pl.ds(first + 128 * i, 128)
        g2 = dot_nt(r["gp"][rows, :], r["wp"][...])
        n = r["n2"][rows, :]
        gr = norm_back(g2, n, r["i2"][rows, :], vec[V_G2 : V_G2 + 1, :])
        low = gr.astype(BF)
        r["n2"][rows, :] = gr
        r["gb"][rows, :] = low
        add = (fold(low.astype(F32)), fold(g2 * n), fold(g2))
        sums = add if sums is None else tuple(a + b for a, b in zip(sums, add))
    return sums


def backward_step(r, t):
    vec, qkv, grad = r["vec"], r["qkv"], r["grad"]
    lane = lax.broadcasted_iota(jnp.int32, (1, 128), 1)
    masks = [(lane < HD).astype(BF), (lane >= HD).astype(BF)]

    def outer(left, right, k, n):
        grad[k, :, :, :, at(n, 256)] = dot(left, right).astype(BF).reshape(4, 2, SR, 256)

    def turn(src, n):
        r["lt"][at(n, 256), :] = src[:, at(n, 256)].T

    @pl.when(t < 4)
    def _():
        def tile(n):
            left = grad[8 + t, :, :, :, 0:ROWS].reshape(CW, ROWS)
            outer(left, r["gb"][:, at(n, 256)], t, n)

        loop(3, tile, 3)

    @pl.when(t == 4)
    def _():
        loop(3, lambda n: turn(r["nl"], n), 3)

    def pre_back(b, n):
        cols = at(n, 256)
        v = dot_nt(r["gb"][...], r["wb"][b, cols, :]) * r["slope"][b, :, cols].astype(F32)
        low = v.astype(BF)
        r["slope"][b, :, cols] = low
        r["sm"][pl.ds(8 + b, 1), cols] = jnp.sum(low.astype(F32), 0, keepdims=True)
        return low

    @pl.when((t >= 4) & (t < 7))
    def _():
        loop(3, lambda n: outer(r["lt"][...], pre_back(t - 4, n), t, n), 3)

    @pl.when(t == 7)
    def _():
        for n in range(3):
            pre_back(3, n)

    @pl.when(t == 9)
    def _():
        loop(3, lambda n: outer(r["lt"][...], r["slope"][3, :, at(n, 256)], 7, n), 3)

    @pl.when(t == 10)
    def _():
        loop(3, lambda n: turn(r["s2"], n), 3)
        v = dot(r["lt"][...], r["gp"][...]).astype(BF)
        r["gmini"][:, :, :, 0:PROJ] = v.reshape(4, 2, SR, PROJ)

    @pl.when((t >= 8) & (t < 11))
    def _():
        n = t - 8
        cols = at(n, 256)
        acc = r["n2"][:, cols]
        for b in range(4):
            acc = acc + dot_nt(r["slope"][b], r["wi"][cols, CW * b : CW * (b + 1)])
        r["n2"][:, cols] = acc

    @pl.when(t == 11)
    def _():
        sums = None
        for i in range(ROWS // 128):
            rows = pl.ds(128 * i, 128)
            g1, n = r["n2"][rows, :], r["n1"][rows, :]
            gr = norm_back(g1, n, r["i1"][rows, :], vec[V_G1 : V_G1 + 1, :])
            low = gr.astype(BF)
            r["n1"][rows, :] = gr
            r["gb"][rows, :] = low
            add = (fold(low.astype(F32)), fold(g1 * n), fold(g1))
            sums = add if sums is None else tuple(a + b for a, b in zip(sums, add))
        for row, v in zip((2, 3, 4), sums):
            r["sm"][row : row + 1, :] = jnp.sum(v, 0, keepdims=True)
        loop(3, lambda n: turn(r["att"], n), 3)
        loop(3, lambda n: outer(r["lt"][...], r["gb"][:, at(n, 256)], 8, n), 3)

    @pl.when(t == 12)
    def _():
        def tile(n):
            r["att"][:, at(n, 256)] = dot_nt(r["gb"][...], r["wo"][at(n, 256), :]).astype(BF)

        loop(3, tile, 3)
        loop(3, lambda n: turn(r["x"], n), 3)

    @pl.when((t >= 13) & (t < 13 + PAIRS))
    def _():
        hp = t - 13
        cols = at(hp, 128)
        segs = [(pl.ds(PLEN * m, PLEN), r["pp"], 12 * m) for m in range(MB)]
        segs.append((pl.ds(PR, QR), r["pq"], 0))
        work = []
        for rows, p_ref, first in segs:
            q, k, v = qkv[0, rows, cols], qkv[1, rows, cols], qkv[2, rows, cols]
            a = r["att"][rows, cols]
            for h in range(2):
                ah = a * masks[h]
                work.append((q * masks[h], ah, p_ref[first + 2 * hp + h], dot_nt(v, ah)))
        grads = []
        for qh, ah, pr, dp in work:
            pf = pr.astype(F32)
            ds = (pf * (dp - jnp.sum(pf * dp, 0, keepdims=True))).astype(BF)
            grads.append(ds)
        bq = bv = 0.0
        for m, (rows, _, _) in enumerate(segs):
            kt = qkv[1, rows, cols].T
            dk = dv = 0.0
            parts = []
            for h in range(2):
                qh, ah, pr, _ = work[2 * m + h]
                ds = grads[2 * m + h]
                parts.append((dot(kt[HD * h : HD * (h + 1)], ds) * 0.125).astype(BF))
                dk = dk + dot(ds, qh)
                dv = dv + dot(pr, ah)
            dq = jnp.concatenate(parts, 0).T
            dv = dv.astype(BF)
            qkv[0, rows, cols] = dq
            qkv[1, rows, cols] = (dk * 0.125).astype(BF)
            qkv[2, rows, cols] = dv
            bq = bq + jnp.sum(dq.astype(F32), 0, keepdims=True)
            bv = bv + jnp.sum(dv.astype(F32), 0, keepdims=True)
        r["sm"][0:1, cols] = bq
        r["sm"][1:2, cols] = bv

    @pl.when((t == 14) | (t == 16) | (t == 18))
    def _():
        i = (t - 14) // 2
        loop(3, lambda b: outer(r["lt"][...], qkv[b, :, at(i, 256)], 9 + i, b), 3)

    @pl.when(t == 19)
    def _():
        small = r["sm"][...].T
        one = lax.broadcasted_iota(jnp.int32, (SR, 128), 1)
        pad = jnp.zeros((SR, 128 - small.shape[1]), F32)
        for s in range(SHARDS):
            v = jnp.concatenate([small[SR * s : SR * (s + 1)], pad], 1)
            b, base = s // 2, 384 * (s % 2)
            v = jnp.where(one < 8, v, 0.0)
            for q in range(4):
                col = small[base + SR * q : base + SR * (q + 1), 8 + b : 9 + b]
                v = jnp.where(one == 8 + q, col, v)
            r["gmini"][s // 2, s % 2, :, PROJ:MW] = v.astype(BF)

    @pl.when((t >= 20) & (t < 23))
    def _():
        n = t - 20
        cols = at(n, 256)
        acc = r["n1"][:, cols]
        for b in range(3):
            acc = acc + dot_nt(qkv[b], r["wq"][cols, CW * b : CW * (b + 1)])
        r["gb"][:, cols] = acc.astype(BF)


def slot_of(t):
    k = jnp.where(t < 7, t, -1)
    for step, which in ((9, 7), (11, 8), (14, 9), (16, 10), (18, 11)):
        k = jnp.where(t == step, which, k)
    return jnp.where(t >= LAST_ENTER, t - LAST_ENTER + NC, k)


LAST_ENTER = 19


class Reducer:
    def __init__(self, r, g, p):
        self.r = r
        self.p = p
        self.z, self.y = g // 2, g % 2
        self.x, self.c = p // 2, p % 2
        z, y, x, c = self.z, self.y, self.x, self.c
        self.sib = (g, p + 1 - 2 * c)
        self.ynb = (g + 1 - 2 * y, p)
        self.xnb = (g, (p + 2) % 4)
        self.outer = (z == 0) | (z == 3)
        self.line = [(2 * ((z + o) % 4) + y, p) for o in range(1, 4)]
        self.own = pl.ds(pl.multiple_of(c * HALF, 16), HALF)
        self.oth = pl.ds(pl.multiple_of((1 - c) * HALF, 16), HALF)

    def unit(self, k, kind):
        r = self.r
        u = lambda: None
        u.k, u.core, u.kind = k, min(kind, 1), kind
        if isinstance(k, int) and k == NC:
            u.width = MW
            u.g = r["gmini"]
            u.cs, u.s, u.ls = CORE_SLOTS, SLOTS, LINE_SLOTS
            for name in ("core_rv", "first_a", "first_b", "second_b", "line_rv", "cross_rv", "done"):
                setattr(u, name, r["m_" + name])
        else:
            u.width = CW
            u.g = r["grad"].at[k]
            u.cs, u.s, u.ls = k % CORE_SLOTS, k % SLOTS, k % LINE_SLOTS
            u.core_rv = r["core_rv"].at[u.cs]
            for name in ("first_a", "first_b", "second_b", "cross_rv"):
                setattr(u, name, r[name].at[u.s])
            u.line_rv = r["line_rv"].at[u.ls]
            u.done = r["done"].at[k]
        return u

    def add_into(self, dst, src):
        dst[...] = (dst[...].astype(F32) + src[...].astype(F32)).astype(BF)

    def half(self, u, xx):
        w = u.width // 2
        return pl.ds(pl.multiple_of(xx * w, 128), w)

    def core_copy(self, u):
        r = self.r
        return remote(
            u.g.at[:, :, self.oth, :], u.core_rv, r["c_s"].at[u.cs], r["c_r"].at[u.cs], self.sib
        )

    def core_end(self, u):
        self.core_copy(u).wait()
        loop(
            SHARDS,
            lambda i: self.add_into(
                u.g.at[i // 2, i % 2, self.own, :], u.core_rv.at[i // 2, i % 2]
            ),
        )

    def one_copy(self, u):
        r = self.r
        sems = r["one_s"].at[u.s], r["one_r"].at[u.s]
        if u.core == 0:
            return remote(u.g.at[:, 1 - self.y, self.own, :], u.first_a, *sems, self.ynb)
        away = self.half(u, 1 - self.x)
        return remote(u.g.at[:, :, self.own, away], u.first_b, *sems, self.xnb)

    def one_start(self, u):
        self.one_copy(u).start()

    def one_end(self, u):
        self.one_copy(u).wait()
        if u.core == 0:
            loop(
                4, lambda i: self.add_into(u.g.at[i, self.y, self.own, :], u.first_a.at[i])
            )
        else:
            mine = self.half(u, self.x)
            loop(
                SHARDS,
                lambda i: self.add_into(
                    u.g.at[i // 2, i % 2, self.own, mine], u.first_b.at[i // 2, i % 2]
                ),
            )

    def two_copy(self, u):
        r = self.r
        return remote(
            u.g.at[:, 1 - self.y, self.own, self.half(u, self.x)],
            u.second_b,
            r["two_s"].at[u.s],
            r["two_r"].at[u.s],
            self.ynb,
        )

    def two_start(self, u):
        self.two_copy(u).start()

    def two_end(self, u):
        self.two_copy(u).wait()
        mine = self.half(u, self.x)
        loop(
            4, lambda i: self.add_into(u.g.at[i, self.y, self.own, mine], u.second_b.at[i])
        )

    def part(self, u, d, y=None):
        cols = slice(None) if u.core == 0 else self.half(u, self.x)
        return u.g.at[d, self.y if y is None else y, self.own, cols]

    def lanes(self, u):
        return ((0, 0), (1, 1)) if u.kind == 2 else ((None, 0),)

    def seen(self, i):
        return jnp.where(self.z < 2, i, 3 - i)

    def landing(self, u, i, j):
        w = u.width // (1 + u.core)
        return u.line_rv.at[i, :, pl.ds(j * w, w)]

    def line_copy(self, u, i, slot, send, y, j):
        r, d = self.r, self.seen(i)
        to = self.seen(jnp.where(self.outer, 1, i))
        return remote(
            self.part(u, d, y),
            self.landing(u, slot, j),
            r["z_s"].at[8 * u.ls + 2 * send + j],
            r["z_r"].at[8 * u.ls + 2 * slot + j],
            (2 * to + self.y, self.p),
        )

    def out_copies(self, u):
        return [self.line_copy(u, i, i - 1, i - 1, *w) for i in (3, 2, 1) for w in self.lanes(u)]

    def own_copies(self, u):
        return [self.line_copy(u, 0, 0, 3, *w) for w in self.lanes(u)]

    def in_copies(self, u, i):
        return [self.line_copy(u, i, 1 if i == 3 else 3, 3 - i, *w) for w in self.lanes(u)]

    def take(self, u, d, slot):
        for y, j in self.lanes(u):
            self.line_copy(u, 0, slot, 0, y, j).wait_recv()
            self.add_into(self.part(u, d, y), self.landing(u, slot, j))

    def line_one(self, u):
        @pl.when(self.outer)
        def _():
            for cp in self.out_copies(u):
                cp.start()

        @pl.when(jnp.logical_not(self.outer))
        def _():
            for cp in self.own_copies(u):
                cp.start()

    def line_two(self, u):
        @pl.when(self.outer)
        def _():
            self.take(u, self.z, 0)
            for cp in self.out_copies(u):
                cp.wait_send()

        @pl.when(jnp.logical_not(self.outer))
        def _():
            for i in (3, 2, 1):
                self.take(u, self.seen(i), i - 1)
                if i > 1:
                    for cp in self.in_copies(u, i):
                        cp.start()
            for cp in self.own_copies(u):
                cp.wait_send()

    def line_end(self, u):
        @pl.when(self.outer)
        def _():
            self.take(u, self.z, 1)

        @pl.when(jnp.logical_not(self.outer))
        def _():
            self.take(u, self.z, 3)
            for i in (3, 2):
                for cp in self.in_copies(u, i):
                    cp.wait_send()

    def late_copy(self, u):
        r = self.r
        return remote(
            self.part(u, self.z, 1 - self.y),
            u.second_b.at[0],
            r["two_s"].at[u.s],
            r["two_r"].at[u.s],
            self.ynb,
        )

    def late_start(self, u):
        self.late_copy(u).start()

    def late_end(self, u):
        self.late_copy(u).wait()
        self.add_into(self.part(u, self.z), u.second_b.at[0])

    def last_copy(self, u):
        r = self.r
        sems = r["last_s"].at[u.s], r["last_r"].at[u.s]
        to = u.cross_rv if u.core == 0 else u.done.at[:, self.half(u, self.x)]
        return remote(self.part(u, self.z), to, *sems, self.xnb)

    def last_start(self, u):
        self.last_copy(u).start()

    def last_end(self, u):
        self.last_copy(u).wait()
        mine = self.part(u, self.z)[...]
        if u.core == 0:
            u.done[...] = (mine.astype(F32) + u.cross_rv[...].astype(F32)).astype(BF)
        else:
            u.done[:, self.half(u, self.x)] = mine

    def to_outputs(self, u, do):
        r, k, own = self.r, u.k, self.own

        def both(dst):
            do(pltpu.make_async_copy(u.done, dst, r["st_sem"].at[k]))
            do(remote(u.done, dst, r["fin_s"].at[k], r["fin_r"].at[k], self.sib))

        if isinstance(k, int) and k == NC:
            both(r["mini_o"].at[own, :])
            return

        @pl.when(k < 4)
        def _():
            both(r["back_o"].at[pl.ds(pl.multiple_of(SR * k + HALF * self.c, 16), HALF), :])

        @pl.when((k >= 4) & (k < 8))
        def _():
            both(r["in_o"].at[own, at(k - 4, CW)])

        @pl.when(k == 8)
        def _():
            both(r["out_o"].at[own, :])

        @pl.when(k > 8)
        def _():
            both(r["qkv_o"].at[own, at(k - 9, CW)])

    def stages(self, kind):
        out = lambda u: self.to_outputs(u, lambda cp: cp.start())
        core_start = lambda u: self.core_copy(u).start()
        if kind == 0:
            return {
                0: [core_start],
                1: [self.core_end, self.one_start],
                4: [self.one_end, self.line_one],
                6: [self.line_two],
                8: [self.line_end, self.last_start],
                10: [self.last_end, out],
            }
        if kind == 1:
            return {
                0: [core_start],
                1: [self.core_end, self.one_start],
                4: [self.one_end, self.two_start],
                6: [self.two_end, self.line_one],
                8: [self.line_two],
                10: [self.line_end, self.last_start],
                12: [self.last_end, out],
            }
        return {
            0: [core_start],
            1: [self.core_end, self.one_start],
            4: [self.one_end, self.line_one],
            6: [self.line_two],
            8: [self.line_end, self.late_start],
            10: [self.late_end, self.last_start],
            12: [self.last_end, out],
        }

    def slot(self, t):
        for core in range(2):

            @pl.when(self.c == core)
            def _():
                kinds = (1, 2) if core else (0,)
                stages = {kind: self.stages(kind) for kind in kinds}
                for s in sorted(stages[kinds[0]], reverse=True):
                    k = t - s
                    valid = (k >= 0) & (k < NC)
                    alike = len(kinds) == 1 or s in (0, 1)
                    for kind in kinds[:1] if alike else kinds:
                        now = valid if alike else valid & (k % 2 == kind - 1)

                        @pl.when(now)
                        def _():
                            for do in stages[kind][s]:
                                do(self.unit(k, kind))

                    @pl.when(k == NC)
                    def _():
                        for do in stages[kinds[0]][s]:
                            do(self.unit(NC, kinds[0]))

    def finish(self, k):
        self.to_outputs(self.unit(k, 0), lambda cp: cp.wait())


VECTORS = ("v_bq", "v_bv", "v_bo", "v_g1", "v_s1", "v_bb", "v_g2", "v_s2", "v_bi")
INPUTS = ("len", "pos") + VECTORS + ("xp_h", "xq_h", "wq_h", "wo_h", "wi_h", "wb_h", "wp_h")


def kernel(spread, names, *refs):
    r = dict(zip(names, refs))
    g = lax.axis_index("group")
    p = lax.axis_index("psg")
    barrier = pltpu.get_barrier_semaphore()

    def greet(dev):
        pl.semaphore_signal(barrier, inc=1, device_id=dev, device_id_type=MESH)

    for o in range(1, PSG):
        greet((g, (p + o) % PSG))
    count = PSG - 1
    if spread:
        red = Reducer(r, g, p)
        for dev in [red.ynb] + red.line:
            greet(dev)
        count = count + 4

    pairs = [
        (r["xp_h"], r["x"].at[pl.ds(0, PR), :]),
        (r["xq_h"], r["x"].at[pl.ds(PR, QR), :]),
        (r["wq_h"], r["wq"]),
        (r["wo_h"], r["wo"]),
        (r["wi_h"], r["wi"]),
        (r["wb_h"], r["wb"]),
        (r["wp_h"], r["wp"]),
    ]
    row = 0
    for name in VECTORS:
        v = r[name][...].astype(F32)
        n = v.shape[0] // D
        for i in range(n):
            r["vec"][row + i : row + i + 1, :] = v[D * i : D * (i + 1)].reshape(1, D)
        row += n
        if name == "v_bq":
            r["vec"][row : row + 1, :] = jnp.zeros((1, D), F32)
            row += 1
    loads = [pltpu.make_async_copy(a, b, r["in_sem"].at[i]) for i, (a, b) in enumerate(pairs)]
    for cp in loads[:3]:
        cp.start()

    def wait(*which):
        for i in which:
            loads[i].wait()
        if 2 in which:
            for cp in loads[3:]:
                cp.start()

    r["wait"] = wait

    def send_queries():
        pl.semaphore_wait(barrier, count)
        for cp in query_copies(r, g, p):
            cp.start()

    forward(r, send_queries)
    maxsim(r, g, p)
    lane = lax.broadcasted_iota(jnp.int32, (1, 128), 1)
    for m in range(MB):
        v = jnp.zeros((1, 128), F32)
        for q in range(QDEV):
            v = jnp.where(lane == q, r["lo"][pl.ds(PSG * QDEV * m + QDEV * p + q, 1), :], v)
        r["loss_o"][m : m + 1, :] = v

    outs = [
        (r["emb"].at[pl.ds(0, PR), :], r["ep_o"]),
        (r["emb"].at[pl.ds(PR, QR), :], r["eq_o"]),
        (r["gb"].at[pl.ds(0, PR), :], r["gxp_o"]),
        (r["gb"].at[pl.ds(PR, QR), :], r["gxq_o"]),
    ]
    if not spread:
        outs += [(r["grad"], r["grad_o"]), (r["gmini"], r["mini_o"])]
    stores = [pltpu.make_async_copy(a, b, r["out_sem"].at[i]) for i, (a, b) in enumerate(outs)]

    def step(t):
        backward_step(r, t)

        @pl.when(t == 22)
        def _():
            for cp in stores:
                cp.start()

        if spread:
            now = slot_of(t)

            @pl.when(now >= 0)
            def _():
                red.slot(now)


    loop(LAST_ENTER + 13 if spread else 23, step)

    for cp in stores:
        cp.wait()
    if spread:
        loop(NC, red.finish)
        red.finish(NC)


def run_step(spread, inputs):
    sds = jax.ShapeDtypeStruct
    outs = {
        "loss_o": sds((MB, 128), F32),
        "eq_o": sds((QR, PROJ), BF),
        "ep_o": sds((PR, PROJ), BF),
        "gxq_o": sds((QR, D), BF),
        "gxp_o": sds((PR, D), BF),
    }
    if spread:
        outs |= {
            "back_o": sds((4 * SR, D), BF),
            "in_o": sds((SR, FF), BF),
            "out_o": sds((SR, D), BF),
            "qkv_o": sds((SR, 3 * D), BF),
            "mini_o": sds((SR, MW), BF),
        }
    else:
        outs |= {
            "grad_o": sds((NC, 4, 2, SR, CW), BF),
            "mini_o": sds((4, 2, SR, MW), BF),
        }
    vm = pltpu.VMEM
    dma = pltpu.SemaphoreType.DMA
    scratch = {
        "vec": vm((16, D), F32),
        "x": vm((ROWS, D), BF),
        "wq": vm((D, 3 * D), BF),
        "wo": vm((D, D), BF),
        "wi": vm((D, FF), BF),
        "wb": vm((4, CW, D), BF),
        "wp": vm((D, PROJ), BF),
        "qkv": vm((3, ROWS, D), BF),
        "pp": vm((MB * 12, PLEN, PLEN), BF),
        "pq": vm((12, QR, QR), BF),
        "att": vm((ROWS, D), BF),
        "n1": vm((ROWS, D), F32),
        "n2": vm((ROWS, D), F32),
        "i1": vm((ROWS, 1), F32),
        "i2": vm((ROWS, 1), F32),
        "il": vm((ROWS, 1), F32),
        "nl": vm((ROWS, D), BF),
        "slope": vm((4, ROWS, CW), BF),
        "s2": vm((ROWS, D), BF),
        "unit": vm((ROWS, PROJ), F32),
        "emb": vm((ROWS, PROJ), BF),
        "de": vm((ROWS, PROJ), BF),
        "gp": vm((ROWS, PROJ), BF),
        "gb": vm((ROWS, D), BF),
        "lt": vm((D, ROWS), BF),
        "sm": vm((16, D), F32),
        "gq": vm((PSG, QR, PROJ), BF),
        "sim": vm((MB, PSG * QDEV * QLEN, PLEN), F32),
        "sc": vm((PSG, MB * PSG * QDEV, 128), F32),
        "lo": vm((MB * PSG * QDEV, 128), F32),
        "gg": vm((PSG, QR, PROJ), BF),
        "gr": vm((PSG, QR, PROJ), BF),
        "grad": vm((NC, 4, 2, SR, CW), BF),
        "gmini": vm((4, 2, SR, MW), BF),
        "in_sem": dma((7,)),
        "out_sem": dma((6,)),
    }
    for name in ("q_s", "q_r", "s_s", "s_r", "g_s", "g_r"):
        scratch[name] = dma((PSG - 1,))
    if spread:
        for lead, slots, w, pre in ((True, (CORE_SLOTS, SLOTS, NC), CW, ""), (False, None, MW, "m_")):
            a, b, c = ((slots[0],), (slots[1],), (slots[2],)) if lead else ((), (), ())
            scratch[pre + "core_rv"] = vm(a + (4, 2, HALF, w), BF)
            scratch[pre + "first_a"] = vm(b + (4, HALF, w), BF)
            scratch[pre + "first_b"] = vm(b + (4, 2, HALF, w // 2), BF)
            scratch[pre + "second_b"] = vm(b + (4, HALF, w // 2), BF)
            scratch[pre + "line_rv"] = vm((LINE_SLOTS,) * len(b) + (4, HALF, w), BF)
            scratch[pre + "cross_rv"] = vm(b + (HALF, w), BF)
            scratch[pre + "done"] = vm(c + (HALF, w), BF)
        for name in ("c_s", "c_r"):
            scratch[name] = dma((CORE_SLOTS + 1,))
        for name in ("one_s", "one_r", "two_s", "two_r", "last_s", "last_r"):
            scratch[name] = dma((SLOTS + 1,))
        for name in ("z_s", "z_r"):
            scratch[name] = dma((8 * (LINE_SLOTS + 1),))
        for name in ("st_sem", "fin_s", "fin_r"):
            scratch[name] = dma((NC + 1,))
    hbm = pl.BlockSpec(memory_space=pl.ANY)
    vmem = pl.BlockSpec(memory_space=pltpu.VMEM)
    smem = pl.BlockSpec(memory_space=pltpu.SMEM)
    names = INPUTS + tuple(outs) + tuple(scratch)
    res = pl.pallas_call(
        functools.partial(kernel, spread, names),
        out_shape=list(outs.values()),
        in_specs=[smem, smem] + [vmem] * len(VECTORS) + [hbm] * 7,
        out_specs=[vmem] + [hbm] * (len(outs) - 1),
        scratch_shapes=list(scratch.values()),
        compiler_params=pltpu.CompilerParams(
            collective_id=0, has_side_effects=True, vmem_limit_bytes=64 << 20
        ),
        name="train_step",
    )(*inputs)
    return dict(zip(outs, res))


WIDE = ("eq_o", "ep_o", "gxq_o", "gxp_o")
GRADS = ("qkv_o", "out_o", "in_o", "back_o")


def finish_kernel(*refs):
    names = ("loss", "mini") + GRADS + WIDE
    n = len(names)
    i = dict(zip(names, refs[:n]))
    o = dict(zip(("loss",) + WIDE + GRADS + ("proj", "bias_in"), refs[n:]))
    o["loss"][...] = i["loss"][:, 0:QDEV]

    def move(v):
        def cast(j):
            o[v][at(j, 32), :] = i[v][at(j, 32), :].astype(o[v].dtype)

        loop(i[v].shape[0] // 32, cast)

    for v in GRADS[1:] + WIDE:
        move(v)
    for b in range(3):
        for n in range(3):
            to = slice(CW * b + 256 * n, CW * b + 256 * (n + 1))
            of = slice(CW * n + 256 * b, CW * n + 256 * (b + 1))
            o["qkv_o"][:, to] = i["qkv_o"][:, of].astype(F32)
    o["proj"][...] = i["mini"][:, 0:PROJ].astype(F32)
    small = i["mini"][:, PROJ:MW].astype(F32).T
    for j, ref in enumerate(refs[-8:]):
        ref[...] = small[j, 0:SR]
    o["bias_in"][...] = jnp.concatenate([small[8 + q : 9 + q, 0:SR] for q in range(4)], 1)[0]


def finish_step(o):
    sds = jax.ShapeDtypeStruct
    like = lambda v, t: sds(o[v].shape, t)
    outs = [sds((MB, QDEV), F32)]
    outs += [like(v, BF) for v in WIDE] + [like(v, F32) for v in GRADS]
    outs += [sds((SR, PROJ), F32), sds((4 * SR,), F32)] + [sds((SR,), F32)] * 8
    vmem = pl.BlockSpec(memory_space=pltpu.VMEM)
    res = pl.pallas_call(
        finish_kernel,
        out_shape=outs,
        in_specs=[vmem] * 10,
        out_specs=[vmem] * 19,
        name="finish",
    )(o["loss_o"], o["mini_o"], *[o[v] for v in GRADS], *[o[v] for v in WIDE])
    moved = dict(zip(("loss_o",) + WIDE, res[:5]))
    qkv, w_out, w_in, back, proj, bias_in = res[5:11]
    v = res[11:]
    return moved, (
        qkv, v[0], v[1], w_out, v[2], v[3], v[4], w_in, bias_in,
        back, v[5], v[6], v[7], proj,
    )


def body(
    query_input,
    passage_input,
    lengths,
    positive,
    w_qkv,
    bias_q,
    bias_v,
    w_out,
    bias_out,
    norm1_gain,
    norm1_bias,
    w_in,
    bias_in,
    w_back,
    bias_back,
    norm2_gain,
    norm2_bias,
    w_proj,
):
    spread = lax.axis_size("group") == SHARDS
    inputs = (
        lengths.reshape(MB),
        positive,
        bias_q,
        bias_v,
        bias_out,
        norm1_gain,
        norm1_bias,
        bias_back,
        norm2_gain,
        norm2_bias,
        bias_in,
        passage_input.reshape(PR, D),
        query_input.reshape(QR, D),
        w_qkv,
        w_out,
        w_in,
        w_back.reshape(4, CW, D),
        w_proj,
    )
    o = run_step(spread, inputs)
    if spread:
        o, finals = finish_step(o)
    else:
        full = o["grad_o"].reshape(NC, SHARDS, SR, CW)
        mini = o["mini_o"].reshape(D, MW)
        small = mini[:, PROJ : PROJ + 8]
        wide = o["mini_o"].reshape(SHARDS, SR, MW)[:, :, PROJ + 8 : PROJ + 12].transpose(0, 2, 1).reshape(FF)
        halves = full[9:12].reshape(3, D, 3, 256).transpose(1, 2, 0, 3).reshape(D, 3 * D)
        terms = (
            halves,
            small[:, 0],
            small[:, 1],
            full[8].reshape(D, D),
            small[:, 2],
            small[:, 3],
            small[:, 4],
            full[4:8].reshape(4, D, CW).transpose(1, 0, 2).reshape(D, FF),
            wide,
            full[0:4].transpose(1, 0, 2, 3).reshape(FF, D),
            small[:, 5],
            small[:, 6],
            small[:, 7],
            mini[:, :PROJ],
        )
        shared = lax.psum_scatter(terms, "group", scatter_dimension=0, tiled=True)
        finals = lax.psum(shared, "psg")
    return (
        o["loss_o"][:, :QDEV],
        o["eq_o"].reshape(MB, QDEV, QLEN, PROJ),
        o["ep_o"].reshape(MB, -1, PLEN, PROJ),
        o["gxq_o"].reshape(query_input.shape),
        o["gxp_o"].reshape(passage_input.shape),
    ) + tuple(part.astype(F32) for part in finals)


def solution(mesh):
    in_specs = (
        P(None, ("group", "psg"), None, None),
        P(None, ("group", "psg"), None, None),
        P(None, ("group", "psg")),
        P(None, "group"),
        P(),
        P(),
        P(),
        P(),
        P(),
        P(),
        P(),
        P(),
        P(),
        P(),
        P(),
        P(),
        P(),
        P(),
    )
    out_specs = (
        P(None, ("group", "psg")),
        P(None, ("group", "psg"), None, None),
        P(None, ("group", "psg"), None, None),
        P(None, ("group", "psg"), None, None),
        P(None, ("group", "psg"), None, None),
        P("group", None),
        P("group"),
        P("group"),
        P("group", None),
        P("group"),
        P("group"),
        P("group"),
        P("group", None),
        P("group"),
        P("group", None),
        P("group"),
        P("group"),
        P("group"),
        P("group", None),
    )
    return jax.shard_map(body, mesh=mesh, in_specs=in_specs, out_specs=out_specs, check_vma=False)
```
